32 devices in a mesh: fsdp: 16 (over z, y, x), dp: 2 (over core).
Axes of the slice: x: 2, y: 2, z: 4, core: 2. Of those that a mesh axis runs over, the one named last changes fastest.
Arguments:
- block_in: bfloat16 [2, 128, 352, 512], P(None, ('fsdp', 'dp')), may hold values from -6 to 6
- offsets: int32 [2, 128, 2], P(None, ('fsdp', 'dp')), may hold values from 35 to 317
- cotangent: bfloat16 [2, 128, 352, 512], P(None, ('fsdp', 'dp')), may hold values from -6 to 6
- w_qkv: float32 [512, 1536], P('fsdp'), may hold values from -0.25 to 0.25
- w_out: float32 [512, 512], P('fsdp'), may hold values from -1.75 to 1.75
- w_up: float32 [512, 2048], P('fsdp'), may hold values from -0.25 to 0.25
- w_down: float32 [2048, 512], P('fsdp'), may hold values from -0.125 to 0.125
- vectors: float32 [6144], P('fsdp'), may hold values from -0.6 to 1.5
- first_qkv: float32 [512, 1536], P('fsdp'), may hold values from -1280 to 1280
- first_out: float32 [512, 512], P('fsdp'), may hold values from -192 to 192
- first_up: float32 [512, 2048], P('fsdp'), may hold values from -640 to 640
- first_down: float32 [2048, 512], P('fsdp'), may hold values from -1024 to 1024
- first_vectors: float32 [6144], P('fsdp'), may hold values from -1280 to 1280
- second_qkv: float32 [512, 1536], P('fsdp'), may hold values from 44154.88 to 176619.52
- second_out: float32 [512, 512], P('fsdp'), may hold values from 901.12 to 3604.48
- second_up: float32 [512, 2048], P('fsdp'), may hold values from 10813.44 to 44154.88
- second_down: float32 [2048, 512], P('fsdp'), may hold values from 32440.32 to 129761.28
- second_vectors: float32 [6144], P('fsdp'), may hold values from 44154.88 to 176619.52
Outputs:
- block_out: bfloat16 [2, 128, 352, 512], P(None, ('fsdp', 'dp'))
- input_grad: float32 [2, 128, 352, 512], P(None, ('fsdp', 'dp'))
- new_qkv: float32 [512, 1536], P('fsdp')
- new_out: float32 [512, 512], P('fsdp')
- new_up: float32 [512, 2048], P('fsdp')
- new_down: float32 [2048, 512], P('fsdp')
- new_vectors: float32 [6144], P('fsdp')
- new_first_qkv: float32 [512, 1536], P('fsdp')
- new_first_out: float32 [512, 512], P('fsdp')
- new_first_up: float32 [512, 2048], P('fsdp')
- new_first_down: float32 [2048, 512], P('fsdp')
- new_first_vectors: float32 [6144], P('fsdp')
- new_second_qkv: float32 [512, 1536], P('fsdp')
- new_second_out: float32 [512, 512], P('fsdp')
- new_second_up: float32 [512, 2048], P('fsdp')
- new_second_down: float32 [2048, 512], P('fsdp')
- new_second_vectors: float32 [6144], P('fsdp')
- copy_qkv: bfloat16 [512, 1536], P('fsdp')
- copy_out: bfloat16 [512, 512], P('fsdp')
- copy_up: bfloat16 [512, 2048], P('fsdp')
- copy_down: bfloat16 [2048, 512], P('fsdp')
- copy_vectors: bfloat16 [6144], P('fsdp')
- matrix_norms: float32 [3, 4], replicated
The draws below stay inside these ranges and needn't reach their ends.
All inputs are finite; a program needn't handle non-finite values.
Results may differ from the reference program's by a relative error of at most 0.017.
Values may be sent and summed in bfloat16 or wider, within the bound.
A program may use at most 256 MiB of HBM per device.

```python
import math
import jax
import jax.numpy as jnp
from jax import lax

D = 512
HEADS = 8
FF = 2048
HEAD_DIM = 64
SEQ = 352
MICRO = 2
STEP = 5
ROWS = 128
TOKENS = 90112
NVEC = 6144


def draw_vectors(key, part):
    index_all = jnp.arange(NVEC)
    column = index_all % (NVEC // D)
    gain_rows = (column == 0) | (column == 5)
    key_gain = jax.random.fold_in(key, 11)
    key_shift = jax.random.fold_in(key, 12)
    gains = jax.random.uniform(key_gain, (NVEC,), jnp.float32, 0.66, 1.5)
    shifts = jnp.clip(0.2 * jax.random.normal(key_shift, (NVEC,), jnp.float32), -0.6, 0.6)
    return jnp.where(gain_rows, gains, shifts).astype(jnp.float32)


def place_ends(entries, key, low, high):
    longest = entries.shape.index(max(entries.shape))
    spots = []
    for shift in (0, 1):
        where = [jax.random.randint(jax.random.fold_in(key, axis), (), 0, length) for axis, length in enumerate(entries.shape)]
        where[longest] = (where[longest] + shift) % entries.shape[longest]
        spots.append(tuple(where))
    return entries.at[spots[0]].set(low).at[spots[1]].set(high)


def levels(own_key, shape, cuts, smallest, largest):
    def one(dim, parts):
        heights = jax.random.uniform(jax.random.fold_in(jax.random.fold_in(own_key, 6), dim), (parts,), jnp.float32, smallest / len(cuts), largest / len(cuts))
        return jnp.repeat(jnp.exp(heights), shape[dim] // parts).reshape((-1,) + (1,) * (len(shape) - dim - 1))

    level = one(*cuts[0])
    for cut in cuts[1:]:
        level = level * one(*cut)
    return level


def noise(own_key, extent, width, reach, pieces=(), held_as=jnp.bfloat16):
    gain = levels(own_key, extent, pieces, -0.22, 0.18) if pieces else 1.0
    array = jax.random.normal(own_key, extent, jnp.float32) * width * gain
    return jnp.minimum(jnp.maximum(array, -reach), reach).astype(held_as)


def setup_inputs(seed: int = 0) -> dict:
    keys = jax.random.split(jax.random.key(seed), 19)
    return {
        "block_in": noise(keys[0], (MICRO, ROWS, SEQ, D), 1.0, 6.0, ((1, 32),)),
        "offsets": place_ends(jax.random.randint(keys[1], (MICRO, ROWS, 2), SEQ // 10, SEQ - SEQ // 10 + 1), jax.random.fold_in(keys[1], 1), SEQ // 10, (SEQ - SEQ // 10 + 1) - 1).astype(jnp.int32),
        "cotangent": noise(keys[2], (MICRO, ROWS, SEQ, D), 1.0, 6.0, ((1, 32),)),
        "w_qkv": noise(keys[3], (D, 3 * D), D ** -0.5, 0.25, ((0, 16),), jnp.float32),
        "w_out": noise(keys[4], (D, D), (D * 8 // SEQ) ** -0.5, 1.75, ((0, 16),), jnp.float32),
        "w_up": noise(keys[5], (D, FF), D ** -0.5, 0.25, ((0, 16),), jnp.float32),
        "w_down": noise(keys[6], (FF, D), FF ** -0.5, 0.125, ((0, 16),), jnp.float32),
        "vectors": draw_vectors(jax.random.fold_in(keys[18], 71), 0),
        "first_qkv": noise(keys[8], (D, 3 * D), (0.7 * TOKENS ** 0.5), 1280.0, ((0, 16),), jnp.float32),
        "first_out": noise(keys[9], (D, D), (0.1 * TOKENS ** 0.5), 192.0, ((0, 16),), jnp.float32),
        "first_up": noise(keys[10], (D, FF), (0.35 * TOKENS ** 0.5), 640.0, ((0, 16),), jnp.float32),
        "first_down": noise(keys[11], (FF, D), (0.6 * TOKENS ** 0.5), 1024.0, ((0, 16),), jnp.float32),
        "first_vectors": noise(keys[12], (NVEC,), (0.7 * TOKENS ** 0.5), 1280.0, ((0, 16),), jnp.float32),
        "second_qkv": jnp.clip(jnp.exp(math.log(176619.52) - 1.3862944 * jax.random.uniform(keys[13], (D, 3 * D), jnp.float32) ** levels(keys[13], (D, 3 * D), ((0, 16),), -0.2, 0.2)), 44154.88, 176619.52),
        "second_out": jnp.clip(jnp.exp(math.log(3604.48) - 1.3862944 * jax.random.uniform(keys[14], (D, D), jnp.float32) ** levels(keys[14], (D, D), ((0, 16),), -0.2, 0.2)), 901.12, 3604.48),
        "second_up": jnp.clip(jnp.exp(math.log(44154.88) - 1.4069136 * jax.random.uniform(keys[15], (D, FF), jnp.float32) ** levels(keys[15], (D, FF), ((0, 16),), -0.2, 0.2)), 10813.44, 44154.88),
        "second_down": jnp.clip(jnp.exp(math.log(129761.28) - 1.3862944 * jax.random.uniform(keys[16], (FF, D), jnp.float32) ** levels(keys[16], (FF, D), ((0, 16),), -0.2, 0.2)), 32440.32, 129761.28),
        "second_vectors": jnp.clip(jnp.exp(math.log(176619.52) - 1.3862944 * jax.random.uniform(keys[17], (NVEC,), jnp.float32) ** levels(keys[17], (NVEC,), ((0, 16),), -0.2, 0.2)), 44154.88, 176619.52),
    }


@jax.custom_vjp
def low(v):
    return lax.optimization_barrier(v.astype(jnp.bfloat16)).astype(jnp.float32)

@jax.custom_vjp
def low_back(v):
    return v

def low_keep(v):
    return (low(v), None)

def low_pass(kept, grad):
    return (grad,)

def back_keep(v):
    return (v, None)

def back_low(kept, grad):
    return (low(grad),)
low.defvjp(low_keep, low_pass)
low_back.defvjp(back_keep, back_low)
highest = lax.Precision.HIGHEST
eps_norm = 1e-05
beta_first = 0.5
beta_second = 0.5
adam_eps = 1e-06
weight_decay = 0.01
matrix_rate = 1.0
vector_rate = 0.1

def layer_norm(values, gain_vec, shift_vec):
    center = values - lax.optimization_barrier(jnp.mean(values, axis=-1, keepdims=True))
    spread = lax.optimization_barrier(jnp.mean(center * center, axis=-1, keepdims=True))
    return center * lax.rsqrt(spread + eps_norm) * gain_vec + shift_vec

def split_vectors(packed):
    table = packed.reshape(D, NVEC // D)
    columns = [table[:, position] for position in range(7)]
    bias_up = table[:, 7:NVEC // D - 1].T.reshape(FF)
    bias_down = table[:, NVEC // D - 1]
    return columns + [bias_up, bias_down]

def segment_ids(rows_offsets):
    places = jnp.arange(SEQ, dtype=jnp.int32)
    past_first = (places[None, :] >= rows_offsets[:, 0:1]).astype(jnp.int32)
    past_second = (places[None, :] >= rows_offsets[:, 1:2]).astype(jnp.int32)
    return past_first + past_second

def rows_forward(params, rows_pair):
    w_qkv, w_out, w_up, w_down, packed = params
    rows_x, rows_offsets = rows_pair
    gain_one, shift_one, bias_query, bias_value, bias_out, gain_two, shift_two, bias_up, bias_down = split_vectors(packed)
    row_count = rows_x.shape[0]
    norm_one = low(layer_norm(rows_x, gain_one, shift_one))
    zero_keys = jnp.zeros((D,), jnp.float32)
    qkv = jnp.einsum('rsd,de->rse', norm_one, w_qkv, precision=highest)
    qkv = low(low_back(qkv + jnp.concatenate([bias_query, zero_keys, bias_value])))
    queries = qkv[..., :D].reshape(row_count, SEQ, HEADS, HEAD_DIM)
    key_heads = qkv[..., D:2 * D].reshape(row_count, SEQ, HEADS, HEAD_DIM)
    value_heads = qkv[..., 2 * D:].reshape(row_count, SEQ, HEADS, HEAD_DIM)
    scores = jnp.einsum('rqhd,rkhd->rhqk', queries, key_heads, precision=highest) * HEAD_DIM ** (-0.5)
    scores = low_back(scores)
    crop_ids = segment_ids(rows_offsets)
    same_crop = (crop_ids[:, :, None] == crop_ids[:, None, :])[:, None, :, :]
    scores = jnp.where(same_crop, scores, -1e+30)
    row_peak = lax.optimization_barrier(jnp.max(scores, axis=-1, keepdims=True))
    exp_scores = jnp.exp(scores - row_peak)
    attn_probs = low(exp_scores / lax.optimization_barrier(jnp.sum(exp_scores, axis=-1, keepdims=True)))
    context = jnp.einsum('rhqk,rkhd->rqhd', attn_probs, value_heads, precision=highest).reshape(row_count, SEQ, D)
    context = low(low_back(context))
    attention = jnp.einsum('rsd,de->rse', context, w_out, precision=highest) + bias_out
    middle = rows_x + low_back(attention)
    norm_two = low(layer_norm(middle, gain_two, shift_two))
    up_values = low_back(jnp.einsum('rsd,df->rsf', norm_two, w_up, precision=highest) + bias_up)
    active = low(jax.nn.gelu(up_values, approximate=True))
    return middle + jnp.einsum('rsf,fd->rsd', active, w_down, precision=highest) + bias_down

def reference(block_in, offsets, cotangent, w_qkv, w_out, w_up, w_down, vectors, first_qkv, first_out, first_up, first_down, first_vectors, second_qkv, second_out, second_up, second_down, second_vectors):
    masters = (w_qkv, w_out, w_up, w_down, vectors)
    firsts = (first_qkv, first_out, first_up, first_down, first_vectors)
    seconds = (second_qkv, second_out, second_up, second_down, second_vectors)
    params = tuple((lax.optimization_barrier(master.astype(jnp.bfloat16)).astype(jnp.float32) for master in masters))
    total_rows = MICRO * ROWS
    group_rows = math.gcd(total_rows, 8)
    inputs = block_in.astype(jnp.float32).reshape(total_rows // group_rows, group_rows, SEQ, D)
    offset_groups = offsets.reshape(total_rows // group_rows, group_rows, 2).astype(jnp.int32)

    def forward_all(params, inputs):

        def one_group(rows_pair):
            return jax.checkpoint(rows_forward)(params, rows_pair)
        return lax.map(one_group, (inputs, offset_groups))
    outputs, pull_back = jax.vjp(forward_all, params, inputs)
    grad_all, input_grad = pull_back(cotangent.astype(jnp.float32).reshape(inputs.shape))
    correct_first = 1.0 - beta_first ** STEP
    correct_second = 1.0 - beta_second ** STEP
    new_masters = []
    new_firsts = []
    new_seconds = []
    weight_norms = []
    update_norms = []
    trust_ratios = []
    for position in range(5):
        gradient = grad_all[position]
        new_first = beta_first * firsts[position] + (1.0 - beta_first) * gradient
        new_second = beta_second * seconds[position] + (1.0 - beta_second) * gradient * gradient
        direction = new_first / correct_first / (jnp.sqrt(new_second / correct_second) + adam_eps)
        master = masters[position]
        if position < 4:
            update = direction + weight_decay * master
            weight_norm = jnp.sqrt(jnp.sum(master * master))
            update_norm = jnp.sqrt(jnp.sum(update * update))
            trust_ratio = weight_norm / update_norm
            new_master = master - matrix_rate * trust_ratio * update
            weight_norms.append(weight_norm)
            update_norms.append(update_norm)
            trust_ratios.append(trust_ratio)
        else:
            new_master = master - vector_rate * direction
        new_masters.append(new_master)
        new_firsts.append(new_first)
        new_seconds.append(new_second)
    matrix_norms = jnp.stack([jnp.stack(weight_norms), jnp.stack(update_norms), jnp.stack(trust_ratios)])
    block_out = outputs.reshape(MICRO, ROWS, SEQ, D).astype(jnp.bfloat16)
    input_grad = input_grad.reshape(MICRO, ROWS, SEQ, D)
    return (block_out, input_grad, new_masters[0], new_masters[1], new_masters[2], new_masters[3], new_masters[4], new_firsts[0], new_firsts[1], new_firsts[2], new_firsts[3], new_firsts[4], new_seconds[0], new_seconds[1], new_seconds[2], new_seconds[3], new_seconds[4], new_masters[0].astype(jnp.bfloat16), new_masters[1].astype(jnp.bfloat16), new_masters[2].astype(jnp.bfloat16), new_masters[3].astype(jnp.bfloat16), new_masters[4].astype(jnp.bfloat16), matrix_norms)
```

```python
import jax
import jax.numpy as jnp
from jax import lax
from jax.experimental import pallas as pl
from jax.experimental.pallas import tpu as pltpu
from jax.sharding import PartitionSpec as P

HEADS = 8
HEAD_DIM = 64
STEP = 5
beta_first = 0.5
beta_second = 0.5
adam_eps = 1e-06
weight_decay = 0.01
matrix_rate = 1.0
vector_rate = 0.1
EPS = 1e-05
F32 = jnp.float32
BF16 = jnp.bfloat16
GROUP = 2
NEG = -1e30
C0 = 0.7978845608028654
C1 = 0.044715
LANES = 128


def nn(a, b):
    return lax.dot_general(a, b, (((1,), (0,)), ((), ())), preferred_element_type=F32)


def nt(a, b):
    return lax.dot_general(a, b, (((1,), (1,)), ((), ())), preferred_element_type=F32)


def tn(a, b):
    return lax.dot_general(a, b, (((0,), (0,)), ((), ())), preferred_element_type=F32)


def xhat_of(v):
    center = v - jnp.mean(v, axis=-1, keepdims=True)
    spread = jnp.mean(center * center, axis=-1, keepdims=True)
    inv = lax.rsqrt(spread + EPS)
    return center * inv, inv


def norm_back(e, xhat, inv):
    return (e - jnp.mean(e, axis=-1, keepdims=True) - xhat * jnp.mean(e * xhat, axis=-1, keepdims=True)) * inv


def crop_of(first, second, shape, axis):
    t = lax.broadcasted_iota(jnp.int32, shape, axis)
    return (t >= first).astype(jnp.int32) + (t >= second).astype(jnp.int32)


def col_sum(v):
    return jnp.sum(v, axis=0, keepdims=True)


def kernel_a(off_ref, x_ref, cot_ref, wqkv_ref, wout_ref, wup_ref, wdn_ref, vec_ref,
             y_ref, qkv_ref, bctx_ref, bmid_ref, gup_out, gdn_out, gout_out, sums_ref,
             gup_ref, gdn_ref, gout_ref, p_ref, ctx_ref, bias_ref, v_ref):
    step = pl.program_id(0)
    rows, length, width = x_ref.shape
    tokens = rows * length
    padded = p_ref.shape[1] // 2
    chunks = wup_ref.shape[1] // width

    @pl.when(step == 0)
    def _():
        gup_ref[...] = jnp.zeros_like(gup_ref)
        gdn_ref[...] = jnp.zeros_like(gdn_ref)
        gout_ref[...] = jnp.zeros_like(gout_ref)
        sums_ref[...] = jnp.zeros_like(sums_ref)
        v_ref[...] = jnp.zeros_like(v_ref)

    x = x_ref[...].reshape(tokens, width).astype(F32)
    xhat, _ = xhat_of(x)
    n1 = (xhat * vec_ref[0:1, :] + vec_ref[1:2, :]).astype(BF16)
    q = (nn(n1, wqkv_ref[:, :width]) + vec_ref[2:3, :]) * HEAD_DIM ** (-0.5)
    qkv_ref[:, :, 0:width] = q.astype(BF16).reshape(rows, length, width)
    qkv_ref[:, :, width:2 * width] = nn(n1, wqkv_ref[:, width:2 * width]).astype(BF16).reshape(rows, length, width)
    v = nn(n1, wqkv_ref[:, 2 * width:]) + vec_ref[3:4, :]
    qkv_ref[:, :, 2 * width:] = v.astype(BF16).reshape(rows, length, width)

    low = lax.broadcasted_iota(jnp.int32, (1, LANES), 1) < HEAD_DIM
    for r in range(rows):
        row = step * rows + r
        crop_q = crop_of(off_ref[2 * row], off_ref[2 * row + 1], (length, 1), 0)
        crop_k = crop_of(off_ref[2 * row], off_ref[2 * row + 1], (1, length), 1)
        bias_ref[...] = jnp.where(crop_q == crop_k, 0.0, NEG)
        for pair in range(width // LANES):
            lanes = slice(pair * LANES, (pair + 1) * LANES)
            qp = qkv_ref[r, :, lanes]
            kp = qkv_ref[r, :, width + pair * LANES:width + (pair + 1) * LANES]
            vp = qkv_ref[r, :, 2 * width + pair * LANES:2 * width + (pair + 1) * LANES]
            total = None
            for half in range(2):
                keep = low if half == 0 else jnp.logical_not(low)
                s = nt(jnp.where(keep, qp, jnp.zeros_like(qp)), kp) + bias_ref[...]
                e = jnp.exp(s - jnp.max(s, axis=-1, keepdims=True))
                p = (e * (1.0 / jnp.sum(e, axis=-1, keepdims=True))).astype(BF16)
                part = nn(p, jnp.where(keep, vp, jnp.zeros_like(vp)))
                total = part if total is None else total + part
            ctx_ref[r, :, lanes] = total.astype(BF16)

    ctx = ctx_ref[...].reshape(tokens, width)
    middle = x_ref[...].reshape(tokens, width).astype(F32) + (nn(ctx, wout_ref[...]) + vec_ref[4:5, :])
    xhat2, inv2 = xhat_of(middle)
    n2 = (xhat2 * vec_ref[5:6, :] + vec_ref[6:7, :]).astype(BF16)
    cot = cot_ref[...].reshape(tokens, width)
    result = middle + vec_ref[7 + chunks:8 + chunks, :]
    back_n2 = jnp.zeros((tokens, width), F32)
    for u in range(chunks):
        cols = slice(u * width, (u + 1) * width)
        up = nn(n2, wup_ref[:, cols]) + vec_ref[7 + u:8 + u, :]
        square = up * up
        th = jnp.tanh(up * (C0 + (C0 * C1) * square))
        half_up = 0.5 * up
        active = (half_up + half_up * th).astype(BF16)
        slope = (0.5 + 0.5 * th) + half_up * (1.0 - th * th) * (C0 + (3.0 * C0 * C1) * square)
        back_up = nt(cot, wdn_ref[cols, :]) * slope
        sums_ref[7 + u:8 + u, :] += col_sum(back_up)
        back_up = back_up.astype(BF16)
        result = result + nn(active, wdn_ref[cols, :])
        back_n2 = back_n2 + nt(back_up, wup_ref[:, cols])
        gdn_ref[:, cols] += tn(cot, active)
        gup_ref[:, cols] += tn(n2, back_up)
    y_ref[...] = result.astype(BF16).reshape(rows, length, width)
    cot32 = cot.astype(F32)
    sums_ref[7 + chunks:8 + chunks, :] += col_sum(cot32)
    sums_ref[5:6, :] += col_sum(back_n2 * xhat2)
    sums_ref[6:7, :] += col_sum(back_n2)
    back_middle = cot32 + norm_back(back_n2 * vec_ref[5:6, :], xhat2, inv2)
    bmid_ref[...] = back_middle.reshape(rows, length, width)
    back_att = back_middle.astype(BF16)
    sums_ref[4:5, :] += col_sum(back_middle)
    gout_ref[...] += tn(ctx, back_att)
    bctx_ref[...] = nt(back_att, wout_ref[...]).astype(BF16).reshape(rows, length, width)

    @pl.when(step == pl.num_programs(0) - 1)
    def _():
        gup_out[...] = gup_ref[...].astype(gup_out.dtype)
        gout_out[...] = gout_ref[...].astype(gout_out.dtype)
        for u in range(chunks):
            gdn_out[u * width:(u + 1) * width, :] = gdn_ref[:, u * width:(u + 1) * width].T.astype(gdn_out.dtype)


def kernel_b(off_ref, x_ref, qkv_ref, bctx_ref, bmid_ref, wqkv_ref, vec_ref,
             xgrad_ref, gqkv_out, sums_ref, gqkv_ref, bqkv_ref, bias_ref):
    step = pl.program_id(0)
    rows, length, width = x_ref.shape
    tokens = rows * length

    @pl.when(step == 0)
    def _():
        gqkv_ref[...] = jnp.zeros_like(gqkv_ref)
        sums_ref[...] = jnp.zeros_like(sums_ref)

    low = lax.broadcasted_iota(jnp.int32, (1, LANES), 1) < HEAD_DIM
    for r in range(rows):
        row = step * rows + r
        crop_k = crop_of(off_ref[2 * row], off_ref[2 * row + 1], (length, 1), 0)
        crop_q = crop_of(off_ref[2 * row], off_ref[2 * row + 1], (1, length), 1)
        bias_ref[...] = jnp.where(crop_q == crop_k, 0.0, NEG)
        for pair in range(width // LANES):
            lanes = slice(pair * LANES, (pair + 1) * LANES)
            klanes = slice(width + pair * LANES, width + (pair + 1) * LANES)
            vlanes = slice(2 * width + pair * LANES, 2 * width + (pair + 1) * LANES)
            qp = qkv_ref[r, :, lanes]
            kp = qkv_ref[r, :, klanes]
            vp = qkv_ref[r, :, vlanes]
            op = bctx_ref[r, :, lanes]
            dq = dk = dv = None
            for half in range(2):
                keep = low if half == 0 else jnp.logical_not(low)
                zero = jnp.zeros_like(qp)
                qh = jnp.where(keep, qp, zero)
                oh = jnp.where(keep, op, zero)
                s = nt(kp, qh) + bias_ref[...]
                e = jnp.exp(s - jnp.max(s, axis=0, keepdims=True))
                p = e * (1.0 / jnp.sum(e, axis=0, keepdims=True))
                dp = nt(vp, oh)
                ds = (p * (dp - jnp.sum(p * dp, axis=0, keepdims=True))).astype(BF16)
                dv_h = nn(p.astype(BF16), oh)
                dk_h = nn(ds, qh)
                dq_h = tn(ds, jnp.where(keep, kp, zero))
                dq = dq_h if dq is None else dq + dq_h
                dk = dk_h if dk is None else dk + dk_h
                dv = dv_h if dv is None else dv + dv_h
            bqkv_ref[r, :, lanes] = (dq * HEAD_DIM ** (-0.5)).astype(BF16)
            bqkv_ref[r, :, klanes] = dk.astype(BF16)
            bqkv_ref[r, :, vlanes] = dv.astype(BF16)

    x = x_ref[...].reshape(tokens, width).astype(F32)
    xhat, inv = xhat_of(x)
    n1 = (xhat * vec_ref[0:1, :] + vec_ref[1:2, :]).astype(BF16)
    back = bqkv_ref[...].reshape(tokens, 3 * width)
    sums_ref[2:3, :] += col_sum(back[:, :width].astype(F32))
    sums_ref[3:4, :] += col_sum(back[:, 2 * width:].astype(F32))
    back_n1 = None
    for part in range(3):
        cols = slice(part * width, (part + 1) * width)
        gqkv_ref[:, cols] += tn(n1, back[:, cols])
        term = nt(back[:, cols], wqkv_ref[:, cols])
        back_n1 = term if back_n1 is None else back_n1 + term
    sums_ref[0:1, :] += col_sum(back_n1 * xhat)
    sums_ref[1:2, :] += col_sum(back_n1)
    grad = bmid_ref[...].reshape(tokens, width) + norm_back(back_n1 * vec_ref[0:1, :], xhat, inv)
    xgrad_ref[...] = grad.reshape(rows, length, width)

    @pl.when(step == pl.num_programs(0) - 1)
    def _():
        gqkv_out[...] = gqkv_ref[...].astype(gqkv_out.dtype)


def whole(shape):
    return pl.BlockSpec(shape, lambda s, *_: (0,) * len(shape), pipeline_mode=pl.Buffered(1))


def per_step(shape):
    return pl.BlockSpec(shape, lambda s, *_: (s,) + (0,) * (len(shape) - 1))


def phase_a(off, x, cot, wqkv, wout, wup, wdn, vec, grad_dtype=BF16):
    rows, length, width = x.shape
    hidden = wup.shape[1]
    padded = -(-length // LANES) * LANES
    blk = lambda w: per_step((GROUP, length, w))
    sds = jax.ShapeDtypeStruct
    return pl.pallas_call(
        kernel_a,
        name="phase_a",
        grid_spec=pltpu.PrefetchScalarGridSpec(
            num_scalar_prefetch=1,
            grid=(rows // GROUP,),
            in_specs=[blk(width), blk(width), whole(wqkv.shape), whole(wout.shape), whole(wup.shape),
                      whole(wdn.shape), whole(vec.shape)],
            out_specs=[blk(width), blk(3 * width), blk(width), blk(width), whole((width, hidden)),
                       whole((hidden, width)), whole((width, width)), whole((16, width))],
            scratch_shapes=[
                pltpu.VMEM((width, hidden), F32), pltpu.VMEM((width, hidden), F32), pltpu.VMEM((width, width), F32),
                pltpu.VMEM((length, 2 * padded), BF16), pltpu.VMEM((GROUP, length, width), BF16),
                pltpu.VMEM((length, length), F32), pltpu.VMEM((2 * padded, LANES), BF16)],
        ),
        out_shape=[sds(x.shape, BF16), sds((rows, length, 3 * width), BF16), sds(x.shape, BF16), sds(x.shape, F32),
                   sds((width, hidden), grad_dtype), sds((hidden, width), grad_dtype), sds((width, width), grad_dtype),
                   sds((16, width), F32)],
        compiler_params=pltpu.CompilerParams(vmem_limit_bytes=62 << 20),
    )(off, x, cot, wqkv, wout, wup, wdn, vec)


def phase_b(off, x, qkv, bctx, bmid, wqkv, vec, grad_dtype=BF16):
    rows, length, width = x.shape
    blk = lambda w: per_step((GROUP, length, w))
    sds = jax.ShapeDtypeStruct
    return pl.pallas_call(
        kernel_b,
        name="phase_b",
        grid_spec=pltpu.PrefetchScalarGridSpec(
            num_scalar_prefetch=1,
            grid=(rows // GROUP,),
            in_specs=[blk(width), blk(3 * width), blk(width), blk(width), whole(wqkv.shape), whole(vec.shape)],
            out_specs=[blk(width), whole(wqkv.shape), whole((16, width))],
            scratch_shapes=[pltpu.VMEM(wqkv.shape, F32), pltpu.VMEM((GROUP, length, 3 * width), BF16),
                            pltpu.VMEM((length, length), F32)],
        ),
        out_shape=[sds(x.shape, F32), sds(wqkv.shape, grad_dtype), sds((16, width), F32)],
        compiler_params=pltpu.CompilerParams(vmem_limit_bytes=62 << 20),
    )(off, x, qkv, bctx, bmid, wqkv, vec)


def shards(block_in, offsets, cotangent, w_qkv, w_out, w_up, w_down, vectors, *moments):
    masters = (w_qkv, w_out, w_up, w_down, vectors)
    firsts, seconds = moments[:5], moments[5:]
    micro, local_rows, length, width = block_in.shape
    rows = micro * local_rows
    copies = [m.astype(BF16) for m in masters]
    wqkv, wout, wup, wdn, packed = [lax.all_gather(c, "fsdp", axis=0, tiled=True) for c in copies]
    vec = jnp.pad(packed.reshape(width, -1).T.astype(F32), ((0, 4), (0, 0)))
    columns = packed.shape[0] // width
    x = block_in.reshape(rows, length, width)
    cot = cotangent.reshape(rows, length, width)
    off = offsets.reshape(-1)
    y, qkv, bctx, bmid, gup, gdn, gout, sums_a = phase_a(off, x, cot, wqkv, wout, wup, wdn, vec)
    xgrad, gqkv, sums_b = phase_b(off, x, qkv, bctx, bmid, wqkv, vec)
    gvec = (sums_a + sums_b)[:columns].T.reshape(-1)
    scattered = [lax.psum_scatter(g, "fsdp", scatter_dimension=0, tiled=True) for g in (gqkv, gout, gup, gdn, gvec)]
    grads = [g.astype(F32) for g in lax.psum(tuple(g.astype(BF16) for g in scattered), "dp")]
    correct_first, correct_second = 1.0 - beta_first**STEP, 1.0 - beta_second**STEP
    new_firsts = [beta_first * m + (1.0 - beta_first) * g for m, g in zip(firsts, grads)]
    new_seconds = [beta_second * s + (1.0 - beta_second) * g * g for s, g in zip(seconds, grads)]
    directions = [m / correct_first / (jnp.sqrt(s / correct_second) + adam_eps) for m, s in zip(new_firsts, new_seconds)]
    updates = [d + weight_decay * w for d, w in zip(directions[:4], masters)]
    squares = jnp.stack([jnp.sum(w * w) for w in masters[:4]] + [jnp.sum(u * u) for u in updates])
    squares = jnp.sqrt(lax.psum(squares, "fsdp"))
    weight_norms, update_norms = squares[:4], squares[4:]
    trust = weight_norms / update_norms
    new_masters = [w - matrix_rate * t * u for w, t, u in zip(masters, trust, updates)]
    new_masters.append(vectors - vector_rate * directions[4])
    return (y.reshape(block_in.shape), xgrad.reshape(block_in.shape), *new_masters, *new_firsts, *new_seconds,
            *[m.astype(BF16) for m in new_masters], jnp.stack([weight_norms, update_norms, trust]))


def solution(mesh):
    batch, matrix, vector = P(None, ("fsdp", "dp"), None, None), P("fsdp", None), P("fsdp")
    params = (matrix,) * 4 + (vector,)
    in_specs = (batch, P(None, ("fsdp", "dp"), None), batch) + params * 3
    out_specs = (batch, batch) + params * 4 + (P(),)
    return jax.shard_map(shards, mesh=mesh, in_specs=in_specs, out_specs=out_specs, check_vma=False)
```

```python
import jax
import jax.numpy as jnp
from jax import lax
from jax.experimental import pallas as pl
from jax.experimental.pallas import tpu as pltpu
from jax.sharding import PartitionSpec as P

HEAD_DIM = 64
STEP = 5
beta_first = 0.5
beta_second = 0.5
adam_eps = 1e-06
weight_decay = 0.01
matrix_rate = 1.0
vector_rate = 0.1
CHIPS = 16
MESH = pl.DeviceIdType.MESH
EPS = 1e-05
F32 = jnp.float32
BF16 = jnp.bfloat16
GROUP = 2
NEG = -1e30
C0 = 0.7978845608028654
C1 = 0.044715
LANES = 128


def nn(a, b):
    return lax.dot_general(a, b, (((1,), (0,)), ((), ())), preferred_element_type=F32)


def nt(a, b):
    return lax.dot_general(a, b, (((1,), (1,)), ((), ())), preferred_element_type=F32)


def tn(a, b):
    return lax.dot_general(a, b, (((0,), (0,)), ((), ())), preferred_element_type=F32)


def xhat_of(v):
    center = v - jnp.mean(v, axis=-1, keepdims=True)
    spread = jnp.mean(center * center, axis=-1, keepdims=True)
    inv = lax.rsqrt(spread + EPS)
    return center * inv, inv


def norm_back(e, xhat, inv):
    return (e - jnp.mean(e, axis=-1, keepdims=True) - xhat * jnp.mean(e * xhat, axis=-1, keepdims=True)) * inv


def crop_of(first, second, shape, axis):
    t = lax.broadcasted_iota(jnp.int32, shape, axis)
    return (t >= first).astype(jnp.int32) + (t >= second).astype(jnp.int32)


def col_sum(v):
    return jnp.sum(v, axis=0, keepdims=True)


def kernel_a(off_ref, x_ref, cot_ref, w1_ref, w2_ref, w3_ref,
             y_ref, qkv_ref, bctx_ref, bmid_ref, g2_out, g3_out, sums_ref,
             gup_ref, gdn_ref, gout_ref, ctx_ref, bias_ref, vec_ref):
    step = pl.program_id(0)
    rows, length, width = x_ref.shape
    tokens = rows * length
    hidden = w3_ref.shape[0]
    chunks = hidden // width
    wqkv_ref, wdn_ref = w1_ref.at[:, 0:3 * width], w3_ref
    wout_ref, wup_ref = w2_ref.at[:, 0:width], w2_ref.at[:, width:width + hidden]

    @pl.when(step == 0)
    def _():
        gup_ref[...] = jnp.zeros_like(gup_ref)
        gdn_ref[...] = jnp.zeros_like(gdn_ref)
        gout_ref[...] = jnp.zeros_like(gout_ref)
        sums_ref[...] = jnp.zeros_like(sums_ref)
        vec_ref[...] = w1_ref[:, 3 * width:].astype(F32).T

    x = x_ref[...].reshape(tokens, width).astype(F32)
    xhat, _ = xhat_of(x)
    n1 = (xhat * vec_ref[0:1, :] + vec_ref[1:2, :]).astype(BF16)
    q = (nn(n1, wqkv_ref[:, :width]) + vec_ref[2:3, :]) * HEAD_DIM ** (-0.5)
    qkv_ref[:, :, 0:width] = q.astype(BF16).reshape(rows, length, width)
    qkv_ref[:, :, width:2 * width] = nn(n1, wqkv_ref[:, width:2 * width]).astype(BF16).reshape(rows, length, width)
    v = nn(n1, wqkv_ref[:, 2 * width:]) + vec_ref[3:4, :]
    qkv_ref[:, :, 2 * width:] = v.astype(BF16).reshape(rows, length, width)

    low = lax.broadcasted_iota(jnp.int32, (1, LANES), 1) < HEAD_DIM
    for r in range(rows):
        row = step * rows + r
        crop_q = crop_of(off_ref[2 * row], off_ref[2 * row + 1], (length, 1), 0)
        crop_k = crop_of(off_ref[2 * row], off_ref[2 * row + 1], (1, length), 1)
        bias_ref[...] = jnp.where(crop_q == crop_k, 0.0, NEG)
        for pair in range(width // LANES):
            lanes = slice(pair * LANES, (pair + 1) * LANES)
            qp = qkv_ref[r, :, lanes]
            kp = qkv_ref[r, :, width + pair * LANES:width + (pair + 1) * LANES]
            vp = qkv_ref[r, :, 2 * width + pair * LANES:2 * width + (pair + 1) * LANES]
            total = None
            for half in range(2):
                keep = low if half == 0 else jnp.logical_not(low)
                s = nt(jnp.where(keep, qp, jnp.zeros_like(qp)), kp) + bias_ref[...]
                e = jnp.exp(s - jnp.max(s, axis=-1, keepdims=True))
                p = (e * (1.0 / jnp.sum(e, axis=-1, keepdims=True))).astype(BF16)
                part = nn(p, jnp.where(keep, vp, jnp.zeros_like(vp)))
                total = part if total is None else total + part
            ctx_ref[r, :, lanes] = total.astype(BF16)

    ctx = ctx_ref[...].reshape(tokens, width)
    middle = x_ref[...].reshape(tokens, width).astype(F32) + (nn(ctx, wout_ref[...]) + vec_ref[4:5, :])
    xhat2, inv2 = xhat_of(middle)
    n2 = (xhat2 * vec_ref[5:6, :] + vec_ref[6:7, :]).astype(BF16)
    cot = cot_ref[...].reshape(tokens, width)
    result = middle + vec_ref[7 + chunks:8 + chunks, :]
    back_n2 = jnp.zeros((tokens, width), F32)
    for u in range(chunks):
        cols = slice(u * width, (u + 1) * width)
        up = nn(n2, wup_ref[:, cols]) + vec_ref[7 + u:8 + u, :]
        square = up * up
        th = jnp.tanh(up * (C0 + (C0 * C1) * square))
        half_up = 0.5 * up
        active = (half_up + half_up * th).astype(BF16)
        slope = (0.5 + 0.5 * th) + half_up * (1.0 - th * th) * (C0 + (3.0 * C0 * C1) * square)
        back_up = nt(cot, wdn_ref[cols, :]) * slope
        sums_ref[7 + u:8 + u, :] += col_sum(back_up)
        back_up = back_up.astype(BF16)
        result = result + nn(active, wdn_ref[cols, :])
        back_n2 = back_n2 + nt(back_up, wup_ref[:, cols])
        gdn_ref[:, cols] += tn(cot, active)
        gup_ref[:, cols] += tn(n2, back_up)
    y_ref[...] = result.astype(BF16).reshape(rows, length, width)
    cot32 = cot.astype(F32)
    sums_ref[7 + chunks:8 + chunks, :] += col_sum(cot32)
    sums_ref[5:6, :] += col_sum(back_n2 * xhat2)
    sums_ref[6:7, :] += col_sum(back_n2)
    back_middle = cot32 + norm_back(back_n2 * vec_ref[5:6, :], xhat2, inv2)
    bmid_ref[...] = back_middle.reshape(rows, length, width)
    back_att = back_middle.astype(BF16)
    sums_ref[4:5, :] += col_sum(back_middle)
    gout_ref[...] += tn(ctx, back_att)
    bctx_ref[...] = nt(back_att, wout_ref[...]).astype(BF16).reshape(rows, length, width)

    @pl.when(step == pl.num_programs(0) - 1)
    def _():
        g2_out[:, 0:width] = gout_ref[...].astype(BF16)
        g2_out[:, width:] = gup_ref[...].astype(BF16)
        for u in range(chunks):
            g3_out[u * width:(u + 1) * width, :] = gdn_ref[:, u * width:(u + 1) * width].T.astype(BF16)


def kernel_b(off_ref, x_ref, qkv_ref, bctx_ref, bmid_ref, w1_ref, sums_a_ref,
             xgrad_ref, g1_out, gqkv_ref, bqkv_ref, bias_ref, sums_ref, vec_ref):
    step = pl.program_id(0)
    rows, length, width = x_ref.shape
    tokens = rows * length

    @pl.when(step == 0)
    def _():
        gqkv_ref[...] = jnp.zeros_like(gqkv_ref)
        sums_ref[...] = sums_a_ref[...]
        vec_ref[...] = w1_ref[:, 3 * width:].astype(F32).T

    low = lax.broadcasted_iota(jnp.int32, (1, LANES), 1) < HEAD_DIM
    for r in range(rows):
        row = step * rows + r
        crop_k = crop_of(off_ref[2 * row], off_ref[2 * row + 1], (length, 1), 0)
        crop_q = crop_of(off_ref[2 * row], off_ref[2 * row + 1], (1, length), 1)
        bias_ref[...] = jnp.where(crop_q == crop_k, 0.0, NEG)
        for pair in range(width // LANES):
            lanes = slice(pair * LANES, (pair + 1) * LANES)
            klanes = slice(width + pair * LANES, width + (pair + 1) * LANES)
            vlanes = slice(2 * width + pair * LANES, 2 * width + (pair + 1) * LANES)
            qp = qkv_ref[r, :, lanes]
            kp = qkv_ref[r, :, klanes]
            vp = qkv_ref[r, :, vlanes]
            op = bctx_ref[r, :, lanes]
            dq = dk = dv = None
            for half in range(2):
                keep = low if half == 0 else jnp.logical_not(low)
                zero = jnp.zeros_like(qp)
                qh = jnp.where(keep, qp, zero)
                oh = jnp.where(keep, op, zero)
                s = nt(kp, qh) + bias_ref[...]
                e = jnp.exp(s - jnp.max(s, axis=0, keepdims=True))
                p = e * (1.0 / jnp.sum(e, axis=0, keepdims=True))
                dp = nt(vp, oh)
                ds = (p * (dp - jnp.sum(p * dp, axis=0, keepdims=True))).astype(BF16)
                dv_h = nn(p.astype(BF16), oh)
                dk_h = nn(ds, qh)
                dq_h = tn(ds, jnp.where(keep, kp, zero))
                dq = dq_h if dq is None else dq + dq_h
                dk = dk_h if dk is None else dk + dk_h
                dv = dv_h if dv is None else dv + dv_h
            bqkv_ref[r, :, lanes] = (dq * HEAD_DIM ** (-0.5)).astype(BF16)
            bqkv_ref[r, :, klanes] = dk.astype(BF16)
            bqkv_ref[r, :, vlanes] = dv.astype(BF16)

    x = x_ref[...].reshape(tokens, width).astype(F32)
    xhat, inv = xhat_of(x)
    n1 = (xhat * vec_ref[0:1, :] + vec_ref[1:2, :]).astype(BF16)
    back = bqkv_ref[...].reshape(tokens, 3 * width)
    sums_ref[2:3, :] += col_sum(back[:, :width].astype(F32))
    sums_ref[3:4, :] += col_sum(back[:, 2 * width:].astype(F32))
    back_n1 = None
    for part in range(3):
        cols = slice(part * width, (part + 1) * width)
        gqkv_ref[:, cols] += tn(n1, back[:, cols])
        term = nt(back[:, cols], w1_ref[:, cols])
        back_n1 = term if back_n1 is None else back_n1 + term
    sums_ref[0:1, :] += col_sum(back_n1 * xhat)
    sums_ref[1:2, :] += col_sum(back_n1)
    grad = bmid_ref[...].reshape(tokens, width) + norm_back(back_n1 * vec_ref[0:1, :], xhat, inv)
    xgrad_ref[...] = grad.reshape(rows, length, width)

    @pl.when(step == pl.num_programs(0) - 1)
    def _():
        g1_out[:, 0:3 * width] = gqkv_ref[...].astype(BF16)
        g1_out[:, 3 * width:] = sums_ref[...].T.astype(BF16)


def whole(shape):
    return pl.BlockSpec(shape, lambda s, *_: (0,) * len(shape), pipeline_mode=pl.Buffered(1))


def per_step(shape):
    return pl.BlockSpec(shape, lambda s, *_: (s,) + (0,) * (len(shape) - 1))


def phase_a(off, x, cot, w1, w2, w3):
    rows, length, width = x.shape
    hidden = w3.shape[0]
    blk = lambda w: per_step((GROUP, length, w))
    sds = jax.ShapeDtypeStruct
    return pl.pallas_call(
        kernel_a,
        name="phase_a",
        grid_spec=pltpu.PrefetchScalarGridSpec(
            num_scalar_prefetch=1,
            grid=(rows // GROUP,),
            in_specs=[blk(width), blk(width), whole(w1.shape), whole(w2.shape), whole(w3.shape)],
            out_specs=[blk(width), blk(3 * width), blk(width), blk(width), whole(w2.shape), whole(w3.shape), whole((LANES, width))],
            scratch_shapes=[
                pltpu.VMEM((width, hidden), F32), pltpu.VMEM((width, hidden), F32), pltpu.VMEM((width, width), F32),
                pltpu.VMEM((GROUP, length, width), BF16), pltpu.VMEM((length, length), F32), pltpu.VMEM((LANES, width), F32)],
        ),
        out_shape=[sds(x.shape, BF16), sds((rows, length, 3 * width), BF16), sds(x.shape, BF16), sds(x.shape, F32),
                   sds(w2.shape, BF16), sds(w3.shape, BF16), sds((LANES, width), F32)],
        compiler_params=pltpu.CompilerParams(vmem_limit_bytes=62 << 20),
    )(off, x, cot, w1, w2, w3)


def phase_b(off, x, qkv, bctx, bmid, w1, sums_a):
    rows, length, width = x.shape
    blk = lambda w: per_step((GROUP, length, w))
    sds = jax.ShapeDtypeStruct
    return pl.pallas_call(
        kernel_b,
        name="phase_b",
        grid_spec=pltpu.PrefetchScalarGridSpec(
            num_scalar_prefetch=1,
            grid=(rows // GROUP,),
            in_specs=[blk(width), blk(3 * width), blk(width), blk(width), whole(w1.shape), whole(sums_a.shape)],
            out_specs=[blk(width), whole(w1.shape)],
            scratch_shapes=[pltpu.VMEM((width, 3 * width), F32), pltpu.VMEM((GROUP, length, 3 * width), BF16),
                            pltpu.VMEM((length, length), F32), pltpu.VMEM((LANES, width), F32), pltpu.VMEM((LANES, width), F32)],
        ),
        out_shape=[sds(x.shape, F32), sds(w1.shape, BF16)],
        compiler_params=pltpu.CompilerParams(vmem_limit_bytes=62 << 20),
    )(off, x, qkv, bctx, bmid, w1, sums_a)


def place():
    chip = lax.axis_index("fsdp")
    core = lax.axis_index("dp")
    return chip, core


def partner(chip, flip):
    out = chip
    for bit in (1, 2, 4, 8):
        if flip & bit:
            out = out + bit - 2 * bit * lax.rem(chip // bit, 2)
    return out


def meet(chip, core):
    barrier = pltpu.get_barrier_semaphore()
    flips = list(range(1, CHIPS))
    for flip in flips:
        pl.semaphore_signal(barrier, inc=1, device_id=(partner(chip, flip), core), device_id_type=MESH)
    pl.semaphore_signal(barrier, inc=1, device_id=(chip, 1 - core), device_id_type=MESH)
    pl.semaphore_wait(barrier, len(flips) + 1)


def remote(src, dst, send_sem, recv_sem, chip, core):
    return pltpu.make_async_remote_copy(src_ref=src, dst_ref=dst, send_sem=send_sem, recv_sem=recv_sem,
                                        device_id=(chip, core), device_id_type=MESH)


class Gather:
    def __init__(self, own, whole, send, near, far, twin, local, chip, core):
        self.own, self.whole, self.chip, self.core = own, whole, chip, core
        self.send, self.near, self.far, self.twin, self.local = send, near, far, twin, local
        rows, cols = own.shape
        self.half = rows // 2
        self.sent = []
        if self.half >= 32:
            q = self.half // 2
            self.cuts = [(pl.ds(core * self.half + i * q, q), slice(None)) for i in range(2)]
        else:
            q = cols // 256 * 128
            self.cuts = [(pl.ds(core * self.half, self.half), pl.ds(0, q)), (pl.ds(core * self.half, self.half), pl.ds(q, cols - q))]
        self.mine = (pl.ds(core * self.half, self.half), slice(None))

    def push(self, src, shard, cut, sem, chip, core):
        copy = remote(src, self.whole.at[shard, cut[0], cut[1]], self.send, sem.at[shard], chip, core)
        copy.start()
        self.sent.append(copy)

    def held(self, shard, cut):
        return self.whole.at[shard, cut[0], cut[1]]

    def wait(self, shard, cut, sem):
        ref = self.held(shard, cut)
        pltpu.make_async_copy(ref, ref, sem.at[shard]).wait()

    def start(self):
        pltpu.make_async_copy(self.own, self.whole.at[self.chip], self.local).start()
        for flip in (1, 2, 4, 8, 12):
            self.push(self.own.at[self.mine[0], self.mine[1]], self.chip, self.mine, self.near, partner(self.chip, flip), self.core)

    def to_twin(self, shard):
        copy = remote(self.held(shard, self.mine), self.held(shard, self.mine), self.send, self.twin, self.chip, 1 - self.core)
        copy.start()
        self.sent.append(copy)

    def spread(self):
        for flip in (4, 8, 12):
            shard = partner(self.chip, flip)
            self.wait(shard, self.mine, self.near)
            for to in (1, 2):
                self.push(self.held(shard, self.mine), shard, self.mine, self.near, partner(self.chip, to), self.core)
            self.to_twin(shard)

    def cross(self):
        for flip in (0, 4, 8, 12):
            for via, to, cut, sem in ((1, 2, 0, self.near), (2, 1, 1, self.far)):
                shard = partner(self.chip, flip ^ via)
                self.wait(shard, self.mine, self.near)
                self.push(self.held(shard, self.cuts[cut]), shard, self.cuts[cut], sem, partner(self.chip, to), self.core)
                self.to_twin(shard)

    def last(self):
        for flip in (0, 4, 8, 12):
            shard = partner(self.chip, flip ^ 3)
            self.wait(shard, self.cuts[0], self.near)
            self.wait(shard, self.cuts[1], self.far)
            self.to_twin(shard)

    def finish(self):
        pltpu.make_async_copy(self.own, self.whole.at[self.chip], self.local).wait()
        theirs = self.whole.at[pl.ds(0, CHIPS - 1), pl.ds((1 - self.core) * self.half, self.half), :]
        pltpu.make_async_copy(theirs, theirs, self.twin).wait()

    def drain(self):
        for copy in self.sent:
            copy.wait_send()


def gather_kernel(*refs):
    owns, wholes = refs[:3], refs[3:6]
    send, near, far, twin, local = refs[6:]
    chip, core = place()
    meet(chip, core)
    gs = [Gather(owns[g], wholes[g], send.at[g], near.at[g], far.at[g], twin.at[g], local.at[g], chip, core) for g in range(3)]
    gs[0].start()
    gs[0].spread()
    gs[1].start()
    gs[0].cross()
    gs[2].start()
    gs[0].last()
    gs[1].spread()
    gs[2].spread()
    gs[1].cross()
    gs[2].cross()
    gs[1].last()
    gs[2].last()
    for g in gs:
        g.finish()
    for g in gs:
        g.drain()


def gather_all(owns, cid):
    sds = jax.ShapeDtypeStruct
    dma = pltpu.SemaphoreType.DMA
    vm = pl.BlockSpec(memory_space=pltpu.VMEM)
    return pl.pallas_call(
        gather_kernel,
        name="gather_weights",
        out_shape=[sds((CHIPS,) + o.shape, o.dtype) for o in owns],
        in_specs=[vm] * 3, out_specs=[vm] * 3,
        scratch_shapes=[dma((3,)), dma((3, CHIPS)), dma((3, CHIPS)), dma((3,)), dma((3,))],
        compiler_params=pltpu.CompilerParams(collective_id=cid, has_side_effects=True, vmem_limit_bytes=40 << 20),
    )(*owns)


class Scatter:
    def __init__(self, grad, got0, part, got1, col, got2, out, twin_out, send, recv, chip, core):
        self.grad, self.got0, self.part, self.got1, self.col, self.got2 = grad, got0, part, got1, col, got2
        self.out, self.twin_out, self.send, self.recv, self.chip, self.core = out, twin_out, send, recv, chip, core
        self.half = grad.shape[2] // 2
        self.z, self.yx = chip // 4, lax.rem(chip, 4)

    def copy0(self):
        return remote(self.grad.at[:, :, pl.ds((1 - self.core) * self.half, self.half), :], self.got0, self.send.at[0], self.recv.at[0],
                      self.chip, 1 - self.core)

    def start0(self):
        self.copy0().start()

    def add0(self):
        self.copy0().wait()

        def one(i, _):
            z, yx = i // 4, lax.rem(i, 4)
            mine = self.grad[z, yx, pl.ds(pl.multiple_of(self.core * self.half, self.half), self.half), :].astype(F32)
            self.part[z, yx] = (mine + self.got0[z, yx].astype(F32)).astype(BF16)
            return 0

        lax.fori_loop(0, CHIPS, one, 0)

    def copy1(self, flip):
        to = partner(self.chip, flip)
        return remote(self.part.at[:, lax.rem(to, 4)], self.got1.at[flip - 1], self.send.at[flip], self.recv.at[flip], to, self.core)

    def start1(self):
        for flip in (3, 1, 2):
            self.copy1(flip).start()

    def add1(self):
        for flip in (1, 2, 3):
            self.copy1(flip).wait()

        def one(z, _):
            total = self.part[z, self.yx].astype(F32)
            for k in range(3):
                total = total + self.got1[k, z].astype(F32)
            self.col[z] = total.astype(BF16)
            return 0

        lax.fori_loop(0, 4, one, 0)

    def copy2(self, flip):
        to = partner(self.chip, 4 * flip)
        return remote(self.col.at[to // 4], self.got2.at[flip - 1], self.send.at[3 + flip], self.recv.at[3 + flip], to, self.core)

    def start2(self):
        for flip in (1, 2, 3):
            self.copy2(flip).start()

    def copy3(self):
        place = (pl.ds(pl.multiple_of(self.core * self.half, self.half), self.half), slice(None))
        return remote(self.out.at[place[0], place[1]], self.twin_out.at[place[0], place[1]], self.send.at[7], self.recv.at[7], self.chip, 1 - self.core)

    def add2(self):
        for flip in (1, 2, 3):
            self.copy2(flip).wait()
        total = self.col[self.z].astype(F32)
        for k in range(3):
            total = total + self.got2[k].astype(F32)
        self.out[pl.ds(pl.multiple_of(self.core * self.half, self.half), self.half), :] = total
        self.copy3().start()

    def finish(self):
        self.copy3().wait_send()
        ref = self.out.at[pl.ds((1 - self.core) * self.half, self.half), :]
        pltpu.make_async_copy(ref, ref, self.recv.at[7]).wait()


def scatter_scratch(shapes):
    out = []
    for rows, cols in shapes:
        half = rows // 2
        out += [pltpu.VMEM((4, 4, half, cols), BF16), pltpu.VMEM((4, 4, half, cols), BF16), pltpu.VMEM((3, 4, half, cols), BF16),
                pltpu.VMEM((4, half, cols), BF16), pltpu.VMEM((3, half, cols), BF16), pltpu.VMEM((rows, cols), F32)]
    return out


def scatter_kernel(*refs):
    n = 3
    grads, outs = refs[:n], refs[n:2 * n]
    bufs = refs[2 * n:2 * n + 6 * n]
    send, recv = refs[2 * n + 6 * n:]
    chip, core = place()
    meet(chip, core)
    ss = []
    for g in range(n):
        got0, part, got1, col, got2, final = bufs[6 * g:6 * g + 6]
        ss.append(Scatter(grads[g], got0, part, got1, col, got2, final, final, send.at[g], recv.at[g], chip, core))
    for s in ss:
        s.start0()
    for s in ss:
        s.add0()
        s.start1()
    for s in ss:
        s.add1()
        s.start2()
    for s in ss:
        s.add2()
    for g, s in enumerate(ss):
        s.finish()
        outs[g][...] = s.out[...]


def scatter_all(grads, cid):
    sds = jax.ShapeDtypeStruct
    dma = pltpu.SemaphoreType.DMA
    vm = pl.BlockSpec(memory_space=pltpu.VMEM)
    shapes = [g.shape[2:] for g in grads]
    return pl.pallas_call(
        scatter_kernel,
        name="scatter_grads",
        out_shape=[sds(s, F32) for s in shapes],
        in_specs=[vm] * 3, out_specs=[vm] * 3,
        scratch_shapes=scatter_scratch(shapes) + [dma((3, 8)), dma((3, 8))],
        compiler_params=pltpu.CompilerParams(collective_id=cid, has_side_effects=True, vmem_limit_bytes=60 << 20),
    )(*grads)


def moments_of(grad, first, second):
    new_first = beta_first * first + (1.0 - beta_first) * grad
    new_second = beta_second * second + (1.0 - beta_second) * grad * grad
    direction = new_first / (1.0 - beta_first**STEP) / (jnp.sqrt(new_second / (1.0 - beta_second**STEP)) + adam_eps)
    return new_first, new_second, direction


def parts_of(r1, r2, r3, widths):
    qkv, out, up = widths
    return r1[:, 0:qkv], r2[:, 0:out], r2[:, out:out + up], r3


def reduce_kernel(*refs):
    n = 3
    grads, masters, firsts, seconds = refs[:n], refs[n:n + 4], refs[n + 4:n + 8], refs[n + 8:n + 12]
    outs, norms_ref = refs[n + 12:2 * n + 12], refs[2 * n + 12]
    bufs = refs[2 * n + 13:2 * n + 13 + 5 * n]
    squares, send, recv, send_sq, recv_sq = refs[2 * n + 13 + 5 * n:]
    chip, core = place()
    meet(chip, core)
    ss = []
    for g in range(n):
        got0, part, got1, col, got2 = bufs[5 * g:5 * g + 5]
        ss.append(Scatter(grads[g], got0, part, got1, col, got2, outs[g], outs[g], send.at[g], recv.at[g], chip, core))
    for s in ss:
        s.start0()
    for s in ss:
        s.add0()
        s.start1()
    for s in ss:
        s.add1()
        s.start2()
    for s in ss:
        s.add2()
    for s in ss:
        s.finish()
    widths = [masters[i].shape[1] for i in range(3)]
    grads_of = (
        outs[0].at[:, 0:widths[0]], outs[1].at[:, 0:widths[1]], outs[1].at[:, widths[1]:widths[1] + widths[2]], outs[2])

    def lanes_of(v):
        total = None
        for j in range(v.shape[1] // LANES):
            piece = v[:, j * LANES:(j + 1) * LANES]
            total = piece if total is None else total + piece
        return jnp.sum(total, axis=0, keepdims=True)

    for i in range(4):
        _, _, direction = moments_of(grads_of[i][...], firsts[i][...], seconds[i][...])
        master = masters[i][...]
        update = direction + weight_decay * master
        squares[0, i:i + 1, :] = lanes_of(master * master)
        squares[0, 4 + i:5 + i, :] = lanes_of(update * update)
    copies = []
    for flip in range(1, CHIPS):
        copy = remote(squares.at[0], squares.at[flip], send_sq.at[flip], recv_sq.at[flip], partner(chip, flip), core)
        copy.start()
        copies.append(copy)
    for copy in copies:
        copy.wait()
    total = squares[0]
    for flip in range(1, CHIPS):
        total = total + squares[flip]
    norms_ref[...] = jnp.broadcast_to(jnp.sqrt(jnp.sum(total, axis=1, keepdims=True)), (8, LANES))


def reduce_all(grads, masters, firsts, seconds, cid):
    sds = jax.ShapeDtypeStruct
    dma = pltpu.SemaphoreType.DMA
    vm = pl.BlockSpec(memory_space=pltpu.VMEM)
    shapes = [g.shape[2:] for g in grads]
    scratch = []
    for rows, cols in shapes:
        half = rows // 2
        scratch += [pltpu.VMEM((4, 4, half, cols), BF16), pltpu.VMEM((4, 4, half, cols), BF16), pltpu.VMEM((3, 4, half, cols), BF16),
                    pltpu.VMEM((4, half, cols), BF16), pltpu.VMEM((3, half, cols), BF16)]
    return pl.pallas_call(
        reduce_kernel,
        name="scatter_grads",
        out_shape=[sds(s, F32) for s in shapes] + [sds((8, LANES), F32)],
        in_specs=[vm] * 15, out_specs=[vm] * 4,
        scratch_shapes=scratch + [pltpu.VMEM((CHIPS, 8, LANES), F32), dma((3, 8)), dma((3, 8)), dma((CHIPS,)), dma((CHIPS,))],
        compiler_params=pltpu.CompilerParams(collective_id=cid, has_side_effects=True, vmem_limit_bytes=60 << 20),
    )(*grads, *masters, *firsts, *seconds)


def update_kernel(r1, r2, r3, norms_ref, *refs):
    masters, firsts, seconds = refs[0:4], refs[4:8], refs[8:12]
    new_m, new_f, new_s, copies, norm_out = refs[12:16], refs[16:20], refs[20:24], refs[24:28], refs[28]
    widths = [masters[i].shape[1] for i in range(3)]
    grads = (r1.at[:, 0:widths[0]], r2.at[:, 0:widths[1]], r2.at[:, widths[1]:widths[1] + widths[2]], r3)
    row = lax.broadcasted_iota(jnp.int32, (3, 4), 0)
    col = lax.broadcasted_iota(jnp.int32, (3, 4), 1)
    table = jnp.zeros((3, 4), F32)
    for i in range(4):
        weight_norm, update_norm = norms_ref[i:i + 1, 0:1], norms_ref[4 + i:5 + i, 0:1]
        trust = weight_norm / update_norm
        first, second, direction = moments_of(grads[i][...], firsts[i][...], seconds[i][...])
        master = masters[i][...]
        new = master - matrix_rate * trust * (direction + weight_decay * master)
        new_m[i][...] = new
        copies[i][...] = new.astype(BF16)
        new_f[i][...] = first
        new_s[i][...] = second
        for r, value in enumerate((weight_norm, update_norm, trust)):
            table = jnp.where((row == r) & (col == i), value, table)
    norm_out[...] = table


def update_all(reduced, norms, masters, firsts, seconds):
    sds = jax.ShapeDtypeStruct
    vm = pl.BlockSpec(memory_space=pltpu.VMEM)
    full = [sds(m.shape, F32) for m in masters]
    return pl.pallas_call(
        update_kernel,
        name="update",
        out_shape=full * 3 + [sds(m.shape, BF16) for m in masters] + [sds((3, 4), F32)],
        in_specs=[vm] * 16, out_specs=[vm] * 17,
        compiler_params=pltpu.CompilerParams(vmem_limit_bytes=40 << 20),
    )(*reduced, norms, *masters, *firsts, *seconds)


def shards(block_in, offsets, cotangent, w_qkv, w_out, w_up, w_down, vectors, *moments):
    masters = (w_qkv, w_out, w_up, w_down, vectors)
    firsts, seconds = moments[:5], moments[5:]
    micro, local_rows, length, width = block_in.shape
    rows = micro * local_rows
    chips = lax.axis_size("fsdp")
    near = chips == CHIPS and lax.axis_size("dp") == 2
    columns = vectors.shape[0] * chips // width
    table = jnp.pad(vectors.reshape(-1, columns).astype(BF16), ((0, 0), (0, LANES - columns)))
    own1 = jnp.concatenate([w_qkv.astype(BF16), table], axis=1)
    own2 = jnp.concatenate([w_out.astype(BF16), w_up.astype(BF16)], axis=1)
    own3 = w_down.astype(BF16)
    if near:
        wholes = [w.reshape(-1, w.shape[2]) for w in gather_all((own1, own2, own3), 0)]
    else:
        wholes = [lax.all_gather(o, "fsdp", axis=0, tiled=True) for o in (own1, own2, own3)]
    w1, w2, w3 = wholes
    x = block_in.reshape(rows, length, width)
    cot = cotangent.reshape(rows, length, width)
    off = offsets.reshape(-1)
    y, qkv, bctx, bmid, g2, g3, sums_a = phase_a(off, x, cot, w1, w2, w3)
    xgrad, g1 = phase_b(off, x, qkv, bctx, bmid, w1, sums_a)
    if near:
        *reduced, norms = reduce_all([g.reshape(4, 4, -1, g.shape[1]) for g in (g1, g2, g3)], masters[:4], firsts[:4], seconds[:4], 1)
    else:
        reduced = [lax.psum(lax.psum_scatter(g.astype(F32), "fsdp", scatter_dimension=0, tiled=True), "dp") for g in (g1, g2, g3)]
        grads = parts_of(*reduced, [m.shape[1] for m in masters[:3]])
        updates = [moments_of(g, m, s)[2] + weight_decay * w for g, m, s, w in zip(grads, firsts, seconds, masters)]
        squares = jnp.stack([jnp.sum(w * w) for w in masters[:4]] + [jnp.sum(u * u) for u in updates])
        norms = jnp.broadcast_to(jnp.sqrt(lax.psum(squares, "fsdp"))[:, None], (8, LANES))
    *news, matrix_norms = update_all(reduced, norms, masters[:4], firsts[:4], seconds[:4])
    vec_first, vec_second, vec_direction = moments_of(reduced[0][:, 3 * width:3 * width + columns].reshape(-1), firsts[4], seconds[4])
    vec_new = vectors - vector_rate * vec_direction
    return (y.reshape(block_in.shape), xgrad.reshape(block_in.shape), *news[0:4], vec_new, *news[4:8], vec_first,
            *news[8:12], vec_second, *news[12:16], vec_new.astype(BF16), matrix_norms)


def solution(mesh):
    batch, matrix, vector = P(None, ("fsdp", "dp"), None, None), P("fsdp", None), P("fsdp")
    params = (matrix,) * 4 + (vector,)
    in_specs = (batch, P(None, ("fsdp", "dp"), None), batch) + params * 3
    out_specs = (batch, batch) + params * 4 + (P(),)
    return jax.shard_map(shards, mesh=mesh, in_specs=in_specs, out_specs=out_specs, check_vma=False)
```

```python
import jax
import jax.numpy as jnp
from jax import lax
from jax.experimental import pallas as pl
from jax.experimental.pallas import tpu as pltpu
from jax.sharding import PartitionSpec as P

HEAD_DIM = 64
STEP = 5
EPS = 1e-05
beta_first = 0.5
beta_second = 0.5
adam_eps = 1e-06
weight_decay = 0.01
matrix_rate = 1.0
vector_rate = 0.1
CHIPS = 16
GROUP = 2
LANES = 128
NEG = -1e30
C0 = 0.7978845608028654
C1 = 0.044715
F32 = jnp.float32
BF16 = jnp.bfloat16
MESH = pl.DeviceIdType.MESH
DMA = pltpu.SemaphoreType.DMA


def nn(a, b):
    return lax.dot_general(a, b, (((1,), (0,)), ((), ())), preferred_element_type=F32)


def nt(a, b):
    return lax.dot_general(a, b, (((1,), (1,)), ((), ())), preferred_element_type=F32)


def tn(a, b):
    return lax.dot_general(a, b, (((0,), (0,)), ((), ())), preferred_element_type=F32)


def xhat_of(v):
    center = v - jnp.mean(v, axis=-1, keepdims=True)
    spread = jnp.mean(center * center, axis=-1, keepdims=True)
    inv = lax.rsqrt(spread + EPS)
    return center * inv, inv


def norm_back(e, xhat, inv):
    return (e - jnp.mean(e, axis=-1, keepdims=True) - xhat * jnp.mean(e * xhat, axis=-1, keepdims=True)) * inv


def crop_of(first, second, shape, axis):
    t = lax.broadcasted_iota(jnp.int32, shape, axis)
    return (t >= first).astype(jnp.int32) + (t >= second).astype(jnp.int32)


def col_sum(v):
    return jnp.sum(v, axis=0, keepdims=True)


def partner(chip, flip):
    out = chip
    for bit in (1, 2, 4, 8):
        if flip & bit:
            out = out + bit - 2 * bit * lax.rem(chip // bit, 2)
    return out


def meet(chip, core, flips):
    barrier = pltpu.get_barrier_semaphore()
    for flip in flips:
        pl.semaphore_signal(barrier, inc=1, device_id=(partner(chip, flip), core), device_id_type=MESH)
    pl.semaphore_signal(barrier, inc=1, device_id=(chip, 1 - core), device_id_type=MESH)
    pl.semaphore_wait(barrier, len(flips) + 1)


def remote(src, dst, send_sem, recv_sem, chip, core):
    return pltpu.make_async_remote_copy(src_ref=src, dst_ref=dst, send_sem=send_sem, recv_sem=recv_sem,
                                        device_id=(chip, core), device_id_type=MESH)


def wait_bytes(ref, sem):
    pltpu.make_async_copy(ref, ref, sem).wait()


class Gather:
    def __init__(self, own, whole, sems, chip, core):
        self.own, self.whole, self.chip, self.core = own, whole, chip, core
        self.send, self.near, self.far, self.twin, self.local = sems
        rows, cols = own.shape
        self.half = rows // 2
        start = pl.multiple_of(core * self.half, self.half)
        self.mine = (pl.ds(start, self.half), slice(None))
        if self.half >= 32:
            q = self.half // 2
            self.cuts = [(pl.ds(start + i * q, q), slice(None)) for i in range(2)]
        else:
            q = cols // 256 * 128
            self.cuts = [(pl.ds(start, self.half), pl.ds(0, q)), (pl.ds(start, self.half), pl.ds(q, cols - q))]

    def held(self, shard, cut):
        return self.whole.at[shard, cut[0], cut[1]]

    def push(self, src, shard, cut, sem, to):
        remote(src, self.held(shard, cut), self.send, sem.at[shard], partner(self.chip, to), self.core).start()

    def wait(self, shard, cut, sem):
        wait_bytes(self.held(shard, cut), sem.at[shard])

    def start(self):
        pltpu.make_async_copy(self.own, self.whole.at[self.chip], self.local).start()
        for flip in (1, 2, 4, 8, 12):
            self.push(self.own.at[self.mine[0], self.mine[1]], self.chip, self.mine, self.near, flip)

    def to_twin(self, shard):
        ref = self.held(shard, self.mine)
        remote(ref, ref, self.send, self.twin, self.chip, 1 - self.core).start()

    def spread(self):
        for flip in (4, 8, 12):
            shard = partner(self.chip, flip)
            self.wait(shard, self.mine, self.near)
            for to in (1, 2):
                self.push(self.held(shard, self.mine), shard, self.mine, self.near, to)
            self.to_twin(shard)

    def cross(self):
        for flip in (0, 4, 8, 12):
            for via, to, cut, sem in ((1, 2, 0, self.near), (2, 1, 1, self.far)):
                shard = partner(self.chip, flip ^ via)
                self.wait(shard, self.mine, self.near)
                self.push(self.held(shard, self.cuts[cut]), shard, self.cuts[cut], sem, to)
                self.to_twin(shard)

    def last(self):
        for flip in (0, 4, 8, 12):
            shard = partner(self.chip, flip ^ 3)
            self.wait(shard, self.cuts[0], self.near)
            self.wait(shard, self.cuts[1], self.far)
            self.to_twin(shard)

    def finish(self):
        pltpu.make_async_copy(self.own, self.whole.at[self.chip], self.local).wait()
        wait_bytes(self.whole.at[pl.ds(0, CHIPS - 1), pl.ds(0, self.half), :], self.twin)

    def drain(self):
        for _ in range(2):
            wait_bytes(self.whole.at[pl.ds(0, CHIPS - 1), pl.ds(0, self.half), :], self.send)


class Scatter:
    def __init__(self, grad, bufs, out, send, recv, chip, core):
        self.grad, self.out, self.send, self.recv, self.chip, self.core = grad, out, send, recv, chip, core
        self.got0, self.part, self.got1, self.col, self.got2 = bufs
        self.half = grad.shape[2] // 2
        self.start_mine = pl.multiple_of(core * self.half, self.half)
        self.z, self.yx = chip // 4, lax.rem(chip, 4)

    def copy0(self):
        theirs = pl.ds(pl.multiple_of((1 - self.core) * self.half, self.half), self.half)
        return remote(self.grad.at[:, :, theirs, :], self.got0, self.send.at[0], self.recv.at[0], self.chip, 1 - self.core)

    def start0(self):
        self.copy0().start()

    def add0(self):
        self.copy0().wait()

        def one(i, _):
            z, yx = i // 4, lax.rem(i, 4)
            mine = self.grad[z, yx, pl.ds(self.start_mine, self.half), :].astype(F32)
            self.part[z, yx] = (mine + self.got0[z, yx].astype(F32)).astype(BF16)
            return 0

        lax.fori_loop(0, CHIPS, one, 0)

    def copy1(self, flip):
        to = partner(self.chip, flip)
        return remote(self.part.at[:, lax.rem(to, 4)], self.got1.at[flip - 1], self.send.at[flip], self.recv.at[flip], to, self.core)

    def start1(self):
        for flip in (3, 1, 2):
            self.copy1(flip).start()

    def add1(self):
        for flip in (1, 2, 3):
            self.copy1(flip).wait()

        def one(z, _):
            total = self.part[z, self.yx].astype(F32)
            for k in range(3):
                total = total + self.got1[k, z].astype(F32)
            self.col[z] = total.astype(BF16)
            return 0

        lax.fori_loop(0, 4, one, 0)

    def copy2(self, flip):
        to = partner(self.chip, 4 * flip)
        return remote(self.col.at[to // 4], self.got2.at[flip - 1], self.send.at[3 + flip], self.recv.at[3 + flip], to, self.core)

    def start2(self):
        for flip in (1, 2, 3):
            self.copy2(flip).start()

    def copy3(self):
        ref = self.out.at[pl.ds(self.start_mine, self.half), :]
        return remote(ref, ref, self.send.at[7], self.recv.at[7], self.chip, 1 - self.core)

    def add2(self):
        for flip in (1, 2, 3):
            self.copy2(flip).wait()
        total = self.col[self.z].astype(F32)
        for k in range(3):
            total = total + self.got2[k].astype(F32)
        self.out[pl.ds(self.start_mine, self.half), :] = total
        self.copy3().start()

    def finish(self):
        self.copy3().wait()


def scatter_bufs(rows, cols):
    half = rows // 2
    return [pltpu.VMEM((4, 4, half, cols), BF16), pltpu.VMEM((4, 4, half, cols), BF16), pltpu.VMEM((3, 4, half, cols), BF16),
            pltpu.VMEM((4, half, cols), BF16), pltpu.VMEM((3, half, cols), BF16)]


ALL_FLIPS = tuple(range(1, CHIPS))
GATHER_FLIPS = (1, 2, 4, 8, 12)


def kernel_a(remote_on, off_ref, x_ref, cot_ref, *refs):
    if remote_on:
        masters, refs = refs[:5], refs[5:]
    else:
        w_in, refs = refs[:3], refs[3:]
    y_ref, qkv_ref, bctx_ref, bmid_ref, g2_out, g3_out, sums_ref = refs[:7]
    refs = refs[7:]
    if remote_on:
        w1_out, refs = refs[0], refs[1:]
    gup_ref, gdn_ref, gout_ref, ctx_ref, bias_ref, vec_ref = refs[:6]
    refs = refs[6:]
    step = pl.program_id(0)
    group, length, width = x_ref.shape
    pairs = pl.num_programs(0) // 2
    tokens = group * length
    hidden = gup_ref.shape[1]
    chunks = hidden // width
    if remote_on:
        wholes, owns, sems, out_sem = refs[0:3], refs[3:6], refs[6:11], refs[11]
        chip, core = lax.axis_index("fsdp"), lax.axis_index("dp")
        gathers = [Gather(owns[g], wholes[g], [s.at[g] for s in sems], chip, core) for g in range(3)]
        w1_ref, w2_ref, w3_ref = [w.reshape(w.shape[0] * w.shape[1], w.shape[2]) for w in wholes]
    else:
        w1_ref, w2_ref, w3_ref = w_in
    wout_ref, wup_ref = w2_ref.at[:, 0:width], w2_ref.at[:, width:width + hidden]

    @pl.when(step == 0)
    def _():
        if remote_on:
            meet(chip, core, GATHER_FLIPS)
            owns[0][:, 0:3 * width] = masters[0][...].astype(BF16)
            owns[0][:, 3 * width:] = masters[4][...].astype(BF16)
            gathers[0].start()
            owns[1][:, 0:width] = masters[1][...].astype(BF16)
            owns[1][:, width:] = masters[2][...].astype(BF16)
            owns[2][...] = masters[3][...].astype(BF16)
        gup_ref[...] = jnp.zeros_like(gup_ref)
        gdn_ref[...] = jnp.zeros_like(gdn_ref)
        gout_ref[...] = jnp.zeros_like(gout_ref)
        sums_ref[...] = jnp.zeros_like(sums_ref)
        if remote_on:
            gathers[0].spread()
            gathers[1].start()
            gathers[0].cross()
            gathers[2].start()
            gathers[0].last()
            gathers[0].finish()
        vec_ref[...] = w1_ref[:, 3 * width:].astype(F32).T

    events = {}
    if remote_on:
        events = {0: gathers[1].spread, 1: gathers[2].spread, 2: gathers[1].cross, 3: gathers[2].cross,
                  4: gathers[1].last, 5: gathers[2].last}

    @pl.when(step < pairs)
    def _():
        x = x_ref[...].reshape(tokens, width).astype(F32)
        xhat, _ = xhat_of(x)
        n1 = (xhat * vec_ref[0:1, :] + vec_ref[1:2, :]).astype(BF16)
        q = (nn(n1, w1_ref[:, 0:width]) + vec_ref[2:3, :]) * HEAD_DIM ** (-0.5)
        qkv_ref[:, :, 0:width] = q.astype(BF16).reshape(group, length, width)
        qkv_ref[:, :, width:2 * width] = nn(n1, w1_ref[:, width:2 * width]).astype(BF16).reshape(group, length, width)
        v = nn(n1, w1_ref[:, 2 * width:3 * width]) + vec_ref[3:4, :]
        qkv_ref[:, :, 2 * width:] = v.astype(BF16).reshape(group, length, width)
        low = lax.broadcasted_iota(jnp.int32, (1, LANES), 1) < HEAD_DIM
        for r in range(group):
            row = step * group + r
            crop_q = crop_of(off_ref[2 * row], off_ref[2 * row + 1], (length, 1), 0)
            crop_k = crop_of(off_ref[2 * row], off_ref[2 * row + 1], (1, length), 1)
            bias_ref[...] = jnp.where(crop_q == crop_k, 0.0, NEG)
            for pair in range(width // LANES):
                lanes = slice(pair * LANES, (pair + 1) * LANES)
                qp = qkv_ref[r, :, lanes]
                kp = qkv_ref[r, :, width + pair * LANES:width + (pair + 1) * LANES]
                vp = qkv_ref[r, :, 2 * width + pair * LANES:2 * width + (pair + 1) * LANES]
                total = None
                for half in range(2):
                    keep = low if half == 0 else jnp.logical_not(low)
                    s = nt(jnp.where(keep, qp, jnp.zeros_like(qp)), kp) + bias_ref[...]
                    e = jnp.exp(s - jnp.max(s, axis=-1, keepdims=True))
                    p = (e * (1.0 / jnp.sum(e, axis=-1, keepdims=True))).astype(BF16)
                    part = nn(p, jnp.where(keep, vp, jnp.zeros_like(vp)))
                    total = part if total is None else total + part
                ctx_ref[row, :, lanes] = total.astype(BF16)
            for point, event in events.items():
                if point % group == r:
                    pl.when(step == point // group)(event)

    @pl.when(step == pairs)
    def _():
        if remote_on:
            gathers[1].finish()
            gathers[2].finish()
            pltpu.make_async_copy(wholes[0], w1_out, out_sem).start()

    @pl.when(step >= pairs)
    def _():
        first_row = (step - pairs) * group
        ctx = ctx_ref[pl.ds(first_row, group)].reshape(tokens, width)
        middle = x_ref[...].reshape(tokens, width).astype(F32) + (nn(ctx, wout_ref[...]) + vec_ref[4:5, :])
        xhat2, inv2 = xhat_of(middle)
        n2 = (xhat2 * vec_ref[5:6, :] + vec_ref[6:7, :]).astype(BF16)
        cot = cot_ref[...].reshape(tokens, width)
        result = middle + vec_ref[7 + chunks:8 + chunks, :]
        back_n2 = jnp.zeros((tokens, width), F32)
        for u in range(chunks):
            cols = slice(u * width, (u + 1) * width)
            up = nn(n2, wup_ref[:, cols]) + vec_ref[7 + u:8 + u, :]
            square = up * up
            th = jnp.tanh(up * (C0 + (C0 * C1) * square))
            half_up = 0.5 * up
            active = (half_up + half_up * th).astype(BF16)
            slope = (0.5 + 0.5 * th) + half_up * (1.0 - th * th) * (C0 + (3.0 * C0 * C1) * square)
            back_up = nt(cot, w3_ref[cols, :]) * slope
            sums_ref[7 + u:8 + u, :] += col_sum(back_up)
            back_up = back_up.astype(BF16)
            result = result + nn(active, w3_ref[cols, :])
            back_n2 = back_n2 + nt(back_up, wup_ref[:, cols])
            gdn_ref[:, cols] += tn(cot, active)
            gup_ref[:, cols] += tn(n2, back_up)
        y_ref[...] = result.astype(BF16).reshape(group, length, width)
        cot32 = cot.astype(F32)
        sums_ref[7 + chunks:8 + chunks, :] += col_sum(cot32)
        sums_ref[5:6, :] += col_sum(back_n2 * xhat2)
        sums_ref[6:7, :] += col_sum(back_n2)
        back_middle = cot32 + norm_back(back_n2 * vec_ref[5:6, :], xhat2, inv2)
        bmid_ref[...] = back_middle.reshape(group, length, width)
        back_att = back_middle.astype(BF16)
        sums_ref[4:5, :] += col_sum(back_middle)
        gout_ref[...] += tn(ctx, back_att)
        bctx_ref[...] = nt(back_att, wout_ref[...]).astype(BF16).reshape(group, length, width)

    @pl.when(step == pl.num_programs(0) - 1)
    def _():
        g2_out[:, 0:width] = gout_ref[...].astype(BF16)
        g2_out[:, width:] = gup_ref[...].astype(BF16)
        for u in range(chunks):
            g3_out[u * width:(u + 1) * width, :] = gdn_ref[:, u * width:(u + 1) * width].T.astype(BF16)
        if remote_on:
            pltpu.make_async_copy(wholes[0], w1_out, out_sem).wait()
            for g in gathers:
                g.drain()


def whole(shape):
    return pl.BlockSpec(shape, lambda s, *_: (0,) * len(shape), pipeline_mode=pl.Buffered(1))


def phase_a(remote_on, off, x, cot, weights):
    rows, length, width = x.shape
    pairs = rows // GROUP
    if remote_on:
        sizes = [(weights[0].shape[0], 3 * width + LANES), (weights[1].shape[0], width + weights[2].shape[1]), weights[3].shape]
        w2_shape, w3_shape = (CHIPS * sizes[1][0], sizes[1][1]), (CHIPS * sizes[2][0], sizes[2][1])
    else:
        w2_shape, w3_shape = weights[1].shape, weights[2].shape
    hidden = w3_shape[0]
    blk = lambda w, index: pl.BlockSpec((GROUP, length, w), index)
    both = lambda s, *_: (lax.rem(s, pairs), 0, 0)
    early = lambda s, *_: (jnp.minimum(s, pairs - 1), 0, 0)
    late = lambda s, *_: (jnp.maximum(s - pairs, 0), 0, 0)
    sds = jax.ShapeDtypeStruct
    out_specs = [blk(width, late), blk(3 * width, early), blk(width, late), blk(width, late), whole(w2_shape), whole(w3_shape),
                 whole((LANES, width))]
    out_shape = [sds(x.shape, BF16), sds((rows, length, 3 * width), BF16), sds(x.shape, BF16), sds(x.shape, F32),
                 sds(w2_shape, BF16), sds(w3_shape, BF16), sds((LANES, width), F32)]
    scratch = [pltpu.VMEM((width, hidden), F32), pltpu.VMEM((width, hidden), F32), pltpu.VMEM((width, width), F32),
               pltpu.VMEM((rows, length, width), BF16), pltpu.VMEM((length, length), F32), pltpu.VMEM((LANES, width), F32)]
    params = dict(vmem_limit_bytes=62 << 20)
    if remote_on:
        out_specs.append(pl.BlockSpec(memory_space=pl.ANY))
        out_shape.append(sds((CHIPS,) + sizes[0], BF16))
        scratch += [pltpu.VMEM((CHIPS,) + s, BF16) for s in sizes] + [pltpu.VMEM(s, BF16) for s in sizes]
        scratch += [DMA((3,)), DMA((3, CHIPS)), DMA((3, CHIPS)), DMA((3,)), DMA((3,)), DMA]
        params.update(collective_id=0, has_side_effects=True)
    return pl.pallas_call(
        lambda *refs: kernel_a(remote_on, *refs),
        name="phase_a",
        grid_spec=pltpu.PrefetchScalarGridSpec(
            num_scalar_prefetch=1,
            grid=(2 * pairs,),
            in_specs=[blk(width, both), blk(width, late)] + [whole(w.shape) for w in weights],
            out_specs=out_specs,
            scratch_shapes=scratch,
        ),
        out_shape=out_shape,
        compiler_params=pltpu.CompilerParams(**params),
    )(off, x, cot, *weights)


def moments_of(grad, first, second):
    new_first = beta_first * first + (1.0 - beta_first) * grad
    new_second = beta_second * second + (1.0 - beta_second) * grad * grad
    direction = new_first / (1.0 - beta_first**STEP) / (jnp.sqrt(new_second / (1.0 - beta_second**STEP)) + adam_eps)
    return new_first, new_second, direction


def lanes_of(v):
    total = None
    for j in range(v.shape[1] // LANES):
        piece = v[:, j * LANES:(j + 1) * LANES]
        total = piece if total is None else total + piece
    return jnp.sum(total, axis=0, keepdims=True)


def kernel_b(remote_on, off_ref, x_ref, qkv_ref, bctx_ref, bmid_ref, w1_ref, sums_a_ref, *refs):
    if remote_on:
        g2_ref, g3_ref, masters, firsts, seconds = refs[0], refs[1], refs[2:6], refs[6:10], refs[10:14]
        xgrad_ref, r1_ref, r2_ref, r3_ref, rv_ref, norms_ref = refs[14:20]
        refs = refs[20:]
    else:
        xgrad_ref, g1_out, gv_out = refs[:3]
        refs = refs[3:]
    gqkv_ref, bqkv_ref, bias_ref, sums_ref, vec_ref = refs[:5]
    refs = refs[5:]
    step = pl.program_id(0)
    group, length, width = x_ref.shape
    pairs = pl.num_programs(0) // 2
    tokens = group * length
    if remote_on:
        bufs, finals, refs = refs[:15], refs[15:18], refs[18:]
        g1_ref, gv_ref, got_v, sum_v, twin_v, squares, send, recv, send_v, recv_v, send_q, recv_q = refs
        chip, core = lax.axis_index("fsdp"), lax.axis_index("dp")
        shape4 = lambda ref: ref.reshape(4, 4, ref.shape[0] // CHIPS, ref.shape[1])
        scatters = [Scatter(g, bufs[5 * i:5 * i + 5], finals[i], send.at[i], recv.at[i], chip, core)
                    for i, g in enumerate((g1_ref, shape4(g2_ref), shape4(g3_ref)))]
        first, early = scatters[0], scatters[1:]

    def start_early():
        for s in early:
            s.start0()

    def early_one():
        for s in early:
            s.add0()
            s.start1()

    def early_two():
        for s in early:
            s.add1()
            s.start2()

    def early_three():
        for s in early:
            s.add2()

    events = {0: early_one, 5: early_two} if remote_on else {}

    @pl.when(step == 0)
    def _():
        if remote_on:
            meet(chip, core, ALL_FLIPS)
            start_early()
        gqkv_ref[...] = jnp.zeros_like(gqkv_ref)
        sums_ref[...] = sums_a_ref[...]
        vec_ref[...] = w1_ref[:, 3 * width:].astype(F32).T

    @pl.when(step < pairs)
    def _():
        low = lax.broadcasted_iota(jnp.int32, (1, LANES), 1) < HEAD_DIM
        for r in range(group):
            row = step * group + r
            crop_k = crop_of(off_ref[2 * row], off_ref[2 * row + 1], (length, 1), 0)
            crop_q = crop_of(off_ref[2 * row], off_ref[2 * row + 1], (1, length), 1)
            bias_ref[...] = jnp.where(crop_q == crop_k, 0.0, NEG)
            for pair in range(width // LANES):
                lanes = slice(pair * LANES, (pair + 1) * LANES)
                klanes = slice(width + pair * LANES, width + (pair + 1) * LANES)
                vlanes = slice(2 * width + pair * LANES, 2 * width + (pair + 1) * LANES)
                qp = qkv_ref[r, :, lanes]
                kp = qkv_ref[r, :, klanes]
                vp = qkv_ref[r, :, vlanes]
                op = bctx_ref[r, :, lanes]
                dq = dk = dv = None
                for half in range(2):
                    keep = low if half == 0 else jnp.logical_not(low)
                    zero = jnp.zeros_like(qp)
                    qh = jnp.where(keep, qp, zero)
                    oh = jnp.where(keep, op, zero)
                    s = nt(kp, qh) + bias_ref[...]
                    e = jnp.exp(s - jnp.max(s, axis=0, keepdims=True))
                    p = e * (1.0 / jnp.sum(e, axis=0, keepdims=True))
                    dp = nt(vp, oh)
                    ds = (p * (dp - jnp.sum(p * dp, axis=0, keepdims=True))).astype(BF16)
                    dv_h = nn(p.astype(BF16), oh)
                    dk_h = nn(ds, qh)
                    dq_h = tn(ds, jnp.where(keep, kp, zero))
                    dq = dq_h if dq is None else dq + dq_h
                    dk = dk_h if dk is None else dk + dk_h
                    dv = dv_h if dv is None else dv + dv_h
                bqkv_ref[row, :, lanes] = (dq * HEAD_DIM ** (-0.5)).astype(BF16)
                bqkv_ref[row, :, klanes] = dk.astype(BF16)
                bqkv_ref[row, :, vlanes] = dv.astype(BF16)
            for point, event in events.items():
                if point % group == r:
                    pl.when(step == point // group)(event)
        x = x_ref[...].reshape(tokens, width).astype(F32)
        xhat, _ = xhat_of(x)
        n1 = (xhat * vec_ref[0:1, :] + vec_ref[1:2, :]).astype(BF16)
        back = bqkv_ref[pl.ds(step * group, group)].reshape(tokens, 3 * width)
        sums_ref[2:3, :] += col_sum(back[:, :width].astype(F32))
        sums_ref[3:4, :] += col_sum(back[:, 2 * width:].astype(F32))
        for part in range(3):
            cols = slice(part * width, (part + 1) * width)
            gqkv_ref[:, cols] += tn(n1, back[:, cols])

    @pl.when(step == pairs)
    def _():
        if remote_on:
            g1_ref[...] = gqkv_ref[...].astype(BF16).reshape(g1_ref.shape)
            first.start0()
            early_three()
        else:
            g1_out[...] = gqkv_ref[...].astype(BF16)

    @pl.when(step >= pairs)
    def _():
        x = x_ref[...].reshape(tokens, width).astype(F32)
        xhat, inv = xhat_of(x)
        back = bqkv_ref[pl.ds((step - pairs) * group, group)].reshape(tokens, 3 * width)
        back_n1 = nt(back, w1_ref[:, 0:3 * width])
        sums_ref[0:1, :] += col_sum(back_n1 * xhat)
        sums_ref[1:2, :] += col_sum(back_n1)
        grad = bmid_ref[...].reshape(tokens, width) + norm_back(back_n1 * vec_ref[0:1, :], xhat, inv)
        xgrad_ref[...] = grad.reshape(group, length, width)

    @pl.when(step == pairs)
    def _():
        if remote_on:
            first.add0()
            first.start1()

    @pl.when(step == pl.num_programs(0) - 1)
    def _():
        if not remote_on:
            gv_out[...] = sums_ref[...].T.astype(BF16)
            return
        gv_ref[...] = sums_ref[...].T.astype(BF16).reshape(gv_ref.shape)
        vec_copies = []
        for flip in ALL_FLIPS:
            to = partner(chip, flip)
            vec_copies.append(remote(gv_ref.at[to], got_v.at[flip - 1], send_v.at[flip], recv_v.at[flip], to, core))
            vec_copies[-1].start()
        first.add1()
        first.start2()
        for copy in vec_copies:
            copy.wait()
        total = gv_ref[chip].astype(F32)
        for flip in ALL_FLIPS:
            total = total + got_v[flip - 1].astype(F32)
        sum_v[...] = total
        twin = remote(sum_v, twin_v, send_v.at[0], recv_v.at[0], chip, 1 - core)
        twin.start()
        for s in early:
            s.finish()
        first.add2()
        twin.wait()
        rv_ref[...] = sum_v[...] + twin_v[...]
        first.finish()
        wide = masters[2].shape[1]
        for final, out in zip(finals, (r1_ref, r2_ref, r3_ref)):
            out[...] = final[...]
        grads = (finals[0], finals[1].at[:, 0:width], finals[1].at[:, width:width + wide], finals[2])
        for i in range(4):
            _, _, direction = moments_of(grads[i][...], firsts[i][...], seconds[i][...])
            master = masters[i][...]
            update = direction + weight_decay * master
            squares[0, i:i + 1, :] = lanes_of(master * master)
            squares[0, 4 + i:5 + i, :] = lanes_of(update * update)
        copies = []
        for flip in ALL_FLIPS:
            copies.append(remote(squares.at[0], squares.at[flip], send_q.at[flip], recv_q.at[flip], partner(chip, flip), core))
            copies[-1].start()
        for copy in copies:
            copy.wait()
        total = squares[0]
        for flip in ALL_FLIPS:
            total = total + squares[flip]
        norms_ref[...] = jnp.broadcast_to(jnp.sqrt(jnp.sum(total, axis=1, keepdims=True)), (8, LANES))


def phase_b(remote_on, off, x, qkv, bctx, bmid, w1, sums_a, grads=(), masters=(), firsts=(), seconds=()):
    rows, length, width = x.shape
    pairs = rows // GROUP
    blk = lambda w, index: pl.BlockSpec((GROUP, length, w), index)
    both = lambda s, *_: (lax.rem(s, pairs), 0, 0)
    early = lambda s, *_: (jnp.minimum(s, pairs - 1), 0, 0)
    late = lambda s, *_: (jnp.maximum(s - pairs, 0), 0, 0)
    sds = jax.ShapeDtypeStruct
    extra = (*grads, *masters, *firsts, *seconds)
    scratch = [pltpu.VMEM((width, 3 * width), F32), pltpu.VMEM((rows, length, 3 * width), BF16), pltpu.VMEM((length, length), F32),
               pltpu.VMEM((LANES, width), F32), pltpu.VMEM((LANES, width), F32)]
    params = dict(vmem_limit_bytes=62 << 20)
    if remote_on:
        sizes = [(width // CHIPS, 3 * width)] + [(g.shape[0] // CHIPS, g.shape[1]) for g in grads]
        small = (width // CHIPS, LANES)
        outs = [sds(s, F32) for s in sizes] + [sds(small, F32), sds((8, LANES), F32)]
        for s in sizes:
            scratch += scatter_bufs(*s)
        scratch += [pltpu.VMEM(s, F32) for s in sizes]
        scratch += [pltpu.VMEM((4, 4) + sizes[0], BF16), pltpu.VMEM((CHIPS,) + small, BF16), pltpu.VMEM((CHIPS - 1,) + small, BF16),
                    pltpu.VMEM(small, F32), pltpu.VMEM(small, F32), pltpu.VMEM((CHIPS, 8, LANES), F32),
                    DMA((3, 8)), DMA((3, 8)), DMA((CHIPS,)), DMA((CHIPS,)), DMA((CHIPS,)), DMA((CHIPS,))]
        params.update(collective_id=1, has_side_effects=True)
    else:
        outs = [sds((width, 3 * width), BF16), sds((width, LANES), BF16)]
    return pl.pallas_call(
        lambda *refs: kernel_b(remote_on, *refs),
        name="phase_b",
        grid_spec=pltpu.PrefetchScalarGridSpec(
            num_scalar_prefetch=1,
            grid=(2 * pairs,),
            in_specs=[blk(width, both), blk(3 * width, early), blk(width, early), blk(width, late), whole(w1.shape), whole(sums_a.shape)]
            + [whole(e.shape) for e in extra],
            out_specs=[blk(width, late)] + [whole(o.shape) for o in outs],
            scratch_shapes=scratch,
        ),
        out_shape=[sds(x.shape, F32)] + outs,
        compiler_params=pltpu.CompilerParams(**params),
    )(off, x, qkv, bctx, bmid, w1, sums_a, *extra)


def update_kernel(r1, r2, r3, norms_ref, *refs):
    masters, firsts, seconds = refs[0:4], refs[4:8], refs[8:12]
    new_m, new_f, new_s, copies, norm_out = refs[12:16], refs[16:20], refs[20:24], refs[24:28], refs[28]
    widths = [masters[i].shape[1] for i in range(3)]
    grads = (r1, r2.at[:, 0:widths[1]], r2.at[:, widths[1]:widths[1] + widths[2]], r3)
    row = lax.broadcasted_iota(jnp.int32, (3, 4), 0)
    col = lax.broadcasted_iota(jnp.int32, (3, 4), 1)
    table = jnp.zeros((3, 4), F32)
    for i in range(4):
        weight_norm, update_norm = norms_ref[i:i + 1, 0:1], norms_ref[4 + i:5 + i, 0:1]
        trust = weight_norm / update_norm
        first, second, direction = moments_of(grads[i][...], firsts[i][...], seconds[i][...])
        master = masters[i][...]
        new = master - matrix_rate * trust * (direction + weight_decay * master)
        new_m[i][...] = new
        copies[i][...] = new.astype(BF16)
        new_f[i][...] = first
        new_s[i][...] = second
        for r, value in enumerate((weight_norm, update_norm, trust)):
            table = jnp.where((row == r) & (col == i), value, table)
    norm_out[...] = table


def update_all(reduced, norms, masters, firsts, seconds):
    sds = jax.ShapeDtypeStruct
    vm = pl.BlockSpec(memory_space=pltpu.VMEM)
    full = [sds(m.shape, F32) for m in masters]
    return pl.pallas_call(
        update_kernel,
        name="update",
        out_shape=full * 3 + [sds(m.shape, BF16) for m in masters] + [sds((3, 4), F32)],
        in_specs=[vm] * 16, out_specs=[vm] * 17,
        compiler_params=pltpu.CompilerParams(vmem_limit_bytes=40 << 20),
    )(*reduced, norms, *masters, *firsts, *seconds)


def shards(block_in, offsets, cotangent, w_qkv, w_out, w_up, w_down, vectors, *moments):
    masters = (w_qkv, w_out, w_up, w_down)
    firsts, seconds = moments[:5], moments[5:]
    micro, local_rows, length, width = block_in.shape
    rows = micro * local_rows
    chips = lax.axis_size("fsdp")
    near = chips == CHIPS and lax.axis_size("dp") == 2
    columns = vectors.shape[0] * chips // width
    table = jnp.pad(vectors.reshape(-1, columns), ((0, 0), (0, LANES - columns)))
    x = block_in.reshape(rows, length, width)
    cot = cotangent.reshape(rows, length, width)
    off = offsets.reshape(-1)
    if near:
        y, qkv, bctx, bmid, g2, g3, sums_a, w1 = phase_a(True, off, x, cot, (*masters, table))
        w1 = w1.reshape(-1, w1.shape[2])
        xgrad, *reduced, norms = phase_b(True, off, x, qkv, bctx, bmid, w1, sums_a, (g2, g3), masters, firsts[:4], seconds[:4])
    else:
        owns = [jnp.concatenate([w_qkv, table], axis=1), jnp.concatenate([w_out, w_up], axis=1), w_down]
        wholes = [lax.all_gather(o.astype(BF16), "fsdp", axis=0, tiled=True) for o in owns]
        y, qkv, bctx, bmid, g2, g3, sums_a = phase_a(False, off, x, cot, wholes)
        xgrad, g1, gv = phase_b(False, off, x, qkv, bctx, bmid, wholes[0], sums_a)
        reduced = [lax.psum(lax.psum_scatter(g.astype(F32), "fsdp", scatter_dimension=0, tiled=True), "dp") for g in (g1, g2, g3, gv)]
        grads = (reduced[0], reduced[1][:, :width], reduced[1][:, width:], reduced[2])
        updates = [moments_of(g, m, s)[2] + weight_decay * w for g, m, s, w in zip(grads, firsts, seconds, masters)]
        squares = jnp.stack([jnp.sum(w * w) for w in masters] + [jnp.sum(u * u) for u in updates])
        norms = jnp.broadcast_to(jnp.sqrt(lax.psum(squares, "fsdp"))[:, None], (8, LANES))
    *news, matrix_norms = update_all(reduced[:3], norms, masters, firsts[:4], seconds[:4])
    vec_first, vec_second, vec_direction = moments_of(reduced[3][:, :columns].reshape(-1), firsts[4], seconds[4])
    vec_new = vectors - vector_rate * vec_direction
    return (y.reshape(block_in.shape), xgrad.reshape(block_in.shape), *news[0:4], vec_new, *news[4:8], vec_first,
            *news[8:12], vec_second, *news[12:16], vec_new.astype(BF16), matrix_norms)


def solution(mesh):
    batch, matrix, vector = P(None, ("fsdp", "dp"), None, None), P("fsdp", None), P("fsdp")
    params = (matrix,) * 4 + (vector,)
    in_specs = (batch, P(None, ("fsdp", "dp"), None), batch) + params * 3
    out_specs = (batch, batch) + params * 4 + (P(),)
    return jax.shard_map(shards, mesh=mesh, in_specs=in_specs, out_specs=out_specs, check_vma=False)
```

```python
import jax
import jax.numpy as jnp
from jax import lax
from jax.experimental import pallas as pl
from jax.experimental.pallas import tpu as pltpu
from jax.sharding import PartitionSpec as P

HEAD_DIM = 64
STEP = 5
EPS = 1e-05
beta_first = 0.5
beta_second = 0.5
adam_eps = 1e-06
weight_decay = 0.01
matrix_rate = 1.0
vector_rate = 0.1
CHIPS = 16
GROUP = 2
LANES = 128
HALVES = 2
SIDE = 256
FOUR = 4
PAD = 384
NEG = -1e30
C0 = 0.7978845608028654
C1 = 0.044715
F32 = jnp.float32
BF16 = jnp.bfloat16
MESH = pl.DeviceIdType.MESH
DMA = pltpu.SemaphoreType.DMA


def nn(a, b):
    return lax.dot_general(a, b, (((1,), (0,)), ((), ())), preferred_element_type=F32)


def nt(a, b):
    return lax.dot_general(a, b, (((1,), (1,)), ((), ())), preferred_element_type=F32)


def tn(a, b):
    return lax.dot_general(a, b, (((0,), (0,)), ((), ())), preferred_element_type=F32)


def xhat_of(v):
    center = v - jnp.mean(v, axis=-1, keepdims=True)
    spread = jnp.mean(center * center, axis=-1, keepdims=True)
    inv = lax.rsqrt(spread + EPS)
    return center * inv, inv


def norm_back(e, xhat, inv):
    return (e - jnp.mean(e, axis=-1, keepdims=True) - xhat * jnp.mean(e * xhat, axis=-1, keepdims=True)) * inv


def crop_of(first, second, shape, axis):
    t = lax.broadcasted_iota(jnp.int32, shape, axis)
    return (t >= first).astype(jnp.int32) + (t >= second).astype(jnp.int32)


def side_of(ref, half, lo, hi):
    v = ref[half, ..., lo:hi]
    return v.reshape(-1, hi - lo)


def stack_heads(ref, tiles, pitch):
    low = lax.broadcasted_iota(jnp.int32, (1, LANES), 1) < HEAD_DIM
    for head in range(FOUR):
        tile = tiles[head // 2]
        keep = low if head % 2 == 0 else jnp.logical_not(low)
        lanes = slice(head // 2 * LANES, head // 2 * LANES + LANES)
        ref[head * pitch:head * pitch + tile.shape[0], lanes] = jnp.where(keep, tile, jnp.zeros_like(tile))


def col_sum(v):
    return jnp.sum(v, axis=0, keepdims=True)


def partner(chip, flip):
    out = chip
    for bit in (1, 2, 4, 8):
        if flip & bit:
            out = out + bit - 2 * bit * lax.rem(chip // bit, 2)
    return out


def meet(chip, core, flips):
    barrier = pltpu.get_barrier_semaphore()
    for flip in flips:
        pl.semaphore_signal(barrier, inc=1, device_id=(partner(chip, flip), core), device_id_type=MESH)
    pl.semaphore_signal(barrier, inc=1, device_id=(chip, 1 - core), device_id_type=MESH)
    pl.semaphore_wait(barrier, len(flips) + 1)


def remote(src, dst, send_sem, recv_sem, chip, core):
    return pltpu.make_async_remote_copy(src_ref=src, dst_ref=dst, send_sem=send_sem, recv_sem=recv_sem,
                                        device_id=(chip, core), device_id_type=MESH)


def wait_bytes(ref, sem):
    pltpu.make_async_copy(ref, ref, sem).wait()


class Gather:
    def __init__(self, whole, cols, send, recv, chip, core, quick):
        self.whole, self.cols, self.chip, self.core, self.send, self.recv, self.quick = whole, cols, chip, core, send, recv, quick
        self.half = whole.shape[-2] // 2
        start = pl.multiple_of(core * self.half, self.half)
        self.rows, self.all = pl.ds(start, self.half), pl.ds(0, cols)
        self.mine = (self.rows, self.all)
        if self.half >= 32:
            q = self.half // 2
            self.cuts = [(pl.ds(start + i * q, q), self.all) for i in range(2)]
        else:
            q = cols // 256 * 128
            self.cuts = [(self.rows, pl.ds(0, q)), (self.rows, pl.ds(q, cols - q))]

    def column(self, flip, cut):
        return self.whole.at[:, lax.rem(partner(self.chip, flip), 4), cut[0], cut[1]]

    def shard(self, flip):
        at = partner(self.chip, flip)
        return self.whole.at[at // 4, lax.rem(at, 4), self.rows, self.all]

    def push(self, ref, sem, to):
        remote(ref, ref, self.send, self.recv.at[sem], partner(self.chip, to), self.core).start()

    def to_twin(self, flip):
        ref = self.column(flip, self.mine)
        remote(ref, ref, self.send, self.recv.at[8], self.chip, 1 - self.core).start()

    def start(self):
        own = self.shard(0)
        for flip in (4, 8, 12):
            self.push(own, flip // 4, flip)
        if self.quick:
            self.push(own, 4, 1)
            self.push(own, 5, 2)

    def spread(self):
        for flip in (4, 8, 12):
            ref = self.shard(flip)
            wait_bytes(ref, self.recv.at[flip // 4])
            if self.quick:
                self.push(ref, 4, 1)
                self.push(ref, 5, 2)
        ref = self.column(0, self.mine)
        if not self.quick:
            self.push(ref, 4, 1)
            self.push(ref, 5, 2)
        self.to_twin(0)

    def cross(self):
        for sem, via, to, cut in ((4, 1, 2, 0), (5, 2, 1, 1)):
            wait_bytes(self.column(via, self.mine), self.recv.at[sem])
            self.push(self.column(via, self.cuts[cut]), 6 + cut, to)
            self.to_twin(via)

    def last(self):
        for cut in range(2):
            wait_bytes(self.column(3, self.cuts[cut]), self.recv.at[6 + cut])
        self.to_twin(3)

    def finish(self):
        wait_bytes(self.whole.at[:, :, pl.ds(0, self.half), self.all], self.recv.at[8])

    def drain(self):
        rows = pl.ds(0, self.half)
        for zs, yxs in (((0, 4), (0, 4)), ((0, 3), (0, 4)), ((0, 1), (0, 3))):
            wait_bytes(self.whole.at[pl.ds(*zs), pl.ds(*yxs), rows, self.all], self.send)


class Scatter:
    def __init__(self, grad, bufs, out, send, recv, chip, core):
        self.grad, self.out, self.send, self.recv, self.chip, self.core = grad, out, send, recv, chip, core
        self.got0, self.part, self.got1, self.col, self.got2 = bufs
        self.half = grad.shape[2] // 2
        self.start_mine = pl.multiple_of(core * self.half, self.half)
        self.z, self.yx = chip // 4, lax.rem(chip, 4)

    def copy0(self):
        theirs = pl.ds(pl.multiple_of((1 - self.core) * self.half, self.half), self.half)
        return remote(self.grad.at[:, :, theirs, :], self.got0, self.send.at[0], self.recv.at[0], self.chip, 1 - self.core)

    def start0(self):
        self.copy0().start()

    def add0(self):
        self.copy0().wait()

        def one(i, _):
            z, yx = i // 4, lax.rem(i, 4)
            mine = self.grad[z, yx, pl.ds(self.start_mine, self.half), :].astype(F32)
            self.part[z, yx] = (mine + self.got0[z, yx].astype(F32)).astype(BF16)
            return 0

        lax.fori_loop(0, CHIPS, one, 0)

    def copy1(self, flip):
        to = partner(self.chip, flip)
        return remote(self.part.at[:, lax.rem(to, 4)], self.got1.at[flip - 1], self.send.at[flip], self.recv.at[flip], to, self.core)

    def start1(self):
        for flip in (3, 1, 2):
            self.copy1(flip).start()

    def add1(self):
        for flip in (1, 2, 3):
            self.copy1(flip).wait()

        def one(z, _):
            total = self.part[z, self.yx].astype(F32)
            for k in range(3):
                total = total + self.got1[k, z].astype(F32)
            self.col[z] = total.astype(BF16)
            return 0

        lax.fori_loop(0, 4, one, 0)

    def copy2(self, flip):
        to = partner(self.chip, 4 * flip)
        return remote(self.col.at[to // 4], self.got2.at[flip - 1], self.send.at[3 + flip], self.recv.at[3 + flip], to, self.core)

    def start2(self):
        for flip in (1, 2, 3):
            self.copy2(flip).start()

    def copy3(self):
        ref = self.out.at[pl.ds(self.start_mine, self.half), :]
        return remote(ref, ref, self.send.at[7], self.recv.at[7], self.chip, 1 - self.core)

    def add2(self):
        for flip in (1, 2, 3):
            self.copy2(flip).wait()
        total = self.col[self.z].astype(F32)
        for k in range(3):
            total = total + self.got2[k].astype(F32)
        self.out[pl.ds(self.start_mine, self.half), :] = total
        self.copy3().start()

    def finish(self):
        self.copy3().wait()


def scatter_bufs(rows, cols):
    half = rows // 2
    return [pltpu.VMEM((4, 4, half, cols), BF16), pltpu.VMEM((4, 4, half, cols), BF16), pltpu.VMEM((3, 4, half, cols), BF16),
            pltpu.VMEM((4, half, cols), BF16), pltpu.VMEM((3, half, cols), BF16)]


class Total:
    def __init__(self, tile, got, send, recv, chip, core):
        self.tile, self.got, self.send, self.recv, self.chip, self.core = tile, got, send, recv, chip, core

    def copies(self, unit):
        base = 0 if unit == 1 else 3
        return [remote(self.tile.at[base // 3], self.got.at[base + k - 1], self.send.at[base + k - 1], self.recv.at[base + k - 1],
                       partner(self.chip, unit * k), self.core) for k in (1, 2, 3)]

    def start(self, unit):
        for copy in self.copies(unit):
            copy.start()

    def add(self, unit):
        base = 0 if unit == 1 else 3
        for copy in self.copies(unit):
            copy.wait()
        total = self.tile[base // 3]
        for k in range(3):
            total = total + self.got[base + k]
        self.tile[base // 3 + 1] = total


FLIPS = (1, 2, 3, 4, 8, 12)


def kernel_a(remote_on, off_ref, x_ref, cot_ref, *refs):
    if remote_on:
        masters, refs = refs[:5], refs[5:]
    else:
        w_in, refs = refs[:3], refs[3:]
    y_ref, qkv_ref, bctx_ref, bmid_ref, lse_ref, dot_ref, g2_out, g3_out, sums_ref = refs[:9]
    refs = refs[9:]
    if remote_on:
        w1_out, refs = refs[0], refs[1:]
    gup_ref, gdn_ref, gout_ref, ctx_ref, n1_ref, bias_ref, kstack_ref, vstack_ref, p_ref, vec_ref = refs[:10]
    refs = refs[10:]
    step = pl.program_id(0)
    group, length, width = x_ref.shape
    pairs = pl.num_programs(0) // 3
    early = HALVES * pairs
    tokens = group * length
    hidden = gup_ref.shape[1]
    chunks = hidden // width
    if remote_on:
        w1_ref, whole2, whole3, send, recv, out_sem = refs
        chip, core = lax.axis_index("fsdp"), lax.axis_index("dp")
        wide = 3 * SIDE
        gathers = [Gather(w, cols, send.at[i], recv.at[i], chip, core, i == 0) for i, (w, cols) in enumerate((
            (w1_ref.at[0], wide + LANES), (w1_ref.at[1], wide), (whole2, width + hidden), (whole3, width)))]
        w2_ref, w3_ref = [w.reshape(CHIPS * w.shape[2], w.shape[3]) for w in (whole2, whole3)]
    else:
        w1_ref, w2_ref, w3_ref = w_in
    wout_ref, wup_ref = w2_ref.at[:, 0:width], w2_ref.at[:, width:width + hidden]

    @pl.when(step == 0)
    def _():
        if remote_on:
            rows = [g.rows for g in gathers]
            z, yx = chip // 4, lax.rem(chip, 4)

            def cast_side(half):
                for part in range(3):
                    at = part * width + half * SIDE
                    w1_ref[half, z, yx, rows[0], part * SIDE:(part + 1) * SIDE] = masters[0][rows[0], at:at + SIDE].astype(BF16)

            cast_side(0)
            w1_ref[0, z, yx, rows[0], wide:] = masters[4][rows[0], :].astype(BF16)
            meet(chip, core, FLIPS)
            gathers[0].start()
            cast_side(1)
            whole2[z, yx, rows[2], 0:width] = masters[1][rows[2], :].astype(BF16)
            whole2[z, yx, rows[2], width:] = masters[2][rows[2], :].astype(BF16)
            whole3[z, yx, rows[3], :] = masters[3][rows[3], :].astype(BF16)
        gup_ref[...] = jnp.zeros_like(gup_ref)
        gdn_ref[...] = jnp.zeros_like(gdn_ref)
        gout_ref[...] = jnp.zeros_like(gout_ref)
        sums_ref[...] = jnp.zeros_like(sums_ref)
        kstack_ref[...] = jnp.zeros_like(kstack_ref)
        vstack_ref[...] = jnp.zeros_like(vstack_ref)
        if remote_on:
            gathers[0].spread()
            gathers[1].start()
            gathers[0].cross()
            gathers[2].start()
            gathers[0].last()
            gathers[3].start()
            gathers[0].finish()
        vec_ref[...] = side_of(w1_ref, 0, 3 * SIDE, 3 * SIDE + LANES).astype(F32).T

    events = {}
    if remote_on:
        events = {0: [gathers[1].spread, gathers[2].spread], 1: [gathers[1].cross, gathers[3].spread], 2: [gathers[1].last, gathers[2].cross],
                  3: [gathers[3].cross], 4: [gathers[2].last], 5: [gathers[3].last]}

    @pl.when(step < pairs)
    def _():
        x = x_ref[...].reshape(tokens, width).astype(F32)
        xhat, _ = xhat_of(x)
        n1 = (xhat * vec_ref[0:1, :] + vec_ref[1:2, :]).astype(BF16)
        n1_ref[pl.ds(step * group, group)] = n1.reshape(group, length, width)

    if remote_on:
        @pl.when(step == pairs)
        def _():
            gathers[1].finish()

    @pl.when(step < early)
    def _():
        half = step // pairs
        first_row = lax.rem(step, pairs) * group
        side = pl.ds(pl.multiple_of(half * SIDE, SIDE), SIDE)
        n1 = n1_ref[pl.ds(first_row, group)].reshape(tokens, width)
        q = ((nn(n1, side_of(w1_ref, half, 0, SIDE)) + vec_ref[2:3, side]) * HEAD_DIM ** (-0.5)).astype(BF16)
        k = nn(n1, side_of(w1_ref, half, SIDE, 2 * SIDE)).astype(BF16)
        v = (nn(n1, side_of(w1_ref, half, 2 * SIDE, 3 * SIDE)) + vec_ref[3:4, side]).astype(BF16)
        for part, value in enumerate((q, k, v)):
            qkv_ref[0, :, :, part * SIDE:(part + 1) * SIDE] = value.reshape(group, length, SIDE)
        lane = lax.broadcasted_iota(jnp.int32, (1, LANES), 1)

        def products(r):
            row = first_row + r
            crop_q = crop_of(off_ref[2 * row], off_ref[2 * row + 1], (length, 1), 0)
            crop_k = crop_of(off_ref[2 * row], off_ref[2 * row + 1], (1, PAD), 1)
            inside = lax.broadcasted_iota(jnp.int32, (1, PAD), 1) < length
            bias_ref[r] = jnp.where((crop_q == crop_k) & inside, 0.0, NEG)
            kr, vr = [[t[r * length:(r + 1) * length, c * LANES:(c + 1) * LANES] for c in range(2)] for t in (k, v)]
            stack_heads(kstack_ref.at[r], kr, PAD)
            stack_heads(vstack_ref.at[r], vr, PAD)
            return nt(q[r * length:(r + 1) * length], kstack_ref[r])

        def softmax(r, head, scores):
            lanes = slice(head * PAD, (head + 1) * PAD)
            s = scores[:, lanes] + bias_ref[r]
            peak = jnp.max(s, axis=-1, keepdims=True)
            e = jnp.exp(s - peak)
            p_ref[r, :, lanes] = e.astype(BF16)
            total = jnp.sum(e, axis=-1, keepdims=True)
            return 1.0 / total, peak + jnp.log(total)

        def contexts(r, stats):
            ctx = nn(p_ref[r], vstack_ref[r])
            for c in range(2):
                inverse = jnp.where(lane < HEAD_DIM, stats[2 * c][0], stats[2 * c + 1][0])
                lanes = pl.ds(pl.multiple_of(half * SIDE + c * LANES, LANES), LANES)
                ctx_ref[first_row + r, :, lanes] = (ctx[:, c * LANES:(c + 1) * LANES] * inverse).astype(BF16)
            table = jnp.zeros((length, LANES), F32)
            for head in range(FOUR):
                table = jnp.where(lane == head, stats[head][1], table)
            table = jnp.concatenate([table, jnp.zeros((PAD - length, LANES), F32)], axis=0)
            lse_ref[0, r] = table.T[:8]

        scores = [products(r) for r in range(group)]
        stats = []
        for r in range(group):
            stats.append([softmax(r, head, scores[r]) for head in range(FOUR)])
            if r:
                contexts(r - 1, stats[r - 1])
        contexts(group - 1, stats[group - 1])
        for at, todo in events.items():
            def run(todo=todo):
                for event in todo:
                    event()
            pl.when(step == at)(run)

    @pl.when(step == early)
    def _():
        if remote_on:
            gathers[2].finish()
            gathers[3].finish()
            pltpu.make_async_copy(w1_ref, w1_out, out_sem).start()

    @pl.when(step >= early)
    def _():
        first_row = (step - early) * group
        ctx = ctx_ref[pl.ds(first_row, group)].reshape(tokens, width)
        middle = x_ref[...].reshape(tokens, width).astype(F32) + (nn(ctx, wout_ref[...]) + vec_ref[4:5, :])
        xhat2, inv2 = xhat_of(middle)
        n2 = (xhat2 * vec_ref[5:6, :] + vec_ref[6:7, :]).astype(BF16)
        cot = cot_ref[...].reshape(tokens, width)
        result = middle + vec_ref[7 + chunks:8 + chunks, :]
        back_n2 = jnp.zeros((tokens, width), F32)

        def weight_grads(cols, active, back_up):
            gdn_ref[:, cols] += tn(cot, active)
            gup_ref[:, cols] += tn(n2, back_up)

        held = None

        def products(u):
            cols = slice(u * SIDE, (u + 1) * SIDE)
            bias = vec_ref[7 + u // 2:8 + u // 2, u % 2 * SIDE:(u % 2 + 1) * SIDE]
            return nn(n2, wup_ref[:, cols]) + bias, nt(cot, w3_ref[cols, :])

        ahead = products(0)
        for u in range(hidden // SIDE):
            cols = slice(u * SIDE, (u + 1) * SIDE)
            up, back_act = ahead
            if u + 1 < hidden // SIDE:
                ahead = products(u + 1)
            if held is not None:
                weight_grads(*held)
            square = up * up
            gate = 0.5 + 0.5 * jnp.tanh(up * (C0 + (C0 * C1) * square))
            active = up * gate
            slope = gate + active * (1.0 - gate) * (2.0 * C0 + (6.0 * C0 * C1) * square)
            active = active.astype(BF16)
            back_up = back_act * slope
            sums_ref[7 + u // 2:8 + u // 2, u % 2 * SIDE:(u % 2 + 1) * SIDE] += col_sum(back_up)
            back_up = back_up.astype(BF16)
            result = result + nn(active, w3_ref[cols, :])
            back_n2 = back_n2 + nt(back_up, wup_ref[:, cols])
            held = (cols, active, back_up)
        weight_grads(*held)
        y_ref[...] = result.astype(BF16).reshape(group, length, width)
        cot32 = cot.astype(F32)
        sums_ref[7 + chunks:8 + chunks, :] += col_sum(cot32)
        sums_ref[5:6, :] += col_sum(back_n2 * xhat2)
        sums_ref[6:7, :] += col_sum(back_n2)
        back_middle = cot32 + norm_back(back_n2 * vec_ref[5:6, :], xhat2, inv2)
        bmid_ref[...] = back_middle.reshape(group, length, width)
        back_att = back_middle.astype(BF16)
        sums_ref[4:5, :] += col_sum(back_middle)
        gout_ref[...] += tn(ctx, back_att)
        back_ctx = nt(back_att, wout_ref[...]).astype(BF16)
        bctx_ref[...] = back_ctx.reshape(group, length, width)
        pick = (lax.broadcasted_iota(jnp.int32, (16, width), 1) // HEAD_DIM == lax.broadcasted_iota(jnp.int32, (16, width), 0)).astype(BF16)
        for r in range(group):
            rows = slice(r * length, (r + 1) * length)
            product = ctx[rows].astype(F32) * back_ctx[rows].astype(F32)
            product = jnp.concatenate([product, jnp.zeros((PAD - length, width), F32)], axis=0)
            high = product.astype(BF16)
            dots = nt(pick, high) + nt(pick, (product - high.astype(F32)).astype(BF16))
            for half in range(HALVES):
                dot_ref[half, r, 0:FOUR, :] = dots[half * FOUR:(half + 1) * FOUR]
                dot_ref[half, r, FOUR:, :] = jnp.zeros((8 - FOUR, PAD), F32)

    @pl.when(step == pl.num_programs(0) - 1)
    def _():
        g2_out[:, 0:width] = gout_ref[...].astype(BF16)
        g2_out[:, width:] = gup_ref[...].astype(BF16)
        for u in range(chunks):
            g3_out[u * width:(u + 1) * width, :] = gdn_ref[:, u * width:(u + 1) * width].T.astype(BF16)
        if remote_on:
            pltpu.make_async_copy(w1_ref, w1_out, out_sem).wait()
            for g in gathers:
                g.drain()


def whole(shape):
    return pl.BlockSpec(shape, lambda s, *_: (0,) * len(shape), pipeline_mode=pl.Buffered(1))


def phase_a(remote_on, off, x, cot, weights):
    rows, length, width = x.shape
    pairs = rows // GROUP
    if remote_on:
        sizes = [(weights[0].shape[0], 3 * SIDE + LANES), (weights[1].shape[0], width + weights[2].shape[1]), weights[3].shape]
        w2_shape, w3_shape = (CHIPS * sizes[1][0], sizes[1][1]), (CHIPS * sizes[2][0], sizes[2][1])
    else:
        w2_shape, w3_shape = weights[1].shape, weights[2].shape
    hidden = w3_shape[0]
    blk = lambda w, index: pl.BlockSpec((GROUP, length, w), index)
    both = lambda s, *_: (lax.rem(s, pairs), 0, 0)
    late = lambda s, *_: (jnp.maximum(s - HALVES * pairs, 0), 0, 0)
    sided = lambda s, *_: (jnp.minimum(s // pairs, HALVES - 1), jnp.where(s < HALVES * pairs, lax.rem(s, pairs), pairs - 1), 0, 0)
    sds = jax.ShapeDtypeStruct
    out_specs = [blk(width, late), pl.BlockSpec((1, GROUP, length, 3 * SIDE), sided), blk(width, late), blk(width, late),
                 pl.BlockSpec((1, GROUP, 8, PAD), sided), pl.BlockSpec((HALVES, GROUP, 8, PAD), lambda s, *_: (0,) + late(s)),
                 whole(w2_shape), whole(w3_shape), whole((LANES, width))]
    out_shape = [sds(x.shape, BF16), sds((HALVES, rows, length, 3 * SIDE), BF16), sds(x.shape, BF16), sds(x.shape, F32),
                 sds((HALVES, rows, 8, PAD), F32), sds((HALVES, rows, 8, PAD), F32),
                 sds(w2_shape, BF16), sds(w3_shape, BF16), sds((LANES, width), F32)]
    scratch = [pltpu.VMEM((width, hidden), F32), pltpu.VMEM((width, hidden), F32), pltpu.VMEM((width, width), F32),
               pltpu.VMEM((rows, length, width), BF16), pltpu.VMEM((rows, length, width), BF16), pltpu.VMEM((GROUP, length, PAD), F32),
               pltpu.VMEM((GROUP, FOUR * PAD, SIDE), BF16), pltpu.VMEM((GROUP, FOUR * PAD, SIDE), BF16),
               pltpu.VMEM((GROUP, length, FOUR * PAD), BF16), pltpu.VMEM((LANES, width), F32)]
    params = dict(vmem_limit_bytes=62 << 20)
    if remote_on:
        out_specs.append(pl.BlockSpec(memory_space=pl.ANY))
        out_shape.append(sds((HALVES, 4, 4) + sizes[0], BF16))
        scratch += [pltpu.VMEM((HALVES, 4, 4) + sizes[0], BF16)] + [pltpu.VMEM((4, 4) + s, BF16) for s in sizes[1:]]
        scratch += [DMA((4,)), DMA((4, 9)), DMA]
        params.update(collective_id=0, has_side_effects=True)
    return pl.pallas_call(
        lambda *refs: kernel_a(remote_on, *refs),
        name="phase_a",
        grid_spec=pltpu.PrefetchScalarGridSpec(
            num_scalar_prefetch=1,
            grid=(3 * pairs,),
            in_specs=[blk(width, both), blk(width, late)] + [whole(w.shape) for w in weights],
            out_specs=out_specs,
            scratch_shapes=scratch,
        ),
        out_shape=out_shape,
        compiler_params=pltpu.CompilerParams(**params),
    )(off, x, cot, *weights)


def moments_of(grad, first, second):
    new_first = beta_first * first + (1.0 - beta_first) * grad
    new_second = beta_second * second + (1.0 - beta_second) * grad * grad
    direction = new_first / (1.0 - beta_first**STEP) / (jnp.sqrt(new_second / (1.0 - beta_second**STEP)) + adam_eps)
    return new_first, new_second, direction


def lanes_of(v):
    total = None
    for j in range(v.shape[1] // LANES):
        piece = v[:, j * LANES:(j + 1) * LANES]
        total = piece if total is None else total + piece
    return jnp.sum(total, axis=0, keepdims=True)


def kernel_b(remote_on, off_ref, x_ref, qkv_ref, bctx_ref, bmid_ref, lse_ref, dot_ref, w1_ref, sums_a_ref, *refs):
    if remote_on:
        g2_ref, g3_ref, masters, firsts, seconds = refs[0], refs[1], refs[2:6], refs[6:10], refs[10:14]
        xgrad_ref, r1a_ref, r1b_ref, r2_ref, r3_ref, rv_ref, norms_ref = refs[14:21]
        refs = refs[21:]
    else:
        xgrad_ref, g1_out, gv_out = refs[:3]
        refs = refs[3:]
    gqkv_ref, bqkv_ref, n1_ref, bias_ref, qstack_ref, ostack_ref, kstack_ref, p_ref, ds_ref, dsk_ref, sums_ref, vec_ref = refs[:12]
    refs = refs[12:]
    step = pl.program_id(0)
    group, length, width = x_ref.shape
    pairs = pl.num_programs(0) // 3
    early_steps = HALVES * pairs
    tokens = group * length
    if remote_on:
        bufs, finals, refs = refs[:25], refs[25:30], refs[30:]
        g1_ref, gv_ref, squares, got_q, send, recv, send_q, recv_q = refs
        chip, core = lax.axis_index("fsdp"), lax.axis_index("dp")
        shape4 = lambda ref: ref.reshape(4, 4, ref.shape[0] // CHIPS, ref.shape[1])
        scatters = [Scatter(g, bufs[5 * i:5 * i + 5], finals[i], send.at[i], recv.at[i], chip, core)
                    for i, g in enumerate((g1_ref.at[0], g1_ref.at[1], shape4(g2_ref), shape4(g3_ref), gv_ref))]
        first, second, mid, down, late = scatters
        norm = Total(squares, got_q, send_q, recv_q, chip, core)

    def one(s):
        def run():
            s.add0()
            s.start1()
        return run

    def two(s):
        def run():
            s.add1()
            s.start2()
        return run

    def both_one():
        one(mid)()
        one(down)()

    events = {0: [both_one], 4: [two(mid), one(first)], 6: [two(down), two(first)], 7: [mid.add2]} if remote_on else {}

    @pl.when(step == 0)
    def _():
        if remote_on:
            meet(chip, core, FLIPS)
            mid.start0()
            down.start0()
        for ref in (gqkv_ref, qstack_ref, ostack_ref, kstack_ref):
            ref[...] = jnp.zeros_like(ref)
        sums_ref[...] = sums_a_ref[...]
        vec_ref[...] = side_of(w1_ref, 0, 3 * SIDE, 3 * SIDE + LANES).astype(F32).T

    @pl.when(step < pairs)
    def _():
        x = x_ref[...].reshape(tokens, width).astype(F32)
        xhat, _ = xhat_of(x)
        n1 = (xhat * vec_ref[0:1, :] + vec_ref[1:2, :]).astype(BF16)
        n1_ref[pl.ds(step * group, group)] = n1.reshape(group, length, width)

    if remote_on:
        @pl.when(step == pairs)
        def _():
            g1_ref[0] = gqkv_ref[0].astype(BF16).reshape(g1_ref.shape[1:])
            first.start0()

    @pl.when(step < early_steps)
    def _():
        half = step // pairs
        first_row = lax.rem(step, pairs) * group

        def products(r):
            row = first_row + r
            crop_k = crop_of(off_ref[2 * row], off_ref[2 * row + 1], (length, 1), 0)
            crop_q = crop_of(off_ref[2 * row], off_ref[2 * row + 1], (1, PAD), 1)
            bias_ref[r] = jnp.where(crop_q == crop_k, 0.0, NEG)
            tiles = lambda ref, at: [ref[..., at + c * LANES:at + (c + 1) * LANES] for c in range(2)]
            stack_heads(qstack_ref.at[r], tiles(qkv_ref.at[0, r], 0), PAD)
            stack_heads(kstack_ref.at[r], tiles(qkv_ref.at[0, r], SIDE), length)
            stack_heads(ostack_ref.at[r], tiles(bctx_ref.at[r], 0), PAD)
            return nt(qkv_ref[0, r, :, SIDE:2 * SIDE], qstack_ref[r]), nt(qkv_ref[0, r, :, 2 * SIDE:], ostack_ref[r])

        def softmax(r, head, scores, back_probs):
            lanes = slice(head * PAD, (head + 1) * PAD)
            p = jnp.exp((scores[:, lanes] + bias_ref[r]) - lse_ref[0, r, head:head + 1, :])
            ds = (p * (back_probs[:, lanes] - dot_ref[0, r, head:head + 1, :])).astype(BF16)
            p_ref[r, :, lanes] = p.astype(BF16)
            ds_ref[r, :, lanes] = ds
            dsk_ref[r, head * length:(head + 1) * length, :] = ds

        def back_value(r):
            bqkv_ref[half, first_row + r, :, 2 * SIDE:] = nn(p_ref[r], ostack_ref[r]).astype(BF16)

        def back_key(r):
            bqkv_ref[half, first_row + r, :, SIDE:2 * SIDE] = nn(ds_ref[r], qstack_ref[r]).astype(BF16)

        def back_query(r):
            dq = tn(dsk_ref[r], kstack_ref[r])[:length] * HEAD_DIM ** (-0.5)
            bqkv_ref[half, first_row + r, :, 0:SIDE] = dq.astype(BF16)

        scores = [products(r) for r in range(group)]
        after = (back_value, back_key, back_query)
        for r in range(group):
            for head in range(FOUR):
                softmax(r, head, *scores[r])
                if r and head < len(after):
                    after[head](r - 1)
        for work in after:
            work(group - 1)
        for at, todo in events.items():
            def run(todo=todo):
                for event in todo:
                    event()
            pl.when(step == at)(run)
        n1 = n1_ref[pl.ds(first_row, group)].reshape(tokens, width)
        back = bqkv_ref[half, pl.ds(first_row, group)].reshape(tokens, 3 * SIDE)
        side = pl.ds(pl.multiple_of(half * SIDE, SIDE), SIDE)
        sums_ref[2:3, side] += col_sum(back[:, :SIDE].astype(F32))
        sums_ref[3:4, side] += col_sum(back[:, 2 * SIDE:].astype(F32))
        gqkv_ref[half] += tn(n1, back)

    @pl.when(step == early_steps)
    def _():
        if remote_on:
            g1_ref[1] = gqkv_ref[1].astype(BF16).reshape(g1_ref.shape[1:])
            second.start0()
            first.add2()
            down.add2()
        else:
            g1_out[...] = gqkv_ref[...].astype(BF16)

    @pl.when(step >= early_steps)
    def _():
        x = x_ref[...].reshape(tokens, width).astype(F32)
        xhat, inv = xhat_of(x)
        back_n1 = None
        for half in range(HALVES):
            back = bqkv_ref[half, pl.ds((step - early_steps) * group, group)].reshape(tokens, 3 * SIDE)
            term = nt(back, side_of(w1_ref, half, 0, 3 * SIDE))
            back_n1 = term if back_n1 is None else back_n1 + term
        sums_ref[0:1, :] += col_sum(back_n1 * xhat)
        sums_ref[1:2, :] += col_sum(back_n1)
        grad = bmid_ref[...].reshape(tokens, width) + norm_back(back_n1 * vec_ref[0:1, :], xhat, inv)
        xgrad_ref[...] = grad.reshape(group, length, width)

    @pl.when(step == early_steps)
    def _():
        if remote_on:
            one(second)()

    @pl.when(step == pl.num_programs(0) - 1)
    def _():
        if not remote_on:
            gv_out[...] = sums_ref[...].T.astype(BF16)
            return
        gv_ref[...] = sums_ref[...].T.astype(BF16).reshape(gv_ref.shape)
        late.start0()
        wide = masters[2].shape[1]
        grads = (None, finals[2].at[:, 0:width], finals[2].at[:, width:width + wide], finals[3])

        def square(i, places):
            sums = [None, None]
            for grad, cols in places:
                master = masters[i][:, cols]
                _, _, direction = moments_of(grad, firsts[i][:, cols], seconds[i][:, cols])
                update = direction + weight_decay * master
                for n, v in enumerate((master, update)):
                    part = lanes_of(v * v)
                    sums[n] = part if sums[n] is None else sums[n] + part
            squares[0, i:i + 1, :] = sums[0]
            squares[0, 4 + i:5 + i, :] = sums[1]

        for s in (first, mid, down):
            s.finish()
        for i in (1, 2, 3):
            square(i, [(grads[i][...], slice(None))])
        late.add0()
        late.start1()
        second.add1()
        second.start2()
        r1a_ref[...] = finals[0][...]
        r2_ref[...] = finals[2][...]
        r3_ref[...] = finals[3][...]
        late.add1()
        late.start2()
        second.add2()
        second.finish()
        square(0, [(finals[half][:, part * SIDE:(part + 1) * SIDE], slice(part * width + half * SIDE, part * width + (half + 1) * SIDE))
                   for half in range(HALVES) for part in range(3)])
        norm.start(1)
        r1b_ref[...] = finals[1][...]
        late.add2()
        norm.add(1)
        norm.start(4)
        late.finish()
        rv_ref[...] = finals[4][...]
        norm.add(4)
        norms_ref[...] = jnp.broadcast_to(jnp.sqrt(jnp.sum(squares[2], axis=1, keepdims=True)), (8, LANES))


def phase_b(remote_on, off, x, qkv, bctx, bmid, lse, dots, w1, sums_a, grads=(), masters=(), firsts=(), seconds=()):
    rows, length, width = x.shape
    pairs = rows // GROUP
    blk = lambda w, index: pl.BlockSpec((GROUP, length, w), index)
    both = lambda s, *_: (lax.rem(s, pairs), 0, 0)
    late = lambda s, *_: (jnp.maximum(s - HALVES * pairs, 0), 0, 0)
    side = lambda s: jnp.minimum(s // pairs, HALVES - 1)
    pair = lambda s: jnp.where(s < HALVES * pairs, lax.rem(s, pairs), pairs - 1)
    sds = jax.ShapeDtypeStruct
    rowed = pl.BlockSpec((1, GROUP, 8, PAD), lambda s, *_: (side(s), pair(s), 0, 0))
    extra = (*grads, *masters, *firsts, *seconds)
    stack = lambda: pltpu.VMEM((GROUP, FOUR * PAD, SIDE), BF16)
    probs = lambda: pltpu.VMEM((GROUP, length, FOUR * PAD), BF16)
    scratch = [pltpu.VMEM((HALVES, width, 3 * SIDE), F32), pltpu.VMEM((HALVES, rows, length, 3 * SIDE), BF16),
               pltpu.VMEM((rows, length, width), BF16), pltpu.VMEM((GROUP, length, PAD), F32), stack(), stack(),
               pltpu.VMEM((GROUP, FOUR * length, SIDE), BF16), probs(), probs(), pltpu.VMEM((GROUP, FOUR * length, PAD), BF16),
               pltpu.VMEM((LANES, width), F32), pltpu.VMEM((LANES, width), F32)]
    params = dict(vmem_limit_bytes=62 << 20)
    if remote_on:
        sizes = [(width // CHIPS, 3 * SIDE)] * HALVES + [(g.shape[0] // CHIPS, g.shape[1]) for g in grads]
        sizes.append((width // CHIPS, LANES))
        outs = [sds(s, F32) for s in sizes] + [sds((8, LANES), F32)]
        for s in sizes:
            scratch += scatter_bufs(*s)
        scratch += [pltpu.VMEM(s, F32) for s in sizes]
        scratch += [pltpu.VMEM((HALVES, 4, 4) + sizes[0], BF16), pltpu.VMEM((4, 4) + sizes[4], BF16),
                    pltpu.VMEM((3, 8, LANES), F32), pltpu.VMEM((6, 8, LANES), F32), DMA((5, 8)), DMA((5, 8)), DMA((6,)), DMA((6,))]
        params.update(collective_id=1, has_side_effects=True)
    else:
        outs = [sds((HALVES, width, 3 * SIDE), BF16), sds((width, LANES), BF16)]
    return pl.pallas_call(
        lambda *refs: kernel_b(remote_on, *refs),
        name="phase_b",
        grid_spec=pltpu.PrefetchScalarGridSpec(
            num_scalar_prefetch=1,
            grid=(3 * pairs,),
            in_specs=[blk(width, both), pl.BlockSpec((1, GROUP, length, 3 * SIDE), lambda s, *_: (side(s), pair(s), 0, 0)),
                      pl.BlockSpec((GROUP, length, SIDE), lambda s, *_: (pair(s), 0, side(s))), blk(width, late),
                      rowed, rowed, whole(w1.shape),
                      whole(sums_a.shape)] + [whole(e.shape) for e in extra],
            out_specs=[blk(width, late)] + [whole(o.shape) for o in outs],
            scratch_shapes=scratch,
        ),
        out_shape=[sds(x.shape, F32)] + outs,
        compiler_params=pltpu.CompilerParams(**params),
    )(off, x, qkv, bctx, bmid, lse, dots, w1, sums_a, *extra)


def update_kernel(y_ref, xgrad_ref, r1a, r1b, r2, r3, norms_ref, *refs):
    masters, firsts, seconds = refs[0:4], refs[4:8], refs[8:12]
    y_out, xgrad_out = refs[12:14]
    new_m, new_f, new_s, copies, norm_out = refs[14:18], refs[18:22], refs[22:26], refs[26:30], refs[30]
    moves = []
    for i, (src, dst) in enumerate(((xgrad_ref, xgrad_out), (y_ref, y_out))):
        held, sems = refs[31 + i], refs[33]
        for row in range(src.shape[0]):
            moves.append((pltpu.make_async_copy(src.at[row], held.at[row], sems.at[0, i, row]),
                          pltpu.make_async_copy(held.at[row], dst.at[row], sems.at[1, i, row])))
            moves[-1][0].start()
    for arrive, leave in moves:
        arrive.wait()
        leave.start()
    width, wide = masters[1].shape[1], masters[2].shape[1]
    places = [(0, (r1a, r1b)[half][:, part * SIDE:(part + 1) * SIDE], slice(part * width + half * SIDE, part * width + (half + 1) * SIDE))
              for half in range(HALVES) for part in range(3)]
    places += [(1, r2[:, 0:width], slice(None)), (2, r2[:, width:width + wide], slice(None)), (3, r3[...], slice(None))]
    row = lax.broadcasted_iota(jnp.int32, (3, 4), 0)
    col = lax.broadcasted_iota(jnp.int32, (3, 4), 1)
    table = jnp.zeros((3, 4), F32)
    for i, grad, cols in places:
        weight_norm, update_norm = norms_ref[i:i + 1, 0:1], norms_ref[4 + i:5 + i, 0:1]
        trust = weight_norm / update_norm
        first, second, direction = moments_of(grad, firsts[i][:, cols], seconds[i][:, cols])
        master = masters[i][:, cols]
        new = master - matrix_rate * trust * (direction + weight_decay * master)
        new_m[i][:, cols] = new
        copies[i][:, cols] = new.astype(BF16)
        new_f[i][:, cols] = first
        new_s[i][:, cols] = second
        for r, value in enumerate((weight_norm, update_norm, trust)):
            table = jnp.where((row == r) & (col == i), value, table)
    norm_out[...] = table
    for _, leave in moves:
        leave.wait()


def update_all(y, xgrad, reduced, norms, masters, firsts, seconds):
    sds = jax.ShapeDtypeStruct
    place = pl.BlockSpec(memory_space=pl.ANY)
    ins = (*reduced, norms, *masters, *firsts, *seconds)
    outs = [sds(m.shape, F32) for m in masters] * 3 + [sds(m.shape, BF16) for m in masters] + [sds((3, 4), F32)]
    return pl.pallas_call(
        update_kernel,
        name="update",
        grid=(1,),
        out_shape=[sds(y.shape, y.dtype), sds(xgrad.shape, xgrad.dtype)] + outs,
        in_specs=[place, place] + [whole(a.shape) for a in ins],
        out_specs=[place, place] + [whole(o.shape) for o in outs],
        scratch_shapes=[pltpu.VMEM(xgrad.shape, xgrad.dtype), pltpu.VMEM(y.shape, y.dtype), DMA((2, 2, y.shape[0]))],
        compiler_params=pltpu.CompilerParams(vmem_limit_bytes=62 << 20),
    )(y, xgrad, *ins)


def shards(block_in, offsets, cotangent, w_qkv, w_out, w_up, w_down, vectors, *moments):
    masters = (w_qkv, w_out, w_up, w_down)
    firsts, seconds = moments[:5], moments[5:]
    micro, local_rows, length, width = block_in.shape
    rows = micro * local_rows
    chips = lax.axis_size("fsdp")
    near = chips == CHIPS and lax.axis_size("dp") == 2
    columns = vectors.shape[0] * chips // width
    table = jnp.pad(vectors.reshape(-1, columns), ((0, 0), (0, LANES - columns)))
    x = block_in.reshape(rows, length, width)
    cot = cotangent.reshape(rows, length, width)
    off = offsets.reshape(-1)
    if near:
        y, qkv, bctx, bmid, lse, dots, g2, g3, sums_a, w1 = phase_a(True, off, x, cot, (*masters, table))
        xgrad, *reduced, norms = phase_b(True, off, x, qkv, bctx, bmid, lse, dots, w1, sums_a, (g2, g3), masters, firsts[:4], seconds[:4])
    else:
        sides = w_qkv.reshape(-1, 3, HALVES, SIDE).transpose(2, 0, 1, 3).reshape(HALVES, -1, 3 * SIDE)
        owns = [jnp.concatenate([sides, jnp.broadcast_to(table, (HALVES,) + table.shape)], axis=2),
                jnp.concatenate([w_out, w_up], axis=1), w_down]
        wholes = [lax.all_gather(o.astype(BF16), "fsdp", axis=o.ndim - 2, tiled=True) for o in owns]
        y, qkv, bctx, bmid, lse, dots, g2, g3, sums_a = phase_a(False, off, x, cot, wholes)
        xgrad, g1, gv = phase_b(False, off, x, qkv, bctx, bmid, lse, dots, wholes[0], sums_a)
        reduced = [lax.psum(lax.psum_scatter(g.astype(F32), "fsdp", scatter_dimension=0, tiled=True), "dp")
                   for g in (g1[0], g1[1], g2, g3, gv)]
        grad1 = jnp.stack(reduced[:2]).reshape(HALVES, -1, 3, SIDE).transpose(1, 2, 0, 3).reshape(w_qkv.shape)
        grads = (grad1, reduced[2][:, :width], reduced[2][:, width:], reduced[3])
        updates = [moments_of(g, m, s)[2] + weight_decay * w for g, m, s, w in zip(grads, firsts, seconds, masters)]
        squares = jnp.stack([jnp.sum(w * w) for w in masters] + [jnp.sum(u * u) for u in updates])
        norms = jnp.broadcast_to(jnp.sqrt(lax.psum(squares, "fsdp"))[:, None], (8, LANES))
    y, xgrad, *news, matrix_norms = update_all(y, xgrad, reduced[:4], norms, masters, firsts[:4], seconds[:4])
    vec_first, vec_second, vec_direction = moments_of(reduced[4][:, :columns].reshape(-1), firsts[4], seconds[4])
    vec_new = vectors - vector_rate * vec_direction
    return (y.reshape(block_in.shape), xgrad.reshape(block_in.shape), *news[0:4], vec_new, *news[4:8], vec_first,
            *news[8:12], vec_second, *news[12:16], vec_new.astype(BF16), matrix_norms)


def solution(mesh):
    batch, matrix, vector = P(None, ("fsdp", "dp"), None, None), P("fsdp", None), P("fsdp")
    params = (matrix,) * 4 + (vector,)
    in_specs = (batch, P(None, ("fsdp", "dp"), None), batch) + params * 3
    out_specs = (batch, batch) + params * 4 + (P(),)
    return jax.shard_map(shards, mesh=mesh, in_specs=in_specs, out_specs=out_specs, check_vma=False)
```

```python
import jax
import jax.numpy as jnp
from jax import lax
from jax.experimental import pallas as pl
from jax.experimental.pallas import tpu as pltpu
from jax.sharding import PartitionSpec as P

HEAD_DIM = 64
STEP = 5
EPS = 1e-05
beta_first = 0.5
beta_second = 0.5
adam_eps = 1e-06
weight_decay = 0.01
matrix_rate = 1.0
vector_rate = 0.1
CHIPS = 16
GROUP = 2
LANES = 128
HALVES = 2
SIDE = 256
FOUR = 4
PAD = 384
NEG = -1e30
C0 = 0.7978845608028654
C1 = 0.044715
F32 = jnp.float32
BF16 = jnp.bfloat16
MESH = pl.DeviceIdType.MESH
DMA = pltpu.SemaphoreType.DMA


def nn(a, b):
    return lax.dot_general(a, b, (((1,), (0,)), ((), ())), preferred_element_type=F32)


def nt(a, b):
    return lax.dot_general(a, b, (((1,), (1,)), ((), ())), preferred_element_type=F32)


def tn(a, b):
    return lax.dot_general(a, b, (((0,), (0,)), ((), ())), preferred_element_type=F32)


def xhat_of(v):
    center = v - jnp.mean(v, axis=-1, keepdims=True)
    spread = jnp.mean(center * center, axis=-1, keepdims=True)
    inv = lax.rsqrt(spread + EPS)
    return center * inv, inv


def norm_back(e, xhat, inv):
    return (e - jnp.mean(e, axis=-1, keepdims=True) - xhat * jnp.mean(e * xhat, axis=-1, keepdims=True)) * inv


def crop_of(first, second, shape, axis):
    t = lax.broadcasted_iota(jnp.int32, shape, axis)
    return (t >= first).astype(jnp.int32) + (t >= second).astype(jnp.int32)


def side_of(ref, half, lo, hi):
    v = ref[half, ..., lo:hi]
    return v.reshape(-1, hi - lo)


def stack_heads(ref, tiles, pitch):
    low = lax.broadcasted_iota(jnp.int32, (1, LANES), 1) < HEAD_DIM
    for head in range(FOUR):
        tile = tiles[head // 2]
        keep = low if head % 2 == 0 else jnp.logical_not(low)
        lanes = slice(head // 2 * LANES, head // 2 * LANES + LANES)
        ref[head * pitch:head * pitch + tile.shape[0], lanes] = jnp.where(keep, tile, jnp.zeros_like(tile))


def offsets_of(ref, row):
    micro, inner = row // ref.shape[1], lax.rem(row, ref.shape[1])
    both = ref[micro, pl.ds(inner, 1), :]
    return both[:, 0:1], both[:, 1:2]


def col_sum(v):
    return jnp.sum(v, axis=0, keepdims=True)


def partner(chip, flip):
    out = chip
    for bit in (1, 2, 4, 8):
        if flip & bit:
            out = out + bit - 2 * bit * lax.rem(chip // bit, 2)
    return out


def meet(chip, core, flips, others):
    barrier = pltpu.get_barrier_semaphore()
    for flip in flips:
        pl.semaphore_signal(barrier, inc=1, device_id=(partner(chip, flip), core), device_id_type=MESH)
    for flip in others:
        pl.semaphore_signal(barrier, inc=1, device_id=(partner(chip, flip), 1 - core), device_id_type=MESH)
    pl.semaphore_wait(barrier, len(flips) + len(others))


def remote(src, dst, send_sem, recv_sem, chip, core):
    return pltpu.make_async_remote_copy(src_ref=src, dst_ref=dst, send_sem=send_sem, recv_sem=recv_sem,
                                        device_id=(chip, core), device_id_type=MESH)


def wait_bytes(ref, sem):
    pltpu.make_async_copy(ref, ref, sem).wait()


class Gather:
    def __init__(self, whole, cols, send, recv, chip, core, quick, calm):
        self.whole, self.cols, self.chip, self.core, self.send, self.recv, self.quick, self.calm = whole, cols, chip, core, send, recv, quick, calm
        self.half = whole.shape[-2] // 2
        start = pl.multiple_of(core * self.half, self.half)
        self.rows, self.all = pl.ds(start, self.half), pl.ds(0, cols)
        self.mine = (self.rows, self.all)
        if self.half >= 32:
            q = self.half // 2
            self.cuts = [(pl.ds(start + i * q, q), self.all) for i in range(2)]
        else:
            q = cols // 256 * 128
            self.cuts = [(self.rows, pl.ds(0, q)), (self.rows, pl.ds(q, cols - q))]

    def column(self, flip, cut):
        return self.whole.at[:, lax.rem(partner(self.chip, flip), 4), cut[0], cut[1]]

    def shard(self, flip):
        at = partner(self.chip, flip)
        return self.whole.at[at // 4, lax.rem(at, 4), self.rows, self.all]

    def push(self, ref, sem, to):
        remote(ref, ref, self.send, self.recv.at[sem], partner(self.chip, to), self.core).start()

    def to_twin(self, flip):
        if self.calm and flip != 3:
            return
        ref = self.whole.at[:, :, self.rows, self.all] if self.calm else self.column(flip, self.mine)
        remote(ref, ref, self.send, self.recv.at[8], self.chip, 1 - self.core).start()

    def start(self):
        own = self.shard(0)
        for flip in (4, 8, 12):
            self.push(own, flip // 4, flip)
        if self.quick:
            self.push(own, 4, 1)
            self.push(own, 5, 2)

    def spread(self):
        for flip in (4, 8, 12):
            ref = self.shard(flip)
            wait_bytes(ref, self.recv.at[flip // 4])
            if self.quick:
                self.push(ref, 4, 1)
                self.push(ref, 5, 2)
        ref = self.column(0, self.mine)
        if not self.quick:
            self.push(ref, 4, 1)
            self.push(ref, 5, 2)
        self.to_twin(0)

    def cross(self):
        for sem, via, to, cut in ((4, 1, 2, 0), (5, 2, 1, 1)):
            wait_bytes(self.column(via, self.mine), self.recv.at[sem])
            self.push(self.column(via, self.cuts[cut]), 6 + cut, to)
            self.to_twin(via)

    def last(self):
        for cut in range(2):
            wait_bytes(self.column(3, self.cuts[cut]), self.recv.at[6 + cut])
        self.to_twin(3)

    def finish(self):
        wait_bytes(self.whole.at[:, :, pl.ds(0, self.half), self.all], self.recv.at[8])

    def drain(self):
        rows = pl.ds(0, self.half)
        for zs, yxs in (((0, 4), (0, 4)), ((0, 3), (0, 4)), ((0, 1), (0, 3))):
            wait_bytes(self.whole.at[pl.ds(*zs), pl.ds(*yxs), rows, self.all], self.send)


class Scatter:
    def __init__(self, grad, bufs, out, send, recv, chip, core):
        self.grad, self.out, self.send, self.recv, self.chip, self.core = grad, out, send, recv, chip, core
        self.got0, self.part, self.got1, self.col, self.got2 = bufs
        self.half = grad.shape[2] // 2
        self.start_mine = pl.multiple_of(core * self.half, self.half)
        self.rows_mine = pl.ds(self.start_mine, self.half)
        self.z, self.yx = chip // 4, lax.rem(chip, 4)

    def copy0(self):
        theirs = pl.ds(pl.multiple_of((1 - self.core) * self.half, self.half), self.half)
        return remote(self.grad.at[:, :, theirs, :], self.got0, self.send.at[0], self.recv.at[0], self.chip, 1 - self.core)

    def start0(self):
        self.copy0().start()

    def add0(self):
        self.copy0().wait()

        def one(i, _):
            z, yx = i // 4, lax.rem(i, 4)
            mine = self.grad[z, yx, pl.ds(self.start_mine, self.half), :].astype(F32)
            self.part[z, yx] = (mine + self.got0[z, yx].astype(F32)).astype(BF16)
            return 0

        lax.fori_loop(0, CHIPS, one, 0)

    def copy1(self, flip):
        to = partner(self.chip, flip)
        return remote(self.part.at[:, lax.rem(to, 4)], self.got1.at[flip - 1], self.send.at[flip], self.recv.at[flip], to, self.core)

    def start1(self):
        for flip in (3, 1, 2):
            self.copy1(flip).start()

    def add1(self):
        for flip in (1, 2, 3):
            self.copy1(flip).wait()

        def one(z, _):
            total = self.part[z, self.yx].astype(F32)
            for k in range(3):
                total = total + self.got1[k, z].astype(F32)
            self.col[z] = total.astype(BF16)
            return 0

        lax.fori_loop(0, 4, one, 0)

    def copy2(self, flip):
        to = partner(self.chip, 4 * flip)
        return remote(self.col.at[to // 4], self.got2.at[flip - 1], self.send.at[3 + flip], self.recv.at[3 + flip], to, self.core)

    def start2(self):
        for flip in (1, 2, 3):
            self.copy2(flip).start()

    def copy3(self):
        ref = self.out.at[pl.ds(self.start_mine, self.half), :]
        return remote(ref, ref, self.send.at[7], self.recv.at[7], self.chip, 1 - self.core)

    def add2(self):
        for flip in (1, 2, 3):
            self.copy2(flip).wait()
        total = self.col[self.z].astype(F32)
        for k in range(3):
            total = total + self.got2[k].astype(F32)
        self.out[pl.ds(self.start_mine, self.half), :] = total
        self.copy3().start()

    def finish(self):
        self.copy3().wait()


def scatter_bufs(rows, cols):
    half = rows // 2
    return [pltpu.VMEM((4, 4, half, cols), BF16), pltpu.VMEM((4, 4, half, cols), BF16), pltpu.VMEM((3, 4, half, cols), BF16),
            pltpu.VMEM((4, half, cols), BF16), pltpu.VMEM((3, half, cols), BF16)]


class Total:
    def __init__(self, tile, got, send, recv, chip, core):
        self.tile, self.got, self.send, self.recv, self.chip, self.core = tile, got, send, recv, chip, core

    def copies(self, turn):
        if turn == 0:
            peers = [(flip, other) for flip in range(4) for other in range(2) if flip or other]
        else:
            peers = [(flip, 0) for flip in (4, 8, 12)]
        out = []
        for n, (flip, other) in enumerate(peers):
            at = 7 * turn + n
            out.append(remote(self.tile.at[turn], self.got.at[at], self.send.at[at], self.recv.at[at], partner(self.chip, flip),
                              1 - self.core if other else self.core))
        return out

    def start(self, turn):
        for copy in self.copies(turn):
            copy.start()

    def add(self, turn):
        copies = self.copies(turn)
        for copy in copies:
            copy.wait()
        total = self.tile[turn]
        for n in range(len(copies)):
            total = total + self.got[7 * turn + n]
        self.tile[turn + 1] = total


FLIPS = (1, 2, 3, 4, 8, 12)


def kernel_a(remote_on, off_ref, x_ref, cot_ref, *refs):
    if remote_on:
        masters, refs = refs[:5], refs[5:]
    else:
        w_in, refs = refs[:3], refs[3:]
    y_ref, qkv_ref, bctx_ref, bmid_ref, lse_ref, dot_ref, g2_out, g3_out, sums_ref = refs[:9]
    refs = refs[9:]
    if remote_on:
        w1_out, refs = refs[0], refs[1:]
    gup_ref, gdn_ref, gout_ref, ctx_ref, n1_ref, bias_ref, kstack_ref, vstack_ref, p_ref, vec_ref = refs[:10]
    refs = refs[10:]
    step = pl.program_id(0)
    group, length, width = x_ref.shape
    pairs = pl.num_programs(0) // 3
    early = HALVES * pairs
    tokens = group * length
    hidden = gup_ref.shape[1]
    chunks = hidden // width
    if remote_on:
        w1_ref, whole2, whole3, send, recv, out_sem = refs
        chip, core = lax.axis_index("fsdp"), lax.axis_index("dp")
        wide = 3 * SIDE
        gathers = [Gather(w, cols, send.at[i], recv.at[i], chip, core, i == 0, i in (1, 2)) for i, (w, cols) in enumerate((
            (w1_ref.at[0], wide + LANES), (w1_ref.at[1], wide), (whole2, width + hidden), (whole3, width)))]
        w2_ref, w3_ref = [w.reshape(CHIPS * w.shape[2], w.shape[3]) for w in (whole2, whole3)]
    else:
        w1_ref, w2_ref, w3_ref = w_in
    wout_ref, wup_ref = w2_ref.at[:, 0:width], w2_ref.at[:, width:width + hidden]

    @pl.when(step == 0)
    def _():
        if remote_on:
            rows = [g.rows for g in gathers]
            z, yx = chip // 4, lax.rem(chip, 4)

            def cast_side(half):
                for part in range(3):
                    at = part * width + half * SIDE
                    w1_ref[half, z, yx, rows[0], part * SIDE:(part + 1) * SIDE] = masters[0][rows[0], at:at + SIDE].astype(BF16)

            cast_side(0)
            columns = masters[4].shape[1]
            w1_ref[0, z, yx, rows[0], wide:] = jnp.zeros((gathers[0].half, LANES), BF16)
            w1_ref[0, z, yx, rows[0], wide:wide + columns] = masters[4][rows[0], :].astype(BF16)
            meet(chip, core, FLIPS, (0,))
            gathers[0].start()
            cast_side(1)
            whole2[z, yx, rows[2], 0:width] = masters[1][rows[2], :].astype(BF16)
            whole2[z, yx, rows[2], width:] = masters[2][rows[2], :].astype(BF16)
            whole3[z, yx, rows[3], :] = masters[3][rows[3], :].astype(BF16)
        gup_ref[...] = jnp.zeros_like(gup_ref)
        gdn_ref[...] = jnp.zeros_like(gdn_ref)
        gout_ref[...] = jnp.zeros_like(gout_ref)
        sums_ref[...] = jnp.zeros_like(sums_ref)
        kstack_ref[...] = jnp.zeros_like(kstack_ref)
        vstack_ref[...] = jnp.zeros_like(vstack_ref)
        if remote_on:
            gathers[0].spread()
            for g in gathers[1:]:
                g.start()
            gathers[0].cross()
            gathers[0].last()
            gathers[1].spread()
            gathers[0].finish()
        vec_ref[...] = side_of(w1_ref, 0, 3 * SIDE, 3 * SIDE + LANES).astype(F32).T

    events = {}
    if remote_on:
        events = {0: [gathers[1].cross], 1: [gathers[2].spread], 2: [gathers[1].last], 3: [gathers[2].cross, gathers[3].spread], 5: [gathers[2].last], 6: [gathers[3].cross]}

    @pl.when(step < pairs)
    def _():
        x = x_ref[...].reshape(tokens, width).astype(F32)
        xhat, _ = xhat_of(x)
        n1 = (xhat * vec_ref[0:1, :] + vec_ref[1:2, :]).astype(BF16)
        n1_ref[pl.ds(step * group, group)] = n1.reshape(group, length, width)

    if remote_on:
        @pl.when(step == pairs)
        def _():
            gathers[1].finish()

    @pl.when(step < early)
    def _():
        half = step // pairs
        first_row = lax.rem(step, pairs) * group
        side = pl.ds(pl.multiple_of(half * SIDE, SIDE), SIDE)
        n1 = n1_ref[pl.ds(first_row, group)].reshape(tokens, width)
        q = ((nn(n1, side_of(w1_ref, half, 0, SIDE)) + vec_ref[2:3, side]) * HEAD_DIM ** (-0.5)).astype(BF16)
        k = nn(n1, side_of(w1_ref, half, SIDE, 2 * SIDE)).astype(BF16)
        v = (nn(n1, side_of(w1_ref, half, 2 * SIDE, 3 * SIDE)) + vec_ref[3:4, side]).astype(BF16)
        for part, value in enumerate((q, k, v)):
            qkv_ref[0, :, :, part * SIDE:(part + 1) * SIDE] = value.reshape(group, length, SIDE)
        lane = lax.broadcasted_iota(jnp.int32, (1, LANES), 1)

        def products(r):
            row = first_row + r
            crop_q = crop_of(*offsets_of(off_ref, row), (length, 1), 0)
            crop_k = crop_of(*offsets_of(off_ref, row), (1, PAD), 1)
            inside = lax.broadcasted_iota(jnp.int32, (1, PAD), 1) < length
            bias_ref[r] = jnp.where((crop_q == crop_k) & inside, 0.0, NEG)
            kr, vr = [[t[r * length:(r + 1) * length, c * LANES:(c + 1) * LANES] for c in range(2)] for t in (k, v)]
            stack_heads(kstack_ref.at[r], kr, PAD)
            stack_heads(vstack_ref.at[r], vr, PAD)
            return nt(q[r * length:(r + 1) * length], kstack_ref[r])

        def softmax(r, head, scores):
            lanes = slice(head * PAD, (head + 1) * PAD)
            s = scores[:, lanes] + bias_ref[r]
            peak = jnp.max(s, axis=-1, keepdims=True)
            e = jnp.exp(s - peak)
            p_ref[r, :, lanes] = e.astype(BF16)
            total = jnp.sum(e, axis=-1, keepdims=True)
            return 1.0 / total, peak + jnp.log(total)

        def contexts(r, stats):
            ctx = nn(p_ref[r], vstack_ref[r])
            for c in range(2):
                inverse = jnp.where(lane < HEAD_DIM, stats[2 * c][0], stats[2 * c + 1][0])
                lanes = pl.ds(pl.multiple_of(half * SIDE + c * LANES, LANES), LANES)
                ctx_ref[first_row + r, :, lanes] = (ctx[:, c * LANES:(c + 1) * LANES] * inverse).astype(BF16)
            table = jnp.zeros((length, LANES), F32)
            for head in range(FOUR):
                table = jnp.where(lane == head, stats[head][1], table)
            table = jnp.concatenate([table, jnp.zeros((PAD - length, LANES), F32)], axis=0)
            lse_ref[0, r] = table.T[:8]

        scores = [products(r) for r in range(group)]
        stats = []
        for r in range(group):
            stats.append([softmax(r, head, scores[r]) for head in range(FOUR)])
            if r:
                contexts(r - 1, stats[r - 1])
        contexts(group - 1, stats[group - 1])
        for at, todo in events.items():
            def run(todo=todo):
                for event in todo:
                    event()
            pl.when(step == at)(run)

    @pl.when(step == early)
    def _():
        if remote_on:
            gathers[3].last()
            gathers[2].finish()
            gathers[3].finish()
            pltpu.make_async_copy(w1_ref, w1_out, out_sem).start()

    @pl.when(step >= early)
    def _():
        first_row = (step - early) * group
        ctx = ctx_ref[pl.ds(first_row, group)].reshape(tokens, width)
        middle = x_ref[...].reshape(tokens, width).astype(F32) + (nn(ctx, wout_ref[...]) + vec_ref[4:5, :])
        xhat2, inv2 = xhat_of(middle)
        n2 = (xhat2 * vec_ref[5:6, :] + vec_ref[6:7, :]).astype(BF16)
        cot = cot_ref[...].reshape(tokens, width)
        result = middle + vec_ref[7 + chunks:8 + chunks, :]
        back_n2 = jnp.zeros((tokens, width), F32)

        def weight_grads(cols, active, back_up):
            gdn_ref[:, cols] += tn(cot, active)
            gup_ref[:, cols] += tn(n2, back_up)

        held = None

        def products(u):
            cols = slice(u * SIDE, (u + 1) * SIDE)
            bias = vec_ref[7 + u // 2:8 + u // 2, u % 2 * SIDE:(u % 2 + 1) * SIDE]
            return nn(n2, wup_ref[:, cols]) + bias, nt(cot, w3_ref[cols, :])

        ahead = products(0)
        for u in range(hidden // SIDE):
            cols = slice(u * SIDE, (u + 1) * SIDE)
            up, back_act = ahead
            if u + 1 < hidden // SIDE:
                ahead = products(u + 1)
            if held is not None:
                weight_grads(*held)
            square = up * up
            gate = 0.5 + 0.5 * jnp.tanh(up * (C0 + (C0 * C1) * square))
            active = up * gate
            slope = gate + active * (1.0 - gate) * (2.0 * C0 + (6.0 * C0 * C1) * square)
            active = active.astype(BF16)
            back_up = back_act * slope
            sums_ref[7 + u // 2:8 + u // 2, u % 2 * SIDE:(u % 2 + 1) * SIDE] += col_sum(back_up)
            back_up = back_up.astype(BF16)
            result = result + nn(active, w3_ref[cols, :])
            back_n2 = back_n2 + nt(back_up, wup_ref[:, cols])
            held = (cols, active, back_up)
        weight_grads(*held)
        y_ref[...] = result.astype(BF16).reshape(group, length, width)
        cot32 = cot.astype(F32)
        sums_ref[7 + chunks:8 + chunks, :] += col_sum(cot32)
        sums_ref[5:6, :] += col_sum(back_n2 * xhat2)
        sums_ref[6:7, :] += col_sum(back_n2)
        back_middle = cot32 + norm_back(back_n2 * vec_ref[5:6, :], xhat2, inv2)
        back_att = back_middle.astype(BF16)
        bmid_ref[...] = back_att.reshape(group, length, width)
        sums_ref[4:5, :] += col_sum(back_middle)
        gout_ref[...] += tn(ctx, back_att)
        back_ctx = nt(back_att, wout_ref[...]).astype(BF16)
        bctx_ref[...] = back_ctx.reshape(group, length, width)
        pick = (lax.broadcasted_iota(jnp.int32, (16, width), 1) // HEAD_DIM == lax.broadcasted_iota(jnp.int32, (16, width), 0)).astype(BF16)
        for r in range(group):
            rows = slice(r * length, (r + 1) * length)
            product = ctx[rows].astype(F32) * back_ctx[rows].astype(F32)
            product = jnp.concatenate([product, jnp.zeros((PAD - length, width), F32)], axis=0)
            high = product.astype(BF16)
            dots = nt(pick, high) + nt(pick, (product - high.astype(F32)).astype(BF16))
            for half in range(HALVES):
                dot_ref[half, r, 0:FOUR, :] = dots[half * FOUR:(half + 1) * FOUR]
                dot_ref[half, r, FOUR:, :] = jnp.zeros((8 - FOUR, PAD), F32)

    @pl.when(step == pl.num_programs(0) - 1)
    def _():
        g2_out[:, 0:width] = gout_ref[...].astype(BF16)
        g2_out[:, width:] = gup_ref[...].astype(BF16)
        for u in range(chunks):
            g3_out[u * width:(u + 1) * width, :] = gdn_ref[:, u * width:(u + 1) * width].T.astype(BF16)
        if remote_on:
            pltpu.make_async_copy(w1_ref, w1_out, out_sem).wait()
            for g in gathers:
                g.drain()


def whole(shape):
    return pl.BlockSpec(shape, lambda s, *_: (0,) * len(shape), pipeline_mode=pl.Buffered(1))


def phase_a(remote_on, off, x, cot, weights):
    rows, length, width = x.shape
    pairs = rows // GROUP
    if remote_on:
        sizes = [(weights[0].shape[0], 3 * SIDE + LANES), (weights[1].shape[0], width + weights[2].shape[1]), weights[3].shape]
        w2_shape, w3_shape = (CHIPS * sizes[1][0], sizes[1][1]), (CHIPS * sizes[2][0], sizes[2][1])
    else:
        w2_shape, w3_shape = weights[1].shape, weights[2].shape
    hidden = w3_shape[0]
    blk = lambda w, index: pl.BlockSpec((GROUP, length, w), index)
    both = lambda s, *_: (lax.rem(s, pairs), 0, 0)
    late = lambda s, *_: (jnp.maximum(s - HALVES * pairs, 0), 0, 0)
    sided = lambda s, *_: (jnp.minimum(s // pairs, HALVES - 1), jnp.where(s < HALVES * pairs, lax.rem(s, pairs), pairs - 1), 0, 0)
    sds = jax.ShapeDtypeStruct
    out_specs = [blk(width, late), pl.BlockSpec((1, GROUP, length, 3 * SIDE), sided), blk(width, late), blk(width, late),
                 pl.BlockSpec((1, GROUP, 8, PAD), sided), pl.BlockSpec((HALVES, GROUP, 8, PAD), lambda s, *_: (0,) + late(s)),
                 whole(w2_shape), whole(w3_shape), whole((LANES, width))]
    out_shape = [sds(x.shape, BF16), sds((HALVES, rows, length, 3 * SIDE), BF16), sds(x.shape, BF16), sds(x.shape, BF16),
                 sds((HALVES, rows, 8, PAD), F32), sds((HALVES, rows, 8, PAD), F32),
                 sds(w2_shape, BF16), sds(w3_shape, BF16), sds((LANES, width), F32)]
    scratch = [pltpu.VMEM((width, hidden), F32), pltpu.VMEM((width, hidden), F32), pltpu.VMEM((width, width), F32),
               pltpu.VMEM((rows, length, width), BF16), pltpu.VMEM((rows, length, width), BF16), pltpu.VMEM((GROUP, length, PAD), F32),
               pltpu.VMEM((GROUP, FOUR * PAD, SIDE), BF16), pltpu.VMEM((GROUP, FOUR * PAD, SIDE), BF16),
               pltpu.VMEM((GROUP, length, FOUR * PAD), BF16), pltpu.VMEM((LANES, width), F32)]
    params = dict(vmem_limit_bytes=62 << 20)
    if remote_on:
        out_specs.append(pl.BlockSpec(memory_space=pl.ANY))
        out_shape.append(sds((HALVES, 4, 4) + sizes[0], BF16))
        scratch += [pltpu.VMEM((HALVES, 4, 4) + sizes[0], BF16)] + [pltpu.VMEM((4, 4) + s, BF16) for s in sizes[1:]]
        scratch += [DMA((4,)), DMA((4, 9)), DMA]
        params.update(collective_id=0, has_side_effects=True)
    return pl.pallas_call(
        lambda *refs: kernel_a(remote_on, *refs),
        name="phase_a",
        grid_spec=pltpu.PrefetchScalarGridSpec(
            num_scalar_prefetch=0,
            grid=(3 * pairs,),
            in_specs=[whole(off.shape), blk(width, both), blk(width, late)] + [whole(w.shape) for w in weights],
            out_specs=out_specs,
            scratch_shapes=scratch,
        ),
        out_shape=out_shape,
        compiler_params=pltpu.CompilerParams(**params),
    )(off, x, cot, *weights)


def moments_of(grad, first, second):
    new_first = beta_first * first + (1.0 - beta_first) * grad
    new_second = beta_second * second + (1.0 - beta_second) * grad * grad
    direction = new_first / (1.0 - beta_first**STEP) / (jnp.sqrt(new_second / (1.0 - beta_second**STEP)) + adam_eps)
    return new_first, new_second, direction


def lanes_of(v):
    total = None
    for j in range(v.shape[1] // LANES):
        piece = v[:, j * LANES:(j + 1) * LANES]
        total = piece if total is None else total + piece
    return jnp.sum(total, axis=0, keepdims=True)


def kernel_b(remote_on, off_ref, x_ref, qkv_ref, bctx_ref, bmid_ref, lse_ref, dot_ref, w1_ref, sums_a_ref, *refs):
    if remote_on:
        far = refs[0:14]
        xgrad_ref, r1a_ref, r1b_ref, r2_ref, r3_ref, rv_ref, norms_ref = refs[14:21]
        refs = refs[21:]
    else:
        xgrad_ref, g1_out, gv_out = refs[:3]
        refs = refs[3:]
    gqkv_ref, bqkv_ref, n1_ref, bias_ref, qstack_ref, ostack_ref, kstack_ref, p_ref, ds_ref, dsk_ref, sums_ref, vec_ref = refs[:12]
    refs = refs[12:]
    step = pl.program_id(0)
    group, length, width = x_ref.shape
    pairs = pl.num_programs(0) // 3
    early_steps = HALVES * pairs
    tokens = group * length
    if remote_on:
        bufs, finals, refs = refs[:20], refs[20:24], refs[24:]
        g1a_ref, g1b_ref, tile_ref, got_q, late_ref, send, recv, send_q, recv_q = refs[:9]
        held, sem_in = refs[9:23], refs[23]
        loads = [pltpu.make_async_copy(src, dst, sem_in.at[i]) for i, (src, dst) in enumerate(zip(far, held))]
        g2_ref, g3_ref, masters, firsts, seconds = held[0], held[1], held[2:6], held[6:10], held[10:14]
        chip, core = lax.axis_index("fsdp"), lax.axis_index("dp")
        shape4 = lambda ref: ref.reshape(4, 4, ref.shape[0] // CHIPS, ref.shape[1])
        scatters = [Scatter(g, bufs[5 * i:5 * i + 5], finals[i], send.at[i], recv.at[i], chip, core)
                    for i, g in enumerate((g1a_ref, g1b_ref, shape4(g2_ref), shape4(g3_ref)))]
        first, second, mid, down = scatters
        norm = Total(tile_ref, got_q, send_q, recv_q, chip, core)

    def one(s):
        def run():
            s.add0()
            s.start1()
        return run

    def two(s):
        def run():
            s.add1()
            s.start2()
        return run

    def both_one():
        one(mid)()
        one(down)()

    events = {0: [both_one], 4: [two(mid), one(first)], 6: [two(down), two(first)], 7: [mid.add2]} if remote_on else {}

    @pl.when(step == 0)
    def _():
        if remote_on:
            loads[0].start()
            loads[1].start()
            meet(chip, core, FLIPS, (0, 1, 2, 3))
            loads[0].wait()
            mid.start0()
            loads[1].wait()
            down.start0()
            for load in loads[2:]:
                load.start()
        for ref in (gqkv_ref, qstack_ref, ostack_ref, kstack_ref):
            ref[...] = jnp.zeros_like(ref)
        sums_ref[...] = sums_a_ref[...]
        vec_ref[...] = side_of(w1_ref, 0, 3 * SIDE, 3 * SIDE + LANES).astype(F32).T

    @pl.when(step < pairs)
    def _():
        x = x_ref[...].reshape(tokens, width).astype(F32)
        xhat, _ = xhat_of(x)
        n1 = (xhat * vec_ref[0:1, :] + vec_ref[1:2, :]).astype(BF16)
        n1_ref[pl.ds(step * group, group)] = n1.reshape(group, length, width)

    if remote_on:
        @pl.when(step == pairs)
        def _():
            g1a_ref[...] = gqkv_ref[0].astype(BF16).reshape(g1a_ref.shape)
            first.start0()

    @pl.when(step < early_steps)
    def _():
        half = step // pairs
        first_row = lax.rem(step, pairs) * group

        def products(r):
            row = first_row + r
            crop_k = crop_of(*offsets_of(off_ref, row), (length, 1), 0)
            crop_q = crop_of(*offsets_of(off_ref, row), (1, PAD), 1)
            bias_ref[r] = jnp.where(crop_q == crop_k, 0.0, NEG)
            tiles = lambda ref, at: [ref[..., at + c * LANES:at + (c + 1) * LANES] for c in range(2)]
            stack_heads(qstack_ref.at[r], tiles(qkv_ref.at[0, r], 0), PAD)
            stack_heads(kstack_ref.at[r], tiles(qkv_ref.at[0, r], SIDE), length)
            stack_heads(ostack_ref.at[r], tiles(bctx_ref.at[r], 0), PAD)
            return nt(qkv_ref[0, r, :, SIDE:2 * SIDE], qstack_ref[r]), nt(qkv_ref[0, r, :, 2 * SIDE:], ostack_ref[r])

        def softmax(r, head, scores, back_probs):
            lanes = slice(head * PAD, (head + 1) * PAD)
            p = jnp.exp((scores[:, lanes] + bias_ref[r]) - lse_ref[0, r, head:head + 1, :])
            ds = (p * (back_probs[:, lanes] - dot_ref[0, r, head:head + 1, :])).astype(BF16)
            p_ref[r, :, lanes] = p.astype(BF16)
            ds_ref[r, :, lanes] = ds
            dsk_ref[r, head * length:(head + 1) * length, :] = ds

        def back_value(r):
            bqkv_ref[half, first_row + r, :, 2 * SIDE:] = nn(p_ref[r], ostack_ref[r]).astype(BF16)

        def back_key(r):
            bqkv_ref[half, first_row + r, :, SIDE:2 * SIDE] = nn(ds_ref[r], qstack_ref[r]).astype(BF16)

        def back_query(r):
            dq = tn(dsk_ref[r], kstack_ref[r])[:length] * HEAD_DIM ** (-0.5)
            bqkv_ref[half, first_row + r, :, 0:SIDE] = dq.astype(BF16)

        scores = [products(r) for r in range(group)]
        after = (back_value, back_key, back_query)
        for r in range(group):
            for head in range(FOUR):
                softmax(r, head, *scores[r])
                if r and head < len(after):
                    after[head](r - 1)
        for work in after:
            work(group - 1)
        for at, todo in events.items():
            def run(todo=todo):
                for event in todo:
                    event()
            pl.when(step == at)(run)
        n1 = n1_ref[pl.ds(first_row, group)].reshape(tokens, width)
        back = bqkv_ref[half, pl.ds(first_row, group)].reshape(tokens, 3 * SIDE)
        side = pl.ds(pl.multiple_of(half * SIDE, SIDE), SIDE)
        sums_ref[2:3, side] += col_sum(back[:, :SIDE].astype(F32))
        sums_ref[3:4, side] += col_sum(back[:, 2 * SIDE:].astype(F32))
        gqkv_ref[half] += tn(n1, back)

    @pl.when(step == early_steps)
    def _():
        if remote_on:
            g1b_ref[..., 0:3 * SIDE] = gqkv_ref[1].astype(BF16).reshape(g1a_ref.shape)
            g1b_ref[..., 3 * SIDE:] = sums_ref[...].T.astype(BF16).reshape(g1a_ref.shape[:3] + (LANES,))
            second.start0()
            first.add2()
            down.add2()
        else:
            g1_out[...] = gqkv_ref[...].astype(BF16)

    @pl.when(step >= early_steps)
    def _():
        x = x_ref[...].reshape(tokens, width).astype(F32)
        xhat, inv = xhat_of(x)
        back_n1 = None
        for half in range(HALVES):
            back = bqkv_ref[half, pl.ds((step - early_steps) * group, group)].reshape(tokens, 3 * SIDE)
            term = nt(back, side_of(w1_ref, half, 0, 3 * SIDE))
            back_n1 = term if back_n1 is None else back_n1 + term
        sums_ref[0:1, :] += col_sum(back_n1 * xhat)
        sums_ref[1:2, :] += col_sum(back_n1)
        grad = bmid_ref[...].reshape(tokens, width).astype(F32) + norm_back(back_n1 * vec_ref[0:1, :], xhat, inv)
        xgrad_ref[...] = grad.astype(BF16).reshape(group, length, width)

    @pl.when(step == early_steps)
    def _():
        if remote_on:
            one(second)()

    @pl.when(step == pl.num_programs(0) - 1)
    def _():
        if not remote_on:
            gv_out[...] = sums_ref[...].T.astype(BF16)
            return
        wide = masters[2].shape[1]
        mine, deep = mid.rows_mine, down.rows_mine

        def square(i, rows, places):
            sums = [None, None]
            for grad, cols in places:
                master = masters[i][rows, cols]
                _, _, direction = moments_of(grad, firsts[i][rows, cols], seconds[i][rows, cols])
                update = direction + weight_decay * master
                for n, v in enumerate((master, update)):
                    part = lanes_of(v * v)
                    sums[n] = part if sums[n] is None else sums[n] + part
            tile_ref[0, i:i + 1, width:] = sums[0]
            tile_ref[0, 4 + i:5 + i, width:] = sums[1]

        for load in loads[2:]:
            load.wait()
        tile_ref[0, :, 0:width] = jnp.zeros((8, width), F32)
        tile_ref[0, 0:2, 0:width] = sums_ref[0:2, :]
        full = slice(None)
        square(1, mine, [(finals[2][mine, 0:width], full)])
        square(2, mine, [(finals[2][mine, width:width + wide], full)])
        square(3, deep, [(finals[3][deep, :], full)])
        second.add1()
        second.start2()
        for s in (first, mid, down):
            s.finish()
        r1a_ref[...] = finals[0][...]
        r2_ref[...] = finals[2][...]
        r3_ref[...] = finals[3][...]
        second.add2()
        square(0, mine, [(finals[half][mine, part * SIDE:(part + 1) * SIDE], slice(part * width + half * SIDE, part * width + (half + 1) * SIDE))
                         for half in range(HALVES) for part in range(3)])
        norm.start(0)
        second.finish()
        r1b_ref[...] = finals[1][:, 0:3 * SIDE]
        norm.add(0)
        norm.start(1)
        norm.add(1)
        norms_ref[...] = jnp.broadcast_to(jnp.sqrt(jnp.sum(tile_ref[2, :, width:], axis=1, keepdims=True)), (8, LANES))
        late = jnp.concatenate([tile_ref[2, :, 0:width], jnp.zeros((LANES - 8, width), F32)], axis=0)
        late_ref[...] = late.T
        mine_late = late_ref[pl.ds(pl.multiple_of(chip * rv_ref.shape[0], rv_ref.shape[0]), rv_ref.shape[0]), :]
        rv_ref[...] = jnp.where(lax.broadcasted_iota(jnp.int32, (1, LANES), 1) < 2, mine_late, finals[1][:, 3 * SIDE:])


def phase_b(remote_on, off, x, qkv, bctx, bmid, lse, dots, w1, sums_a, grads=(), masters=(), firsts=(), seconds=()):
    rows, length, width = x.shape
    pairs = rows // GROUP
    blk = lambda w, index: pl.BlockSpec((GROUP, length, w), index)
    both = lambda s, *_: (lax.rem(s, pairs), 0, 0)
    late = lambda s, *_: (jnp.maximum(s - HALVES * pairs, 0), 0, 0)
    side = lambda s: jnp.minimum(s // pairs, HALVES - 1)
    pair = lambda s: jnp.where(s < HALVES * pairs, lax.rem(s, pairs), pairs - 1)
    sds = jax.ShapeDtypeStruct
    rowed = pl.BlockSpec((1, GROUP, 8, PAD), lambda s, *_: (side(s), pair(s), 0, 0))
    extra = (*grads, *masters, *firsts, *seconds)
    stack = lambda: pltpu.VMEM((GROUP, FOUR * PAD, SIDE), BF16)
    probs = lambda: pltpu.VMEM((GROUP, length, FOUR * PAD), BF16)
    scratch = [pltpu.VMEM((HALVES, width, 3 * SIDE), F32), pltpu.VMEM((HALVES, rows, length, 3 * SIDE), BF16),
               pltpu.VMEM((rows, length, width), BF16), pltpu.VMEM((GROUP, length, PAD), F32), stack(), stack(),
               pltpu.VMEM((GROUP, FOUR * length, SIDE), BF16), probs(), probs(), pltpu.VMEM((GROUP, FOUR * length, PAD), BF16),
               pltpu.VMEM((LANES, width), F32), pltpu.VMEM((LANES, width), F32)]
    params = dict(vmem_limit_bytes=62 << 20)
    if remote_on:
        thin = width // CHIPS
        sizes = [(thin, 3 * SIDE), (thin, 3 * SIDE + LANES)] + [(g.shape[0] // CHIPS, g.shape[1]) for g in grads]
        outs = [sds(s, F32) for s in [sizes[0]] * HALVES + sizes[2:] + [(thin, LANES), (8, LANES)]]
        for s in sizes:
            scratch += scatter_bufs(*s)
        scratch += [pltpu.VMEM(s, F32) for s in sizes]
        scratch += [pltpu.VMEM((4, 4) + sizes[0], BF16), pltpu.VMEM((4, 4) + sizes[1], BF16), pltpu.VMEM((3, 8, width + LANES), F32),
                    pltpu.VMEM((10, 8, width + LANES), F32), pltpu.VMEM((width, LANES), F32), DMA((4, 8)), DMA((4, 8)), DMA((10,)), DMA((10,))]
        scratch += [pltpu.VMEM(e.shape, e.dtype) for e in extra] + [DMA((len(extra),))]
        params.update(collective_id=1, has_side_effects=True)
    else:
        outs = [sds((HALVES, width, 3 * SIDE), BF16), sds((width, LANES), BF16)]
    return pl.pallas_call(
        lambda *refs: kernel_b(remote_on, *refs),
        name="phase_b",
        grid_spec=pltpu.PrefetchScalarGridSpec(
            num_scalar_prefetch=0,
            grid=(3 * pairs,),
            in_specs=[whole(off.shape), blk(width, both), pl.BlockSpec((1, GROUP, length, 3 * SIDE), lambda s, *_: (side(s), pair(s), 0, 0)),
                      pl.BlockSpec((GROUP, length, SIDE), lambda s, *_: (pair(s), 0, side(s))), blk(width, late),
                      rowed, rowed, whole(w1.shape),
                      whole(sums_a.shape)] + [pl.BlockSpec(memory_space=pl.ANY)] * len(extra),
            out_specs=[blk(width, late)] + [whole(o.shape) for o in outs],
            scratch_shapes=scratch,
        ),
        out_shape=[sds(x.shape, BF16)] + outs,
        compiler_params=pltpu.CompilerParams(**params),
    )(off, x, qkv, bctx, bmid, lse, dots, w1, sums_a, *extra)


def update_kernel(*refs):
    n_in, n_out = 17, 17
    y_ref, xgrad_ref, y_out, xgrad_out = refs[0], refs[1], refs[2 + n_in], refs[3 + n_in]
    ins, outs = refs[2:2 + n_in], refs[4 + n_in:4 + n_in + n_out]
    held_y, held_x, wide_x = refs[4 + n_in + n_out:7 + n_in + n_out]
    kept = refs[7 + n_in + n_out:]
    held_in, held_out, sem_in, sem_out, sems = kept[:n_in], kept[n_in:n_in + n_out], *kept[n_in + n_out:]
    count = y_ref.shape[0]
    load = [pltpu.make_async_copy(src, dst, sem_in.at[i]) for i, (src, dst) in enumerate(zip(ins, held_in))]
    load_x = [pltpu.make_async_copy(xgrad_ref.at[row], held_x.at[row], sems.at[0, row]) for row in range(count)]
    load_y = [pltpu.make_async_copy(y_ref.at[row], held_y.at[row], sems.at[1, row]) for row in range(count)]
    store_x = [pltpu.make_async_copy(wide_x.at[row], xgrad_out.at[row], sems.at[2, row]) for row in range(count)]
    store_y = [pltpu.make_async_copy(held_y.at[row], y_out.at[row], sems.at[3, row]) for row in range(count)]
    for copy in load_x + load + load_y:
        copy.start()
    for row in range(count):
        load_x[row].wait()
        wide_x[row] = held_x[row].astype(F32)
        store_x[row].start()
    for copy in load:
        copy.wait()
    r1a, r1b, r2, r3, norms_ref = held_in[:5]
    masters, firsts, seconds = held_in[5:9], held_in[9:13], held_in[13:17]
    new_m, new_f, new_s, copies, norm_out = held_out[0:4], held_out[4:8], held_out[8:12], held_out[12:16], held_out[16]
    store = [pltpu.make_async_copy(src, dst, sem_out.at[i]) for i, (src, dst) in enumerate(zip(held_out, outs))]
    width, wide = masters[1].shape[1], masters[2].shape[1]
    full = slice(None)
    places = [(3, r3[...], full, True), (2, r2[:, width:width + wide], full, True), (1, r2[:, 0:width], full, True)]
    places += [(0, (r1a, r1b)[half][:, part * SIDE:(part + 1) * SIDE], slice(part * width + half * SIDE, part * width + (half + 1) * SIDE),
                half == HALVES - 1 and part == 2) for half in range(HALVES) for part in range(3)]
    row = lax.broadcasted_iota(jnp.int32, (3, 4), 0)
    col = lax.broadcasted_iota(jnp.int32, (3, 4), 1)
    table = jnp.zeros((3, 4), F32)
    for i, grad, cols, final in places:
        weight_norm, update_norm = norms_ref[i:i + 1, 0:1], norms_ref[4 + i:5 + i, 0:1]
        trust = weight_norm / update_norm
        first, second, direction = moments_of(grad, firsts[i][:, cols], seconds[i][:, cols])
        master = masters[i][:, cols]
        new = master - matrix_rate * trust * (direction + weight_decay * master)
        new_m[i][:, cols] = new
        copies[i][:, cols] = new.astype(BF16)
        new_f[i][:, cols] = first
        new_s[i][:, cols] = second
        if final:
            for block in range(4):
                store[4 * block + i].start()
        for r, value in enumerate((weight_norm, update_norm, trust)):
            table = jnp.where((row == r) & (col == i), value, table)
    norm_out[...] = table
    store[16].start()
    for row in range(count):
        load_y[row].wait()
        store_y[row].start()
    for copy in store_x + store + store_y:
        copy.wait()


def update_all(y, xgrad, reduced, norms, masters, firsts, seconds):
    sds = jax.ShapeDtypeStruct
    place = pl.BlockSpec(memory_space=pl.ANY)
    ins = (*reduced, norms, *masters, *firsts, *seconds)
    outs = [sds(m.shape, F32) for m in masters] * 3 + [sds(m.shape, BF16) for m in masters] + [sds((3, 4), F32)]
    return pl.pallas_call(
        update_kernel,
        name="update",
        out_shape=[sds(y.shape, y.dtype), sds(xgrad.shape, F32)] + outs,
        in_specs=[place] * (2 + len(ins)),
        out_specs=[place] * (2 + len(outs)),
        scratch_shapes=[pltpu.VMEM(y.shape, y.dtype), pltpu.VMEM(xgrad.shape, xgrad.dtype), pltpu.VMEM(xgrad.shape, F32)]
        + [pltpu.VMEM(a.shape, a.dtype) for a in (*ins, *outs)] + [DMA((len(ins),)), DMA((len(outs),)), DMA((4, y.shape[0]))],
        compiler_params=pltpu.CompilerParams(vmem_limit_bytes=62 << 20),
    )(y, xgrad, *ins)


def shards(block_in, offsets, cotangent, w_qkv, w_out, w_up, w_down, vectors, *moments):
    masters = (w_qkv, w_out, w_up, w_down)
    firsts, seconds = moments[:5], moments[5:]
    micro, local_rows, length, width = block_in.shape
    rows = micro * local_rows
    chips = lax.axis_size("fsdp")
    near = chips == CHIPS and lax.axis_size("dp") == 2
    columns = vectors.shape[0] * chips // width
    table = vectors.reshape(-1, columns)
    x = block_in.reshape(rows, length, width)
    cot = cotangent.reshape(rows, length, width)
    off = offsets
    if near:
        y, qkv, bctx, bmid, lse, dots, g2, g3, sums_a, w1 = phase_a(True, off, x, cot, (*masters, table))
        xgrad, *reduced, norms = phase_b(True, off, x, qkv, bctx, bmid, lse, dots, w1, sums_a, (g2, g3), masters, firsts[:4], seconds[:4])
    else:
        table = jnp.pad(table, ((0, 0), (0, LANES - columns)))
        sides = w_qkv.reshape(-1, 3, HALVES, SIDE).transpose(2, 0, 1, 3).reshape(HALVES, -1, 3 * SIDE)
        owns = [jnp.concatenate([sides, jnp.broadcast_to(table, (HALVES,) + table.shape)], axis=2),
                jnp.concatenate([w_out, w_up], axis=1), w_down]
        wholes = [lax.all_gather(o.astype(BF16), "fsdp", axis=o.ndim - 2, tiled=True) for o in owns]
        y, qkv, bctx, bmid, lse, dots, g2, g3, sums_a = phase_a(False, off, x, cot, wholes)
        xgrad, g1, gv = phase_b(False, off, x, qkv, bctx, bmid, lse, dots, wholes[0], sums_a)
        reduced = [lax.psum(lax.psum_scatter(g.astype(F32), "fsdp", scatter_dimension=0, tiled=True), "dp")
                   for g in (g1[0], g1[1], g2, g3, gv)]
        grad1 = jnp.stack(reduced[:2]).reshape(HALVES, -1, 3, SIDE).transpose(1, 2, 0, 3).reshape(w_qkv.shape)
        grads = (grad1, reduced[2][:, :width], reduced[2][:, width:], reduced[3])
        updates = [moments_of(g, m, s)[2] + weight_decay * w for g, m, s, w in zip(grads, firsts, seconds, masters)]
        squares = jnp.stack([jnp.sum(w * w) for w in masters] + [jnp.sum(u * u) for u in updates])
        norms = jnp.broadcast_to(jnp.sqrt(lax.psum(squares, "fsdp"))[:, None], (8, LANES))
    y, xgrad, *news, matrix_norms = update_all(y, xgrad, reduced[:4], norms, masters, firsts[:4], seconds[:4])
    vec_first, vec_second, vec_direction = moments_of(reduced[4][:, :columns].reshape(-1), firsts[4], seconds[4])
    vec_new = vectors - vector_rate * vec_direction
    return (y.reshape(block_in.shape), xgrad.reshape(block_in.shape), *news[0:4], vec_new, *news[4:8], vec_first,
            *news[8:12], vec_second, *news[12:16], vec_new.astype(BF16), matrix_norms)


def solution(mesh):
    batch, matrix, vector = P(None, ("fsdp", "dp"), None, None), P("fsdp", None), P("fsdp")
    params = (matrix,) * 4 + (vector,)
    in_specs = (batch, P(None, ("fsdp", "dp"), None), batch) + params * 3
    out_specs = (batch, batch) + params * 4 + (P(),)
    return jax.shard_map(shards, mesh=mesh, in_specs=in_specs, out_specs=out_specs, check_vma=False)
```

```python
import jax
import jax.numpy as jnp
from jax import lax
from jax.experimental import pallas as pl
from jax.experimental.pallas import tpu as pltpu
from jax.sharding import PartitionSpec as P

HEAD_DIM = 64
STEP = 5
EPS = 1e-05
beta_first = 0.5
beta_second = 0.5
adam_eps = 1e-06
weight_decay = 0.01
matrix_rate = 1.0
vector_rate = 0.1
CHIPS = 16
GROUP = 2
LANES = 128
HALVES = 2
SIDE = 256
FOUR = 4
PAD = 384
NEG = -1e30
C0 = 0.7978845608028654
C1 = 0.044715
F32 = jnp.float32
BF16 = jnp.bfloat16
MESH = pl.DeviceIdType.MESH
DMA = pltpu.SemaphoreType.DMA


def nn(a, b):
    return lax.dot_general(a, b, (((1,), (0,)), ((), ())), preferred_element_type=F32)


def nt(a, b):
    return lax.dot_general(a, b, (((1,), (1,)), ((), ())), preferred_element_type=F32)


def tn(a, b):
    return lax.dot_general(a, b, (((0,), (0,)), ((), ())), preferred_element_type=F32)


def xhat_of(v):
    center = v - jnp.mean(v, axis=-1, keepdims=True)
    spread = jnp.mean(center * center, axis=-1, keepdims=True)
    inv = lax.rsqrt(spread + EPS)
    return center * inv, inv


def norm_back(e, xhat, inv):
    return (e - jnp.mean(e, axis=-1, keepdims=True) - xhat * jnp.mean(e * xhat, axis=-1, keepdims=True)) * inv


def crop_of(first, second, shape, axis):
    t = lax.broadcasted_iota(jnp.int32, shape, axis).astype(F32)
    return (t >= first).astype(jnp.int32) + (t >= second).astype(jnp.int32)


def side_of(ref, half, lo, hi):
    v = ref[half, ..., lo:hi]
    return v.reshape(-1, hi - lo)


def stack_heads(ref, tiles, pitch):
    low = lax.broadcasted_iota(jnp.int32, (1, LANES), 1) < HEAD_DIM
    for head in range(FOUR):
        tile = tiles[head // 2]
        keep = low if head % 2 == 0 else jnp.logical_not(low)
        lanes = slice(head // 2 * LANES, head // 2 * LANES + LANES)
        ref[head * pitch:head * pitch + tile.shape[0], lanes] = jnp.where(keep, tile, jnp.zeros_like(tile))


def offsets_of(ref, row):
    micro, inner = row // ref.shape[2], lax.rem(row, ref.shape[2])
    table = ref[micro].astype(F32)
    at = lax.broadcasted_iota(jnp.int32, (1, ref.shape[2]), 1)
    both = jnp.sum(jnp.where(at == inner, table, 0.0), axis=1, keepdims=True)
    return both[0:1], both[1:2]


def flat_places(rows, columns, at, axis_row, axis_lane, shape):
    row = lax.broadcasted_iota(jnp.int32, shape, axis_row)
    lane = lax.broadcasted_iota(jnp.int32, shape, axis_lane)
    return [row * columns + c == lane + at * LANES for c in range(columns)]


def table_of(flat, rows, columns):
    masks = [flat_places(rows, columns, at, 0, 1, (rows, LANES)) for at in range(flat.shape[0])]
    lane = lax.broadcasted_iota(jnp.int32, (1, LANES), 1)
    table = jnp.zeros((rows, LANES), F32)
    for c in range(columns):
        found = jnp.zeros((rows, LANES), F32)
        for at in range(flat.shape[0]):
            found = jnp.where(masks[at][c], flat[at:at + 1, :], found)
        table = jnp.where(lane == c, jnp.sum(found, axis=1, keepdims=True), table)
    return table


def flat_of(table, columns, count):
    rows = table.shape[0]
    out = []
    for at in range(count):
        masks = flat_places(rows, columns, at, 0, 1, (rows, LANES))
        found = jnp.zeros((rows, LANES), F32)
        for c in range(columns):
            found = jnp.where(masks[c], table[:, c:c + 1], found)
        out.append(jnp.sum(found, axis=0, keepdims=True))
    return out


def col_sum(v):
    return jnp.sum(v, axis=0, keepdims=True)


def partner(chip, flip):
    out = chip
    for bit in (1, 2, 4, 8):
        if flip & bit:
            out = out + bit - 2 * bit * lax.rem(chip // bit, 2)
    return out


def meet(chip, core, flips, others):
    barrier = pltpu.get_barrier_semaphore()
    for flip in flips:
        pl.semaphore_signal(barrier, inc=1, device_id=(partner(chip, flip), core), device_id_type=MESH)
    for flip in others:
        pl.semaphore_signal(barrier, inc=1, device_id=(partner(chip, flip), 1 - core), device_id_type=MESH)
    pl.semaphore_wait(barrier, len(flips) + len(others))


def remote(src, dst, send_sem, recv_sem, chip, core):
    return pltpu.make_async_remote_copy(src_ref=src, dst_ref=dst, send_sem=send_sem, recv_sem=recv_sem,
                                        device_id=(chip, core), device_id_type=MESH)


def wait_bytes(ref, sem):
    pltpu.make_async_copy(ref, ref, sem).wait()


class Gather:
    def __init__(self, whole, cols, send, recv, chip, core, quick, calm):
        self.whole, self.cols, self.chip, self.core, self.send, self.recv, self.quick, self.calm = whole, cols, chip, core, send, recv, quick, calm
        self.half = whole.shape[-2] // 2
        start = pl.multiple_of(core * self.half, self.half)
        self.rows, self.all = pl.ds(start, self.half), pl.ds(0, cols)
        self.mine = (self.rows, self.all)
        if self.half >= 32:
            q = self.half // 2
            self.cuts = [(pl.ds(start + i * q, q), self.all) for i in range(2)]
        else:
            q = cols // 256 * 128
            self.cuts = [(self.rows, pl.ds(0, q)), (self.rows, pl.ds(q, cols - q))]

    def column(self, flip, cut):
        return self.whole.at[:, lax.rem(partner(self.chip, flip), 4), cut[0], cut[1]]

    def shard(self, flip):
        at = partner(self.chip, flip)
        return self.whole.at[at // 4, lax.rem(at, 4), self.rows, self.all]

    def push(self, ref, sem, to):
        remote(ref, ref, self.send, self.recv.at[sem], partner(self.chip, to), self.core).start()

    def to_twin(self, flip):
        if self.calm and flip != 3:
            return
        ref = self.whole.at[:, :, self.rows, self.all] if self.calm else self.column(flip, self.mine)
        remote(ref, ref, self.send, self.recv.at[8], self.chip, 1 - self.core).start()

    def start(self):
        own = self.shard(0)
        for flip in (4, 8, 12):
            self.push(own, flip // 4, flip)
        if self.quick:
            self.push(own, 4, 1)
            self.push(own, 5, 2)

    def spread(self):
        for flip in (4, 8, 12):
            ref = self.shard(flip)
            wait_bytes(ref, self.recv.at[flip // 4])
            if self.quick:
                self.push(ref, 4, 1)
                self.push(ref, 5, 2)
        ref = self.column(0, self.mine)
        if not self.quick:
            self.push(ref, 4, 1)
            self.push(ref, 5, 2)
        self.to_twin(0)

    def cross(self):
        for sem, via, to, cut in ((4, 1, 2, 0), (5, 2, 1, 1)):
            wait_bytes(self.column(via, self.mine), self.recv.at[sem])
            self.push(self.column(via, self.cuts[cut]), 6 + cut, to)
            self.to_twin(via)

    def last(self):
        for cut in range(2):
            wait_bytes(self.column(3, self.cuts[cut]), self.recv.at[6 + cut])
        self.to_twin(3)

    def finish(self):
        wait_bytes(self.whole.at[:, :, pl.ds(0, self.half), self.all], self.recv.at[8])

    def drain(self):
        rows = pl.ds(0, self.half)
        for zs, yxs in (((0, 4), (0, 4)), ((0, 3), (0, 4)), ((0, 1), (0, 3))):
            wait_bytes(self.whole.at[pl.ds(*zs), pl.ds(*yxs), rows, self.all], self.send)


class Scatter:
    def __init__(self, grad, bufs, out, send, recv, chip, core):
        self.grad, self.out, self.send, self.recv, self.chip, self.core = grad, out, send, recv, chip, core
        self.got0, self.part, self.got1, self.col, self.got2 = bufs
        self.half = grad.shape[2] // 2
        self.start_mine = pl.multiple_of(core * self.half, self.half)
        self.rows_mine = pl.ds(self.start_mine, self.half)
        self.z, self.yx = chip // 4, lax.rem(chip, 4)

    def copy0(self):
        theirs = pl.ds(pl.multiple_of((1 - self.core) * self.half, self.half), self.half)
        return remote(self.grad.at[:, :, theirs, :], self.got0, self.send.at[0], self.recv.at[0], self.chip, 1 - self.core)

    def start0(self):
        self.copy0().start()

    def add0(self):
        self.copy0().wait()

        def one(i, _):
            z, yx = i // 4, lax.rem(i, 4)
            mine = self.grad[z, yx, pl.ds(self.start_mine, self.half), :].astype(F32)
            self.part[z, yx] = (mine + self.got0[z, yx].astype(F32)).astype(BF16)
            return 0

        lax.fori_loop(0, CHIPS, one, 0)

    def copy1(self, flip):
        to = partner(self.chip, flip)
        return remote(self.part.at[:, lax.rem(to, 4)], self.got1.at[flip - 1], self.send.at[flip], self.recv.at[flip], to, self.core)

    def start1(self):
        for flip in (3, 1, 2):
            self.copy1(flip).start()

    def add1(self):
        for flip in (1, 2, 3):
            self.copy1(flip).wait()

        def one(z, _):
            total = self.part[z, self.yx].astype(F32)
            for k in range(3):
                total = total + self.got1[k, z].astype(F32)
            self.col[z] = total.astype(BF16)
            return 0

        lax.fori_loop(0, 4, one, 0)

    def copy2(self, flip):
        to = partner(self.chip, 4 * flip)
        return remote(self.col.at[to // 4], self.got2.at[flip - 1], self.send.at[3 + flip], self.recv.at[3 + flip], to, self.core)

    def start2(self):
        for flip in (1, 2, 3):
            self.copy2(flip).start()

    def copy3(self):
        ref = self.out.at[pl.ds(self.start_mine, self.half), :]
        return remote(ref, ref, self.send.at[7], self.recv.at[7], self.chip, 1 - self.core)

    def add2(self):
        for flip in (1, 2, 3):
            self.copy2(flip).wait()
        total = self.col[self.z].astype(F32)
        for k in range(3):
            total = total + self.got2[k].astype(F32)
        self.out[pl.ds(self.start_mine, self.half), :] = total
        self.copy3().start()

    def finish(self):
        self.copy3().wait()


def scatter_bufs(rows, cols):
    half = rows // 2
    return [pltpu.VMEM((4, 4, half, cols), BF16), pltpu.VMEM((4, 4, half, cols), BF16), pltpu.VMEM((3, 4, half, cols), BF16),
            pltpu.VMEM((4, half, cols), BF16), pltpu.VMEM((3, half, cols), BF16)]


class Total:
    def __init__(self, tile, got, send, recv, chip, core):
        self.tile, self.got, self.send, self.recv, self.chip, self.core = tile, got, send, recv, chip, core

    def copies(self, turn):
        if turn == 0:
            peers = [(flip, other) for flip in range(4) for other in range(2) if flip or other]
        else:
            peers = [(flip, 0) for flip in (4, 8, 12)]
        out = []
        for n, (flip, other) in enumerate(peers):
            at = 7 * turn + n
            out.append(remote(self.tile.at[turn], self.got.at[at], self.send.at[at], self.recv.at[at], partner(self.chip, flip),
                              1 - self.core if other else self.core))
        return out

    def start(self, turn):
        for copy in self.copies(turn):
            copy.start()

    def add(self, turn):
        copies = self.copies(turn)
        for copy in copies:
            copy.wait()
        total = self.tile[turn]
        for n in range(len(copies)):
            total = total + self.got[7 * turn + n]
        self.tile[turn + 1] = total


FLIPS = (1, 2, 3, 4, 8, 12)


def kernel_a(remote_on, off_ref, x_ref, cot_ref, *refs):
    if remote_on:
        masters, refs = refs[:5], refs[5:]
    else:
        w_in, refs = refs[:3], refs[3:]
    y_ref, qkv_ref, bctx_ref, bmid_ref, lse_ref, dot_ref, g2_out, g3_out, sums_ref = refs[:9]
    refs = refs[9:]
    if remote_on:
        w1_out, refs = refs[0], refs[1:]
    gup_ref, gdn_ref, gout_ref, ctx_ref, n1_ref, bias_ref, kstack_ref, vstack_ref, p_ref, vec_ref = refs[:10]
    refs = refs[10:]
    step = pl.program_id(0)
    group, length, width = x_ref.shape
    pairs = pl.num_programs(0) // 3
    early = HALVES * pairs
    tokens = group * length
    hidden = gup_ref.shape[1]
    chunks = hidden // width
    if remote_on:
        w1_ref, whole2, whole3, send, recv, out_sem = refs
        chip, core = lax.axis_index("fsdp"), lax.axis_index("dp")
        wide = 3 * SIDE
        gathers = [Gather(w, cols, send.at[i], recv.at[i], chip, core, i == 0, i in (1, 2)) for i, (w, cols) in enumerate((
            (w1_ref.at[0], wide + LANES), (w1_ref.at[1], wide), (whole2, width + hidden), (whole3, width)))]
        w2_ref, w3_ref = [w.reshape(CHIPS * w.shape[2], w.shape[3]) for w in (whole2, whole3)]
    else:
        w1_ref, w2_ref, w3_ref = w_in
    wout_ref, wup_ref = w2_ref.at[:, 0:width], w2_ref.at[:, width:width + hidden]

    @pl.when(step == 0)
    def _():
        if remote_on:
            rows = [g.rows for g in gathers]
            z, yx = chip // 4, lax.rem(chip, 4)

            def cast_side(half):
                for part in range(3):
                    at = part * width + half * SIDE
                    w1_ref[half, z, yx, rows[0], part * SIDE:(part + 1) * SIDE] = masters[0][rows[0], at:at + SIDE].astype(BF16)

            cast_side(0)
            thin = w1_ref.shape[3]
            table = table_of(masters[4][...], thin, masters[4].shape[0] * LANES // thin)
            w1_ref[0, z, yx, rows[0], wide:] = jnp.where(core == 0, table[:thin // 2], table[thin // 2:]).astype(BF16)
            meet(chip, core, FLIPS, (0,))
            gathers[0].start()
            cast_side(1)
            whole2[z, yx, rows[2], 0:width] = masters[1][rows[2], :].astype(BF16)
            whole2[z, yx, rows[2], width:] = masters[2][rows[2], :].astype(BF16)
            whole3[z, yx, rows[3], :] = masters[3][rows[3], :].astype(BF16)
        gup_ref[...] = jnp.zeros_like(gup_ref)
        gdn_ref[...] = jnp.zeros_like(gdn_ref)
        gout_ref[...] = jnp.zeros_like(gout_ref)
        sums_ref[...] = jnp.zeros_like(sums_ref)
        kstack_ref[...] = jnp.zeros_like(kstack_ref)
        vstack_ref[...] = jnp.zeros_like(vstack_ref)
        if remote_on:
            gathers[0].spread()
            for g in gathers[1:]:
                g.start()
            gathers[0].cross()
            gathers[0].last()
            gathers[1].spread()
            gathers[0].finish()
        vec_ref[...] = side_of(w1_ref, 0, 3 * SIDE, 3 * SIDE + LANES).astype(F32).T

    events = {}
    if remote_on:
        events = {0: [gathers[1].cross, gathers[2].spread], 1: [gathers[1].last], 2: [gathers[3].spread], 3: [gathers[2].cross], 5: [gathers[3].cross, gathers[2].last], 6: [gathers[3].last]}

    @pl.when(step < pairs)
    def _():
        x = x_ref[...].reshape(tokens, width).astype(F32)
        xhat, _ = xhat_of(x)
        n1 = (xhat * vec_ref[0:1, :] + vec_ref[1:2, :]).astype(BF16)
        n1_ref[pl.ds(step * group, group)] = n1.reshape(group, length, width)

    if remote_on:
        @pl.when(step == pairs)
        def _():
            gathers[1].finish()

    @pl.when(step < early)
    def _():
        half = step // pairs
        first_row = lax.rem(step, pairs) * group
        side = pl.ds(pl.multiple_of(half * SIDE, SIDE), SIDE)
        n1 = n1_ref[pl.ds(first_row, group)].reshape(tokens, width)
        q = ((nn(n1, side_of(w1_ref, half, 0, SIDE)) + vec_ref[2:3, side]) * HEAD_DIM ** (-0.5)).astype(BF16)
        k = nn(n1, side_of(w1_ref, half, SIDE, 2 * SIDE)).astype(BF16)
        v = (nn(n1, side_of(w1_ref, half, 2 * SIDE, 3 * SIDE)) + vec_ref[3:4, side]).astype(BF16)
        for part, value in enumerate((q, k, v)):
            qkv_ref[0, :, :, part * SIDE:(part + 1) * SIDE] = value.reshape(group, length, SIDE)
        lane = lax.broadcasted_iota(jnp.int32, (1, LANES), 1)

        def products(r):
            row = first_row + r
            crop_q = crop_of(*offsets_of(off_ref, row), (length, 1), 0)
            crop_k = crop_of(*offsets_of(off_ref, row), (1, PAD), 1)
            inside = lax.broadcasted_iota(jnp.int32, (1, PAD), 1) < length
            bias_ref[r] = jnp.where((crop_q == crop_k) & inside, 0.0, NEG)
            kr, vr = [[t[r * length:(r + 1) * length, c * LANES:(c + 1) * LANES] for c in range(2)] for t in (k, v)]
            stack_heads(kstack_ref.at[r], kr, PAD)
            stack_heads(vstack_ref.at[r], vr, PAD)
            return nt(q[r * length:(r + 1) * length], kstack_ref[r])

        def softmax(r, head, scores):
            lanes = slice(head * PAD, (head + 1) * PAD)
            s = scores[:, lanes] + bias_ref[r]
            peak = jnp.max(s, axis=-1, keepdims=True)
            e = jnp.exp(s - peak)
            p_ref[r, :, lanes] = e.astype(BF16)
            total = jnp.sum(e, axis=-1, keepdims=True)
            return 1.0 / total, peak + jnp.log(total)

        def contexts(r, stats):
            ctx = nn(p_ref[r], vstack_ref[r])
            for c in range(2):
                inverse = jnp.where(lane < HEAD_DIM, stats[2 * c][0], stats[2 * c + 1][0])
                lanes = pl.ds(pl.multiple_of(half * SIDE + c * LANES, LANES), LANES)
                ctx_ref[first_row + r, :, lanes] = (ctx[:, c * LANES:(c + 1) * LANES] * inverse).astype(BF16)
            table = jnp.zeros((length, LANES), F32)
            for head in range(FOUR):
                table = jnp.where(lane == head, stats[head][1], table)
            table = jnp.concatenate([table, jnp.zeros((PAD - length, LANES), F32)], axis=0)
            lse_ref[0, r] = table.T[:8]

        scores = [products(r) for r in range(group)]
        stats = []
        for r in range(group):
            stats.append([softmax(r, head, scores[r]) for head in range(FOUR)])
            if r:
                contexts(r - 1, stats[r - 1])
        contexts(group - 1, stats[group - 1])
        for at, todo in events.items():
            def run(todo=todo):
                for event in todo:
                    event()
            pl.when(step == at)(run)

    @pl.when(step == early)
    def _():
        if remote_on:
            gathers[2].finish()
            gathers[3].finish()
            pltpu.make_async_copy(w1_ref, w1_out, out_sem).start()

    @pl.when(step >= early)
    def _():
        first_row = (step - early) * group
        ctx = ctx_ref[pl.ds(first_row, group)].reshape(tokens, width)
        middle = x_ref[...].reshape(tokens, width).astype(F32) + (nn(ctx, wout_ref[...]) + vec_ref[4:5, :])
        xhat2, inv2 = xhat_of(middle)
        n2 = (xhat2 * vec_ref[5:6, :] + vec_ref[6:7, :]).astype(BF16)
        cot = cot_ref[...].reshape(tokens, width)
        result = middle + vec_ref[7 + chunks:8 + chunks, :]
        back_n2 = jnp.zeros((tokens, width), F32)

        def weight_grads(cols, active, back_up):
            gdn_ref[:, cols] += tn(cot, active)
            gup_ref[:, cols] += tn(n2, back_up)

        held = None

        def products(u):
            cols = slice(u * SIDE, (u + 1) * SIDE)
            bias = vec_ref[7 + u // 2:8 + u // 2, u % 2 * SIDE:(u % 2 + 1) * SIDE]
            return nn(n2, wup_ref[:, cols]) + bias, nt(cot, w3_ref[cols, :])

        ahead = products(0)
        for u in range(hidden // SIDE):
            cols = slice(u * SIDE, (u + 1) * SIDE)
            up, back_act = ahead
            if u + 1 < hidden // SIDE:
                ahead = products(u + 1)
            if held is not None:
                weight_grads(*held)
            square = up * up
            gate = 0.5 + 0.5 * jnp.tanh(up * (C0 + (C0 * C1) * square))
            active = up * gate
            slope = gate + active * (1.0 - gate) * (2.0 * C0 + (6.0 * C0 * C1) * square)
            active = active.astype(BF16)
            back_up = back_act * slope
            sums_ref[7 + u // 2:8 + u // 2, u % 2 * SIDE:(u % 2 + 1) * SIDE] += col_sum(back_up)
            back_up = back_up.astype(BF16)
            result = result + nn(active, w3_ref[cols, :])
            back_n2 = back_n2 + nt(back_up, wup_ref[:, cols])
            held = (cols, active, back_up)
        weight_grads(*held)
        y_ref[...] = result.astype(BF16).reshape(group, length, width)
        cot32 = cot.astype(F32)
        sums_ref[7 + chunks:8 + chunks, :] += col_sum(cot32)
        sums_ref[5:6, :] += col_sum(back_n2 * xhat2)
        sums_ref[6:7, :] += col_sum(back_n2)
        back_middle = cot32 + norm_back(back_n2 * vec_ref[5:6, :], xhat2, inv2)
        back_att = back_middle.astype(BF16)
        bmid_ref[...] = back_att.reshape(group, length, width)
        sums_ref[4:5, :] += col_sum(back_middle)
        gout_ref[...] += tn(ctx, back_att)
        back_ctx = nt(back_att, wout_ref[...]).astype(BF16)
        bctx_ref[...] = back_ctx.reshape(group, length, width)
        pick = (lax.broadcasted_iota(jnp.int32, (16, width), 1) // HEAD_DIM == lax.broadcasted_iota(jnp.int32, (16, width), 0)).astype(BF16)
        for r in range(group):
            rows = slice(r * length, (r + 1) * length)
            product = ctx[rows].astype(F32) * back_ctx[rows].astype(F32)
            product = jnp.concatenate([product, jnp.zeros((PAD - length, width), F32)], axis=0)
            high = product.astype(BF16)
            dots = nt(pick, high) + nt(pick, (product - high.astype(F32)).astype(BF16))
            for half in range(HALVES):
                dot_ref[half, r, 0:FOUR, :] = dots[half * FOUR:(half + 1) * FOUR]
                dot_ref[half, r, FOUR:, :] = jnp.zeros((8 - FOUR, PAD), F32)

    @pl.when(step == pl.num_programs(0) - 1)
    def _():
        g2_out[:, 0:width] = gout_ref[...].astype(BF16)
        g2_out[:, width:] = gup_ref[...].astype(BF16)
        for u in range(chunks):
            g3_out[u * width:(u + 1) * width, :] = gdn_ref[:, u * width:(u + 1) * width].T.astype(BF16)
        if remote_on:
            pltpu.make_async_copy(w1_ref, w1_out, out_sem).wait()
            for g in gathers:
                g.drain()


def whole(shape):
    return pl.BlockSpec(shape, lambda s, *_: (0,) * len(shape), pipeline_mode=pl.Buffered(1))


def phase_a(remote_on, off, x, cot, weights):
    rows, length, width = x.shape
    pairs = rows // GROUP
    if remote_on:
        sizes = [(weights[0].shape[0], 3 * SIDE + LANES), (weights[1].shape[0], width + weights[2].shape[1]), weights[3].shape]
        w2_shape, w3_shape = (CHIPS * sizes[1][0], sizes[1][1]), (CHIPS * sizes[2][0], sizes[2][1])
    else:
        w2_shape, w3_shape = weights[1].shape, weights[2].shape
    hidden = w3_shape[0]
    blk = lambda w, index: pl.BlockSpec((GROUP, length, w), index)
    both = lambda s, *_: (lax.rem(s, pairs), 0, 0)
    late = lambda s, *_: (jnp.maximum(s - HALVES * pairs, 0), 0, 0)
    sided = lambda s, *_: (jnp.minimum(s // pairs, HALVES - 1), jnp.where(s < HALVES * pairs, lax.rem(s, pairs), pairs - 1), 0, 0)
    sds = jax.ShapeDtypeStruct
    out_specs = [blk(width, late), pl.BlockSpec((1, GROUP, length, 3 * SIDE), sided), blk(width, late), blk(width, late),
                 pl.BlockSpec((1, GROUP, 8, PAD), sided), pl.BlockSpec((HALVES, GROUP, 8, PAD), lambda s, *_: (0,) + late(s)),
                 whole(w2_shape), whole(w3_shape), whole((LANES, width))]
    out_shape = [sds(x.shape, BF16), sds((HALVES, rows, length, 3 * SIDE), BF16), sds(x.shape, BF16), sds(x.shape, BF16),
                 sds((HALVES, rows, 8, PAD), F32), sds((HALVES, rows, 8, PAD), F32),
                 sds(w2_shape, BF16), sds(w3_shape, BF16), sds((LANES, width), F32)]
    scratch = [pltpu.VMEM((width, hidden), F32), pltpu.VMEM((width, hidden), F32), pltpu.VMEM((width, width), F32),
               pltpu.VMEM((rows, length, width), BF16), pltpu.VMEM((rows, length, width), BF16), pltpu.VMEM((GROUP, length, PAD), F32),
               pltpu.VMEM((GROUP, FOUR * PAD, SIDE), BF16), pltpu.VMEM((GROUP, FOUR * PAD, SIDE), BF16),
               pltpu.VMEM((GROUP, length, FOUR * PAD), BF16), pltpu.VMEM((LANES, width), F32)]
    params = dict(vmem_limit_bytes=62 << 20)
    if remote_on:
        out_specs.append(pl.BlockSpec(memory_space=pl.ANY))
        out_shape.append(sds((HALVES, 4, 4) + sizes[0], BF16))
        scratch += [pltpu.VMEM((HALVES, 4, 4) + sizes[0], BF16)] + [pltpu.VMEM((4, 4) + s, BF16) for s in sizes[1:]]
        scratch += [DMA((4,)), DMA((4, 9)), DMA]
        params.update(collective_id=0, has_side_effects=True)
    return pl.pallas_call(
        lambda *refs: kernel_a(remote_on, *refs),
        name="phase_a",
        grid_spec=pltpu.PrefetchScalarGridSpec(
            num_scalar_prefetch=0,
            grid=(3 * pairs,),
            in_specs=[whole(off.shape), blk(width, both), blk(width, late)] + [whole(w.shape) for w in weights],
            out_specs=out_specs,
            scratch_shapes=scratch,
        ),
        out_shape=out_shape,
        compiler_params=pltpu.CompilerParams(**params),
    )(off, x, cot, *weights)


def moments_of(grad, first, second):
    new_first = beta_first * first + (1.0 - beta_first) * grad
    new_second = beta_second * second + (1.0 - beta_second) * grad * grad
    direction = new_first / (1.0 - beta_first**STEP) / (jnp.sqrt(new_second / (1.0 - beta_second**STEP)) + adam_eps)
    return new_first, new_second, direction


def lanes_of(v):
    total = None
    for j in range(v.shape[1] // LANES):
        piece = v[:, j * LANES:(j + 1) * LANES]
        total = piece if total is None else total + piece
    return jnp.sum(total, axis=0, keepdims=True)


def kernel_b(remote_on, off_ref, x_ref, qkv_ref, bctx_ref, bmid_ref, lse_ref, dot_ref, w1_ref, sums_a_ref, *refs):
    if remote_on:
        far = refs[0:14]
        xgrad_ref, r1a_ref, r1b_ref, r2_ref, r3_ref, rv_ref, norms_ref = refs[14:21]
        refs = refs[21:]
    else:
        xgrad_ref, g1_out, gv_out = refs[:3]
        refs = refs[3:]
    gqkv_ref, bqkv_ref, n1_ref, bias_ref, qstack_ref, ostack_ref, kstack_ref, p_ref, ds_ref, dsk_ref, sums_ref, vec_ref = refs[:12]
    refs = refs[12:]
    step = pl.program_id(0)
    group, length, width = x_ref.shape
    pairs = pl.num_programs(0) // 3
    early_steps = HALVES * pairs
    tokens = group * length
    if remote_on:
        bufs, finals, refs = refs[:20], refs[20:24], refs[24:]
        g1a_ref, g1b_ref, tile_ref, got_q, late_ref, send, recv, send_q, recv_q = refs[:9]
        held, sem_in = refs[9:23], refs[23]
        loads = [pltpu.make_async_copy(src, dst, sem_in.at[i]) for i, (src, dst) in enumerate(zip(far, held))]
        g2_ref, g3_ref, masters, firsts, seconds = held[0], held[1], held[2:6], held[6:10], held[10:14]
        chip, core = lax.axis_index("fsdp"), lax.axis_index("dp")
        shape4 = lambda ref: ref.reshape(4, 4, ref.shape[0] // CHIPS, ref.shape[1])
        scatters = [Scatter(g, bufs[5 * i:5 * i + 5], finals[i], send.at[i], recv.at[i], chip, core)
                    for i, g in enumerate((g1a_ref, g1b_ref, shape4(g2_ref), shape4(g3_ref)))]
        first, second, mid, down = scatters
        norm = Total(tile_ref, got_q, send_q, recv_q, chip, core)

    def one(s):
        def run():
            s.add0()
            s.start1()
        return run

    def two(s):
        def run():
            s.add1()
            s.start2()
        return run

    def both_one():
        one(mid)()
        one(down)()

    events = {0: [both_one], 4: [two(mid), one(first)], 5: [two(down)], 6: [two(first)], 7: [mid.add2]} if remote_on else {}

    @pl.when(step == 0)
    def _():
        if remote_on:
            loads[0].start()
            loads[1].start()
            meet(chip, core, FLIPS, (0, 1, 2, 3))
            loads[0].wait()
            mid.start0()
            loads[1].wait()
            down.start0()
            for load in loads[2:]:
                load.start()
        for ref in (gqkv_ref, qstack_ref, ostack_ref, kstack_ref):
            ref[...] = jnp.zeros_like(ref)
        sums_ref[...] = sums_a_ref[...]
        vec_ref[...] = side_of(w1_ref, 0, 3 * SIDE, 3 * SIDE + LANES).astype(F32).T

    @pl.when(step < pairs)
    def _():
        x = x_ref[...].reshape(tokens, width).astype(F32)
        xhat, _ = xhat_of(x)
        n1 = (xhat * vec_ref[0:1, :] + vec_ref[1:2, :]).astype(BF16)
        n1_ref[pl.ds(step * group, group)] = n1.reshape(group, length, width)

    if remote_on:
        @pl.when(step == pairs)
        def _():
            g1a_ref[...] = gqkv_ref[0].astype(BF16).reshape(g1a_ref.shape)
            first.start0()

    @pl.when(step < early_steps)
    def _():
        half = step // pairs
        first_row = lax.rem(step, pairs) * group

        def products(r):
            row = first_row + r
            crop_k = crop_of(*offsets_of(off_ref, row), (length, 1), 0)
            crop_q = crop_of(*offsets_of(off_ref, row), (1, PAD), 1)
            bias_ref[r] = jnp.where(crop_q == crop_k, 0.0, NEG)
            tiles = lambda ref, at: [ref[..., at + c * LANES:at + (c + 1) * LANES] for c in range(2)]
            stack_heads(qstack_ref.at[r], tiles(qkv_ref.at[0, r], 0), PAD)
            stack_heads(kstack_ref.at[r], tiles(qkv_ref.at[0, r], SIDE), length)
            stack_heads(ostack_ref.at[r], tiles(bctx_ref.at[r], 0), PAD)
            return nt(qkv_ref[0, r, :, SIDE:2 * SIDE], qstack_ref[r]), nt(qkv_ref[0, r, :, 2 * SIDE:], ostack_ref[r])

        def softmax(r, head, scores, back_probs):
            lanes = slice(head * PAD, (head + 1) * PAD)
            p = jnp.exp((scores[:, lanes] + bias_ref[r]) - lse_ref[0, r, head:head + 1, :])
            ds = (p * (back_probs[:, lanes] - dot_ref[0, r, head:head + 1, :])).astype(BF16)
            p_ref[r, :, lanes] = p.astype(BF16)
            ds_ref[r, :, lanes] = ds
            dsk_ref[r, head * length:(head + 1) * length, :] = ds

        def back_value(r):
            bqkv_ref[half, first_row + r, :, 2 * SIDE:] = nn(p_ref[r], ostack_ref[r]).astype(BF16)

        def back_key(r):
            bqkv_ref[half, first_row + r, :, SIDE:2 * SIDE] = nn(ds_ref[r], qstack_ref[r]).astype(BF16)

        def back_query(r):
            dq = tn(dsk_ref[r], kstack_ref[r])[:length] * HEAD_DIM ** (-0.5)
            bqkv_ref[half, first_row + r, :, 0:SIDE] = dq.astype(BF16)

        scores = [products(r) for r in range(group)]
        after = (back_value, back_key, back_query)
        for r in range(group):
            for head in range(FOUR):
                softmax(r, head, *scores[r])
                if r and head < len(after):
                    after[head](r - 1)
        for work in after:
            work(group - 1)
        for at, todo in events.items():
            def run(todo=todo):
                for event in todo:
                    event()
            pl.when(step == at)(run)
        n1 = n1_ref[pl.ds(first_row, group)].reshape(tokens, width)
        back = bqkv_ref[half, pl.ds(first_row, group)].reshape(tokens, 3 * SIDE)
        side = pl.ds(pl.multiple_of(half * SIDE, SIDE), SIDE)
        sums_ref[2:3, side] += col_sum(back[:, :SIDE].astype(F32))
        sums_ref[3:4, side] += col_sum(back[:, 2 * SIDE:].astype(F32))
        gqkv_ref[half] += tn(n1, back)

    @pl.when(step == early_steps)
    def _():
        if remote_on:
            g1b_ref[..., 0:3 * SIDE] = gqkv_ref[1].astype(BF16).reshape(g1a_ref.shape)
            g1b_ref[..., 3 * SIDE:] = sums_ref[...].T.astype(BF16).reshape(g1a_ref.shape[:3] + (LANES,))
            second.start0()
            first.add2()
            down.add2()
        else:
            g1_out[...] = gqkv_ref[...].astype(BF16)

    @pl.when(step >= early_steps)
    def _():
        x = x_ref[...].reshape(tokens, width).astype(F32)
        xhat, inv = xhat_of(x)
        back_n1 = None
        for half in range(HALVES):
            back = bqkv_ref[half, pl.ds((step - early_steps) * group, group)].reshape(tokens, 3 * SIDE)
            term = nt(back, side_of(w1_ref, half, 0, 3 * SIDE))
            back_n1 = term if back_n1 is None else back_n1 + term
        sums_ref[0:1, :] += col_sum(back_n1 * xhat)
        sums_ref[1:2, :] += col_sum(back_n1)
        grad = bmid_ref[...].reshape(tokens, width).astype(F32) + norm_back(back_n1 * vec_ref[0:1, :], xhat, inv)
        xgrad_ref[...] = grad.astype(BF16).reshape(group, length, width)

    @pl.when(step == early_steps)
    def _():
        if remote_on:
            one(second)()

    @pl.when(step == pl.num_programs(0) - 1)
    def _():
        if not remote_on:
            gv_out[...] = sums_ref[...].T.astype(BF16)
            return
        wide = masters[2].shape[1]
        mine, deep = mid.rows_mine, down.rows_mine

        def square(i, rows, places):
            sums = [None, None]
            for grad, cols in places:
                master = masters[i][rows, cols]
                _, _, direction = moments_of(grad, firsts[i][rows, cols], seconds[i][rows, cols])
                update = direction + weight_decay * master
                for n, v in enumerate((master, update)):
                    part = lanes_of(v * v)
                    sums[n] = part if sums[n] is None else sums[n] + part
            tile_ref[0, i:i + 1, width:] = sums[0]
            tile_ref[0, 4 + i:5 + i, width:] = sums[1]

        for load in loads[2:]:
            load.wait()
        tile_ref[0, :, 0:width] = jnp.zeros((8, width), F32)
        tile_ref[0, 0:2, 0:width] = sums_ref[0:2, :]
        full = slice(None)
        square(1, mine, [(finals[2][mine, 0:width], full)])
        square(2, mine, [(finals[2][mine, width:width + wide], full)])
        square(3, deep, [(finals[3][deep, :], full)])
        second.add1()
        second.start2()
        for s in (first, mid, down):
            s.finish()
        r1a_ref[...] = finals[0][...]
        r2_ref[...] = finals[2][...]
        r3_ref[...] = finals[3][...]
        second.add2()
        square(0, mine, [(finals[half][mine, part * SIDE:(part + 1) * SIDE], slice(part * width + half * SIDE, part * width + (half + 1) * SIDE))
                         for half in range(HALVES) for part in range(3)])
        norm.start(0)
        second.finish()
        r1b_ref[...] = finals[1][:, 0:3 * SIDE]
        norm.add(0)
        norm.start(1)
        norm.add(1)
        norms_ref[...] = jnp.broadcast_to(jnp.sqrt(jnp.sum(tile_ref[2, :, width:], axis=1, keepdims=True)), (8, LANES))
        late = jnp.concatenate([tile_ref[2, :, 0:width], jnp.zeros((LANES - 8, width), F32)], axis=0)
        late_ref[...] = late.T
        thin = width // CHIPS
        mine_late = late_ref[pl.ds(pl.multiple_of(chip * thin, thin), thin), :]
        table = jnp.where(lax.broadcasted_iota(jnp.int32, (1, LANES), 1) < 2, mine_late, finals[1][:, 3 * SIDE:])
        count = rv_ref.shape[0]
        for at, row in enumerate(flat_of(table, count * LANES // table.shape[0], count)):
            rv_ref[at:at + 1, :] = row


def phase_b(remote_on, off, x, qkv, bctx, bmid, lse, dots, w1, sums_a, grads=(), masters=(), firsts=(), seconds=(), flat_rows=0):
    rows, length, width = x.shape
    pairs = rows // GROUP
    blk = lambda w, index: pl.BlockSpec((GROUP, length, w), index)
    both = lambda s, *_: (lax.rem(s, pairs), 0, 0)
    late = lambda s, *_: (jnp.maximum(s - HALVES * pairs, 0), 0, 0)
    side = lambda s: jnp.minimum(s // pairs, HALVES - 1)
    pair = lambda s: jnp.where(s < HALVES * pairs, lax.rem(s, pairs), pairs - 1)
    sds = jax.ShapeDtypeStruct
    rowed = pl.BlockSpec((1, GROUP, 8, PAD), lambda s, *_: (side(s), pair(s), 0, 0))
    extra = (*grads, *masters, *firsts, *seconds)
    stack = lambda: pltpu.VMEM((GROUP, FOUR * PAD, SIDE), BF16)
    probs = lambda: pltpu.VMEM((GROUP, length, FOUR * PAD), BF16)
    scratch = [pltpu.VMEM((HALVES, width, 3 * SIDE), F32), pltpu.VMEM((HALVES, rows, length, 3 * SIDE), BF16),
               pltpu.VMEM((rows, length, width), BF16), pltpu.VMEM((GROUP, length, PAD), F32), stack(), stack(),
               pltpu.VMEM((GROUP, FOUR * length, SIDE), BF16), probs(), probs(), pltpu.VMEM((GROUP, FOUR * length, PAD), BF16),
               pltpu.VMEM((LANES, width), F32), pltpu.VMEM((LANES, width), F32)]
    params = dict(vmem_limit_bytes=62 << 20)
    if remote_on:
        thin = width // CHIPS
        sizes = [(thin, 3 * SIDE), (thin, 3 * SIDE + LANES)] + [(g.shape[0] // CHIPS, g.shape[1]) for g in grads]
        outs = [sds(s, F32) for s in [sizes[0]] * HALVES + sizes[2:] + [(flat_rows, LANES), (8, LANES)]]
        for s in sizes:
            scratch += scatter_bufs(*s)
        scratch += [pltpu.VMEM(s, F32) for s in sizes]
        scratch += [pltpu.VMEM((4, 4) + sizes[0], BF16), pltpu.VMEM((4, 4) + sizes[1], BF16), pltpu.VMEM((3, 8, width + LANES), F32),
                    pltpu.VMEM((10, 8, width + LANES), F32), pltpu.VMEM((width, LANES), F32), DMA((4, 8)), DMA((4, 8)), DMA((10,)), DMA((10,))]
        scratch += [pltpu.VMEM(e.shape, e.dtype) for e in extra] + [DMA((len(extra),))]
        params.update(collective_id=1, has_side_effects=True)
    else:
        outs = [sds((HALVES, width, 3 * SIDE), BF16), sds((width, LANES), BF16)]
    return pl.pallas_call(
        lambda *refs: kernel_b(remote_on, *refs),
        name="phase_b",
        grid_spec=pltpu.PrefetchScalarGridSpec(
            num_scalar_prefetch=0,
            grid=(3 * pairs,),
            in_specs=[whole(off.shape), blk(width, both), pl.BlockSpec((1, GROUP, length, 3 * SIDE), lambda s, *_: (side(s), pair(s), 0, 0)),
                      pl.BlockSpec((GROUP, length, SIDE), lambda s, *_: (pair(s), 0, side(s))), blk(width, late),
                      rowed, rowed, whole(w1.shape),
                      whole(sums_a.shape)] + [pl.BlockSpec(memory_space=pl.ANY)] * len(extra),
            out_specs=[blk(width, late)] + [whole(o.shape) for o in outs],
            scratch_shapes=scratch,
        ),
        out_shape=[sds(x.shape, BF16)] + outs,
        compiler_params=pltpu.CompilerParams(**params),
    )(off, x, qkv, bctx, bmid, lse, dots, w1, sums_a, *extra)


def update_kernel(*refs):
    n_in, n_out = 17, 17
    y_ref, xgrad_ref, y_out, xgrad_out = refs[0], refs[1], refs[2 + n_in], refs[3 + n_in]
    ins, outs = refs[2:2 + n_in], refs[4 + n_in:4 + n_in + n_out]
    held_y, held_x, wide_x = refs[4 + n_in + n_out:7 + n_in + n_out]
    kept = refs[7 + n_in + n_out:]
    held_in, held_out, sem_in, sem_out, sems = kept[:n_in], kept[n_in:n_in + n_out], *kept[n_in + n_out:]
    count = y_ref.shape[0]
    load = [pltpu.make_async_copy(src, dst, sem_in.at[i]) for i, (src, dst) in enumerate(zip(ins, held_in))]
    load_x = [pltpu.make_async_copy(xgrad_ref.at[row], held_x.at[row], sems.at[0, row]) for row in range(count)]
    load_y = [pltpu.make_async_copy(y_ref.at[row], held_y.at[row], sems.at[1, row]) for row in range(count)]
    store_x = [pltpu.make_async_copy(wide_x.at[row], xgrad_out.at[row], sems.at[2, row]) for row in range(count)]
    store_y = [pltpu.make_async_copy(held_y.at[row], y_out.at[row], sems.at[3, row]) for row in range(count)]
    for copy in load_x + load + load_y:
        copy.start()
    for row in range(count):
        load_x[row].wait()
        wide_x[row] = held_x[row].astype(F32)
        store_x[row].start()
    for copy in load:
        copy.wait()
    r1a, r1b, r2, r3, norms_ref = held_in[:5]
    masters, firsts, seconds = held_in[5:9], held_in[9:13], held_in[13:17]
    new_m, new_f, new_s, copies, norm_out = held_out[0:4], held_out[4:8], held_out[8:12], held_out[12:16], held_out[16]
    store = [pltpu.make_async_copy(src, dst, sem_out.at[i]) for i, (src, dst) in enumerate(zip(held_out, outs))]
    width, wide = masters[1].shape[1], masters[2].shape[1]
    full = slice(None)
    places = [(3, r3[...], full, True), (2, r2[:, width:width + wide], full, True), (1, r2[:, 0:width], full, True)]
    places += [(0, (r1a, r1b)[half][:, part * SIDE:(part + 1) * SIDE], slice(part * width + half * SIDE, part * width + (half + 1) * SIDE),
                half == HALVES - 1 and part == 2) for half in range(HALVES) for part in range(3)]
    row = lax.broadcasted_iota(jnp.int32, (3, 4), 0)
    col = lax.broadcasted_iota(jnp.int32, (3, 4), 1)
    table = jnp.zeros((3, 4), F32)
    for i, grad, cols, final in places:
        weight_norm, update_norm = norms_ref[i:i + 1, 0:1], norms_ref[4 + i:5 + i, 0:1]
        trust = weight_norm / update_norm
        first, second, direction = moments_of(grad, firsts[i][:, cols], seconds[i][:, cols])
        master = masters[i][:, cols]
        new = master - matrix_rate * trust * (direction + weight_decay * master)
        new_m[i][:, cols] = new
        copies[i][:, cols] = new.astype(BF16)
        new_f[i][:, cols] = first
        new_s[i][:, cols] = second
        if final:
            for block in range(4):
                store[4 * block + i].start()
        for r, value in enumerate((weight_norm, update_norm, trust)):
            table = jnp.where((row == r) & (col == i), value, table)
    norm_out[...] = table
    store[16].start()
    for row in range(count):
        load_y[row].wait()
        store_y[row].start()
    for copy in store_x + store + store_y:
        copy.wait()


def update_all(y, xgrad, reduced, norms, masters, firsts, seconds):
    sds = jax.ShapeDtypeStruct
    place = pl.BlockSpec(memory_space=pl.ANY)
    ins = (*reduced, norms, *masters, *firsts, *seconds)
    outs = [sds(m.shape, F32) for m in masters] * 3 + [sds(m.shape, BF16) for m in masters] + [sds((3, 4), F32)]
    return pl.pallas_call(
        update_kernel,
        name="update",
        out_shape=[sds(y.shape, y.dtype), sds(xgrad.shape, F32)] + outs,
        in_specs=[place] * (2 + len(ins)),
        out_specs=[place] * (2 + len(outs)),
        scratch_shapes=[pltpu.VMEM(y.shape, y.dtype), pltpu.VMEM(xgrad.shape, xgrad.dtype), pltpu.VMEM(xgrad.shape, F32)]
        + [pltpu.VMEM(a.shape, a.dtype) for a in (*ins, *outs)] + [DMA((len(ins),)), DMA((len(outs),)), DMA((4, y.shape[0]))],
        compiler_params=pltpu.CompilerParams(vmem_limit_bytes=62 << 20),
    )(y, xgrad, *ins)


def shards(block_in, offsets, cotangent, w_qkv, w_out, w_up, w_down, vectors, *moments):
    masters = (w_qkv, w_out, w_up, w_down)
    firsts, seconds = moments[:5], moments[5:]
    micro, local_rows, length, width = block_in.shape
    rows = micro * local_rows
    chips = lax.axis_size("fsdp")
    near = chips == CHIPS and lax.axis_size("dp") == 2 and vectors.shape[0] % LANES == 0
    columns = vectors.shape[0] * chips // width
    x = block_in.reshape(rows, length, width)
    cot = cotangent.reshape(rows, length, width)
    off = offsets.transpose(0, 2, 1)
    if near:
        flat = vectors.reshape(-1, LANES)
        y, qkv, bctx, bmid, lse, dots, g2, g3, sums_a, w1 = phase_a(True, off, x, cot, (*masters, flat))
        xgrad, *reduced, norms = phase_b(True, off, x, qkv, bctx, bmid, lse, dots, w1, sums_a, (g2, g3), masters, firsts[:4], seconds[:4],
                                           flat.shape[0])
    else:
        table = jnp.pad(vectors.reshape(-1, columns), ((0, 0), (0, LANES - columns)))
        sides = w_qkv.reshape(-1, 3, HALVES, SIDE).transpose(2, 0, 1, 3).reshape(HALVES, -1, 3 * SIDE)
        owns = [jnp.concatenate([sides, jnp.broadcast_to(table, (HALVES,) + table.shape)], axis=2),
                jnp.concatenate([w_out, w_up], axis=1), w_down]
        wholes = [lax.all_gather(o.astype(BF16), "fsdp", axis=o.ndim - 2, tiled=True) for o in owns]
        y, qkv, bctx, bmid, lse, dots, g2, g3, sums_a = phase_a(False, off, x, cot, wholes)
        xgrad, g1, gv = phase_b(False, off, x, qkv, bctx, bmid, lse, dots, wholes[0], sums_a)
        reduced = [lax.psum(lax.psum_scatter(g.astype(F32), "fsdp", scatter_dimension=0, tiled=True), "dp")
                   for g in (g1[0], g1[1], g2, g3, gv)]
        reduced[4] = reduced[4][:, :columns]
        grad1 = jnp.stack(reduced[:2]).reshape(HALVES, -1, 3, SIDE).transpose(1, 2, 0, 3).reshape(w_qkv.shape)
        grads = (grad1, reduced[2][:, :width], reduced[2][:, width:], reduced[3])
        updates = [moments_of(g, m, s)[2] + weight_decay * w for g, m, s, w in zip(grads, firsts, seconds, masters)]
        squares = jnp.stack([jnp.sum(w * w) for w in masters] + [jnp.sum(u * u) for u in updates])
        norms = jnp.broadcast_to(jnp.sqrt(lax.psum(squares, "fsdp"))[:, None], (8, LANES))
    y, xgrad, *news, matrix_norms = update_all(y, xgrad, reduced[:4], norms, masters, firsts[:4], seconds[:4])
    vec_first, vec_second, vec_direction = moments_of(reduced[4].reshape(-1), firsts[4], seconds[4])
    vec_new = vectors - vector_rate * vec_direction
    return (y.reshape(block_in.shape), xgrad.reshape(block_in.shape), *news[0:4], vec_new, *news[4:8], vec_first,
            *news[8:12], vec_second, *news[12:16], vec_new.astype(BF16), matrix_norms)


def solution(mesh):
    batch, matrix, vector = P(None, ("fsdp", "dp"), None, None), P("fsdp", None), P("fsdp")
    params = (matrix,) * 4 + (vector,)
    in_specs = (batch, P(None, ("fsdp", "dp"), None), batch) + params * 3
    out_specs = (batch, batch) + params * 4 + (P(),)
    return jax.shard_map(shards, mesh=mesh, in_specs=in_specs, out_specs=out_specs, check_vma=False)
```

```python
import jax
import jax.numpy as jnp
from jax import lax
from jax.experimental import pallas as pl
from jax.experimental.pallas import tpu as pltpu
from jax.sharding import PartitionSpec as P

HEAD_DIM = 64
STEP = 5
EPS = 1e-05
beta_first = 0.5
beta_second = 0.5
adam_eps = 1e-06
weight_decay = 0.01
matrix_rate = 1.0
vector_rate = 0.1
CHIPS = 16
GROUP = 2
LANES = 128
HALVES = 2
SIDE = 256
FOUR = 4
PAD = 384
NEG = -1e30
C0 = 0.7978845608028654
C1 = 0.044715
F32 = jnp.float32
BF16 = jnp.bfloat16
MESH = pl.DeviceIdType.MESH
DMA = pltpu.SemaphoreType.DMA


def nn(a, b):
    return lax.dot_general(a, b, (((1,), (0,)), ((), ())), preferred_element_type=F32)


def nt(a, b):
    return lax.dot_general(a, b, (((1,), (1,)), ((), ())), preferred_element_type=F32)


def tn(a, b):
    return lax.dot_general(a, b, (((0,), (0,)), ((), ())), preferred_element_type=F32)


def xhat_of(v):
    center = v - jnp.mean(v, axis=-1, keepdims=True)
    spread = jnp.mean(center * center, axis=-1, keepdims=True)
    inv = lax.rsqrt(spread + EPS)
    return center * inv, inv


def norm_back(e, xhat, inv):
    return (e - jnp.mean(e, axis=-1, keepdims=True) - xhat * jnp.mean(e * xhat, axis=-1, keepdims=True)) * inv


def crop_of(first, second, shape, axis):
    t = lax.broadcasted_iota(jnp.int32, shape, axis).astype(F32)
    return (t >= first).astype(jnp.int32) + (t >= second).astype(jnp.int32)


def side_of(ref, half, lo, hi):
    v = ref[half, ..., lo:hi]
    return v.reshape(-1, hi - lo)


def stack_heads(ref, tiles, pitch):
    low = lax.broadcasted_iota(jnp.int32, (1, LANES), 1) < HEAD_DIM
    for head in range(FOUR):
        tile = tiles[head // 2]
        keep = low if head % 2 == 0 else jnp.logical_not(low)
        lanes = slice(head // 2 * LANES, head // 2 * LANES + LANES)
        ref[head * pitch:head * pitch + tile.shape[0], lanes] = jnp.where(keep, tile, jnp.zeros_like(tile))


def offsets_of(ref, row):
    micro, inner = row // ref.shape[2], lax.rem(row, ref.shape[2])
    table = ref[micro].astype(F32)
    at = lax.broadcasted_iota(jnp.int32, (1, ref.shape[2]), 1)
    both = jnp.sum(jnp.where(at == inner, table, 0.0), axis=1, keepdims=True)
    return both[0:1], both[1:2]


def flat_places(rows, columns, at, axis_row, axis_lane, shape):
    row = lax.broadcasted_iota(jnp.int32, shape, axis_row)
    lane = lax.broadcasted_iota(jnp.int32, shape, axis_lane)
    return [row * columns + c == lane + at * LANES for c in range(columns)]


def table_of(flat, rows, columns):
    masks = [flat_places(rows, columns, at, 0, 1, (rows, LANES)) for at in range(flat.shape[0])]
    lane = lax.broadcasted_iota(jnp.int32, (1, LANES), 1)
    table = jnp.zeros((rows, LANES), F32)
    for c in range(columns):
        found = jnp.zeros((rows, LANES), F32)
        for at in range(flat.shape[0]):
            found = jnp.where(masks[at][c], flat[at:at + 1, :], found)
        table = jnp.where(lane == c, jnp.sum(found, axis=1, keepdims=True), table)
    return table


def flat_of(table, columns, count):
    rows = table.shape[0]
    out = []
    for at in range(count):
        masks = flat_places(rows, columns, at, 0, 1, (rows, LANES))
        found = jnp.zeros((rows, LANES), F32)
        for c in range(columns):
            found = jnp.where(masks[c], table[:, c:c + 1], found)
        out.append(jnp.sum(found, axis=0, keepdims=True))
    return out


def col_sum(v):
    return jnp.sum(v, axis=0, keepdims=True)


def partner(chip, flip):
    out = chip
    for bit in (1, 2, 4, 8):
        if flip & bit:
            out = out + bit - 2 * bit * lax.rem(chip // bit, 2)
    return out


def meet(chip, core, flips, others):
    barrier = pltpu.get_barrier_semaphore()
    for flip in flips:
        pl.semaphore_signal(barrier, inc=1, device_id=(partner(chip, flip), core), device_id_type=MESH)
    for flip in others:
        pl.semaphore_signal(barrier, inc=1, device_id=(partner(chip, flip), 1 - core), device_id_type=MESH)
    pl.semaphore_wait(barrier, len(flips) + len(others))


def remote(src, dst, send_sem, recv_sem, chip, core):
    return pltpu.make_async_remote_copy(src_ref=src, dst_ref=dst, send_sem=send_sem, recv_sem=recv_sem,
                                        device_id=(chip, core), device_id_type=MESH)


def wait_bytes(ref, sem):
    pltpu.make_async_copy(ref, ref, sem).wait()


class Gather:
    def __init__(self, whole, cols, send, recv, chip, core, quick, calm):
        self.whole, self.cols, self.chip, self.core, self.send, self.recv, self.quick, self.calm = whole, cols, chip, core, send, recv, quick, calm
        self.half = whole.shape[-2] // 2
        start = pl.multiple_of(core * self.half, self.half)
        self.rows, self.all = pl.ds(start, self.half), pl.ds(0, cols)
        self.mine = (self.rows, self.all)
        if self.half >= 32:
            q = self.half // 2
            self.cuts = [(pl.ds(start + i * q, q), self.all) for i in range(2)]
        else:
            q = cols // 256 * 128
            self.cuts = [(self.rows, pl.ds(0, q)), (self.rows, pl.ds(q, cols - q))]

    def column(self, flip, cut):
        return self.whole.at[:, lax.rem(partner(self.chip, flip), 4), cut[0], cut[1]]

    def shard(self, flip):
        at = partner(self.chip, flip)
        return self.whole.at[at // 4, lax.rem(at, 4), self.rows, self.all]

    def push(self, ref, sem, to):
        remote(ref, ref, self.send, self.recv.at[sem], partner(self.chip, to), self.core).start()

    def to_twin(self, flip):
        if self.calm and flip != 3:
            return
        ref = self.whole.at[:, :, self.rows, self.all] if self.calm else self.column(flip, self.mine)
        remote(ref, ref, self.send, self.recv.at[8], self.chip, 1 - self.core).start()

    def start(self):
        own = self.shard(0)
        for flip in (4, 8, 12):
            self.push(own, flip // 4, flip)
        if self.quick:
            self.push(own, 4, 1)
            self.push(own, 5, 2)

    def spread(self):
        for flip in (4, 8, 12):
            ref = self.shard(flip)
            wait_bytes(ref, self.recv.at[flip // 4])
            if self.quick:
                self.push(ref, 4, 1)
                self.push(ref, 5, 2)
        ref = self.column(0, self.mine)
        if not self.quick:
            self.push(ref, 4, 1)
            self.push(ref, 5, 2)
        self.to_twin(0)

    def cross(self):
        for sem, via, to, cut in ((4, 1, 2, 0), (5, 2, 1, 1)):
            wait_bytes(self.column(via, self.mine), self.recv.at[sem])
            self.push(self.column(via, self.cuts[cut]), 6 + cut, to)
            self.to_twin(via)

    def last(self):
        for cut in range(2):
            wait_bytes(self.column(3, self.cuts[cut]), self.recv.at[6 + cut])
        self.to_twin(3)

    def finish(self):
        wait_bytes(self.whole.at[:, :, pl.ds(0, self.half), self.all], self.recv.at[8])

    def drain(self):
        rows = pl.ds(0, self.half)
        for zs, yxs in (((0, 4), (0, 4)), ((0, 3), (0, 4)), ((0, 1), (0, 3))):
            wait_bytes(self.whole.at[pl.ds(*zs), pl.ds(*yxs), rows, self.all], self.send)


class Scatter:
    def __init__(self, grad, bufs, out, send, recv, chip, core):
        self.grad, self.out, self.send, self.recv, self.chip, self.core = grad, out, send, recv, chip, core
        self.got0, self.part, self.got1, self.col, self.got2 = bufs
        self.half = grad.shape[2] // 2
        self.start_mine = pl.multiple_of(core * self.half, self.half)
        self.rows_mine = pl.ds(self.start_mine, self.half)
        self.z, self.yx = chip // 4, lax.rem(chip, 4)

    def copy0(self):
        theirs = pl.ds(pl.multiple_of((1 - self.core) * self.half, self.half), self.half)
        return remote(self.grad.at[:, :, theirs, :], self.got0, self.send.at[0], self.recv.at[0], self.chip, 1 - self.core)

    def start0(self):
        self.copy0().start()

    def add0(self):
        self.copy0().wait()

        def one(i, _):
            z, yx = i // 4, lax.rem(i, 4)
            mine = self.grad[z, yx, pl.ds(self.start_mine, self.half), :].astype(F32)
            self.part[z, yx] = (mine + self.got0[z, yx].astype(F32)).astype(BF16)
            return 0

        lax.fori_loop(0, CHIPS, one, 0)

    def copy1(self, flip):
        to = partner(self.chip, flip)
        return remote(self.part.at[:, lax.rem(to, 4)], self.got1.at[flip - 1], self.send.at[flip], self.recv.at[flip], to, self.core)

    def start1(self):
        for flip in (3, 1, 2):
            self.copy1(flip).start()

    def add1(self):
        for flip in (1, 2, 3):
            self.copy1(flip).wait()

        def one(z, _):
            total = self.part[z, self.yx].astype(F32)
            for k in range(3):
                total = total + self.got1[k, z].astype(F32)
            self.col[z] = total.astype(BF16)
            return 0

        lax.fori_loop(0, 4, one, 0)

    def copy2(self, flip):
        to = partner(self.chip, 4 * flip)
        return remote(self.col.at[to // 4], self.got2.at[flip - 1], self.send.at[3 + flip], self.recv.at[3 + flip], to, self.core)

    def start2(self):
        for flip in (1, 2, 3):
            self.copy2(flip).start()

    def copy3(self):
        ref = self.out.at[pl.ds(self.start_mine, self.half), :]
        return remote(ref, ref, self.send.at[7], self.recv.at[7], self.chip, 1 - self.core)

    def add2(self):
        for flip in (1, 2, 3):
            self.copy2(flip).wait()
        total = self.col[self.z].astype(F32)
        for k in range(3):
            total = total + self.got2[k].astype(F32)
        self.out[pl.ds(self.start_mine, self.half), :] = total
        self.copy3().start()

    def finish(self):
        self.copy3().wait()


def scatter_bufs(rows, cols):
    half = rows // 2
    return [pltpu.VMEM((4, 4, half, cols), BF16), pltpu.VMEM((4, 4, half, cols), BF16), pltpu.VMEM((3, 4, half, cols), BF16),
            pltpu.VMEM((4, half, cols), BF16), pltpu.VMEM((3, half, cols), BF16)]


class Total:
    def __init__(self, tile, got, send, recv, chip, core):
        self.tile, self.got, self.send, self.recv, self.chip, self.core = tile, got, send, recv, chip, core

    def copies(self, turn):
        if turn == 0:
            peers = [(flip, other) for flip in range(4) for other in range(2) if flip or other]
        else:
            peers = [(flip, 0) for flip in (4, 8, 12)]
        out = []
        for n, (flip, other) in enumerate(peers):
            at = 7 * turn + n
            out.append(remote(self.tile.at[turn], self.got.at[at], self.send.at[at], self.recv.at[at], partner(self.chip, flip),
                              1 - self.core if other else self.core))
        return out

    def start(self, turn):
        for copy in self.copies(turn):
            copy.start()

    def add(self, turn):
        copies = self.copies(turn)
        for copy in copies:
            copy.wait()
        total = self.tile[turn]
        for n in range(len(copies)):
            total = total + self.got[7 * turn + n]
        self.tile[turn + 1] = total


FLIPS = (1, 2, 3, 4, 8, 12)


def kernel_a(remote_on, off_ref, x_ref, cot_ref, *refs):
    if remote_on:
        masters, refs = refs[:5], refs[5:]
    else:
        w_in, refs = refs[:3], refs[3:]
    y_ref, qkv_ref, bctx_ref, bmid_ref, lse_ref, dot_ref, g2_out, g3_out, sums_ref = refs[:9]
    refs = refs[9:]
    if remote_on:
        w1_out, refs = refs[0], refs[1:]
    gup_ref, gdn_ref, gout_ref, ctx_ref, n1_ref, bias_ref, kstack_ref, vstack_ref, p_ref, vec_ref = refs[:10]
    refs = refs[10:]
    step = pl.program_id(0)
    group, length, width = x_ref.shape
    pairs = pl.num_programs(0) // 3
    early = HALVES * pairs
    tokens = group * length
    hidden = gup_ref.shape[1]
    chunks = hidden // width
    if remote_on:
        w1_ref, whole2, whole3, send, recv, out_sem = refs
        chip, core = lax.axis_index("fsdp"), lax.axis_index("dp")
        wide = 3 * SIDE
        gathers = [Gather(w, cols, send.at[i], recv.at[i], chip, core, i in (0, 2), i in (1, 2)) for i, (w, cols) in enumerate((
            (w1_ref.at[0], wide + LANES), (w1_ref.at[1], wide), (whole2, width + hidden), (whole3, width)))]
        w2_ref, w3_ref = [w.reshape(CHIPS * w.shape[2], w.shape[3]) for w in (whole2, whole3)]
    else:
        w1_ref, w2_ref, w3_ref = w_in
    wout_ref, wup_ref = w2_ref.at[:, 0:width], w2_ref.at[:, width:width + hidden]

    @pl.when(step == 0)
    def _():
        if remote_on:
            rows = [g.rows for g in gathers]
            z, yx = chip // 4, lax.rem(chip, 4)

            def cast_side(half):
                for part in range(3):
                    at = part * width + half * SIDE
                    w1_ref[half, z, yx, rows[0], part * SIDE:(part + 1) * SIDE] = masters[0][rows[0], at:at + SIDE].astype(BF16)

            cast_side(0)
            thin = w1_ref.shape[3]
            table = table_of(masters[4][...], thin, masters[4].shape[0] * LANES // thin)
            w1_ref[0, z, yx, rows[0], wide:] = jnp.where(core == 0, table[:thin // 2], table[thin // 2:]).astype(BF16)
            meet(chip, core, FLIPS, (0,))
            gathers[0].start()
            cast_side(1)
            whole2[z, yx, rows[2], 0:width] = masters[1][rows[2], :].astype(BF16)
            whole2[z, yx, rows[2], width:] = masters[2][rows[2], :].astype(BF16)
            whole3[z, yx, rows[3], :] = masters[3][rows[3], :].astype(BF16)
        gup_ref[...] = jnp.zeros_like(gup_ref)
        gdn_ref[...] = jnp.zeros_like(gdn_ref)
        gout_ref[...] = jnp.zeros_like(gout_ref)
        sums_ref[...] = jnp.zeros_like(sums_ref)
        kstack_ref[...] = jnp.zeros_like(kstack_ref)
        vstack_ref[...] = jnp.zeros_like(vstack_ref)
        if remote_on:
            gathers[0].spread()
            for g in gathers[1:]:
                g.start()
            gathers[0].cross()
            gathers[0].last()
            gathers[1].spread()
            gathers[0].finish()
        vec_ref[...] = side_of(w1_ref, 0, 3 * SIDE, 3 * SIDE + LANES).astype(F32).T

    events = {}
    if remote_on:
        events = {0: [gathers[1].cross, gathers[2].spread], 1: [gathers[1].last], 2: [gathers[3].spread], 4: [gathers[2].cross], 5: [gathers[3].cross], 6: [gathers[2].last], 7: [gathers[3].last]}

    @pl.when(step < pairs)
    def _():
        x = x_ref[...].reshape(tokens, width).astype(F32)
        xhat, _ = xhat_of(x)
        n1 = (xhat * vec_ref[0:1, :] + vec_ref[1:2, :]).astype(BF16)
        n1_ref[pl.ds(step * group, group)] = n1.reshape(group, length, width)

    if remote_on:
        @pl.when(step == pairs)
        def _():
            gathers[1].finish()

    @pl.when(step < early)
    def _():
        half = step // pairs
        first_row = lax.rem(step, pairs) * group
        side = pl.ds(pl.multiple_of(half * SIDE, SIDE), SIDE)
        n1 = n1_ref[pl.ds(first_row, group)].reshape(tokens, width)
        q = ((nn(n1, side_of(w1_ref, half, 0, SIDE)) + vec_ref[2:3, side]) * HEAD_DIM ** (-0.5)).astype(BF16)
        k = nn(n1, side_of(w1_ref, half, SIDE, 2 * SIDE)).astype(BF16)
        v = (nn(n1, side_of(w1_ref, half, 2 * SIDE, 3 * SIDE)) + vec_ref[3:4, side]).astype(BF16)
        for part, value in enumerate((q, k, v)):
            qkv_ref[0, :, :, part * SIDE:(part + 1) * SIDE] = value.reshape(group, length, SIDE)
        lane = lax.broadcasted_iota(jnp.int32, (1, LANES), 1)

        def products(r):
            row = first_row + r
            crop_q = crop_of(*offsets_of(off_ref, row), (length, 1), 0)
            crop_k = crop_of(*offsets_of(off_ref, row), (1, PAD), 1)
            inside = lax.broadcasted_iota(jnp.int32, (1, PAD), 1) < length
            bias_ref[r] = jnp.where((crop_q == crop_k) & inside, 0.0, NEG)
            kr, vr = [[t[r * length:(r + 1) * length, c * LANES:(c + 1) * LANES] for c in range(2)] for t in (k, v)]
            stack_heads(kstack_ref.at[r], kr, PAD)
            stack_heads(vstack_ref.at[r], vr, PAD)
            return nt(q[r * length:(r + 1) * length], kstack_ref[r])

        def softmax(r, head, scores):
            lanes = slice(head * PAD, (head + 1) * PAD)
            s = scores[:, lanes] + bias_ref[r]
            peak = jnp.max(s, axis=-1, keepdims=True)
            e = jnp.exp(s - peak)
            p_ref[r, :, lanes] = e.astype(BF16)
            total = jnp.sum(e, axis=-1, keepdims=True)
            return 1.0 / total, peak + jnp.log(total)

        def contexts(r, stats):
            ctx = nn(p_ref[r], vstack_ref[r])
            for c in range(2):
                inverse = jnp.where(lane < HEAD_DIM, stats[2 * c][0], stats[2 * c + 1][0])
                lanes = pl.ds(pl.multiple_of(half * SIDE + c * LANES, LANES), LANES)
                ctx_ref[first_row + r, :, lanes] = (ctx[:, c * LANES:(c + 1) * LANES] * inverse).astype(BF16)
            table = jnp.zeros((length, LANES), F32)
            for head in range(FOUR):
                table = jnp.where(lane == head, stats[head][1], table)
            table = jnp.concatenate([table, jnp.zeros((PAD - length, LANES), F32)], axis=0)
            lse_ref[0, r] = table.T[:8]

        scores = [products(r) for r in range(group)]
        stats = []
        for r in range(group):
            stats.append([softmax(r, head, scores[r]) for head in range(FOUR)])
            if r:
                contexts(r - 1, stats[r - 1])
        contexts(group - 1, stats[group - 1])
        for at, todo in events.items():
            def run(todo=todo):
                for event in todo:
                    event()
            pl.when(step == at)(run)

    @pl.when(step == early)
    def _():
        if remote_on:
            gathers[2].finish()
            gathers[3].finish()
            pltpu.make_async_copy(w1_ref, w1_out, out_sem).start()

    @pl.when(step >= early)
    def _():
        first_row = (step - early) * group
        ctx = ctx_ref[pl.ds(first_row, group)].reshape(tokens, width)
        middle = x_ref[...].reshape(tokens, width).astype(F32) + (nn(ctx, wout_ref[...]) + vec_ref[4:5, :])
        xhat2, inv2 = xhat_of(middle)
        n2 = (xhat2 * vec_ref[5:6, :] + vec_ref[6:7, :]).astype(BF16)
        cot = cot_ref[...].reshape(tokens, width)
        result = middle + vec_ref[7 + chunks:8 + chunks, :]
        back_n2 = jnp.zeros((tokens, width), F32)

        def weight_grads(cols, active, back_up):
            gdn_ref[:, cols] += tn(cot, active)
            gup_ref[:, cols] += tn(n2, back_up)

        held = None

        def products(u):
            cols = slice(u * SIDE, (u + 1) * SIDE)
            bias = vec_ref[7 + u // 2:8 + u // 2, u % 2 * SIDE:(u % 2 + 1) * SIDE]
            return nn(n2, wup_ref[:, cols]) + bias, nt(cot, w3_ref[cols, :])

        ahead = products(0)
        for u in range(hidden // SIDE):
            cols = slice(u * SIDE, (u + 1) * SIDE)
            up, back_act = ahead
            if u + 1 < hidden // SIDE:
                ahead = products(u + 1)
            if held is not None:
                weight_grads(*held)
            square = up * up
            gate = 0.5 + 0.5 * jnp.tanh(up * (C0 + (C0 * C1) * square))
            active = up * gate
            slope = gate + active * (1.0 - gate) * (2.0 * C0 + (6.0 * C0 * C1) * square)
            active = active.astype(BF16)
            back_up = back_act * slope
            sums_ref[7 + u // 2:8 + u // 2, u % 2 * SIDE:(u % 2 + 1) * SIDE] += col_sum(back_up)
            back_up = back_up.astype(BF16)
            result = result + nn(active, w3_ref[cols, :])
            back_n2 = back_n2 + nt(back_up, wup_ref[:, cols])
            held = (cols, active, back_up)
        weight_grads(*held)
        y_ref[...] = result.astype(BF16).reshape(group, length, width)
        cot32 = cot.astype(F32)
        sums_ref[7 + chunks:8 + chunks, :] += col_sum(cot32)
        sums_ref[5:6, :] += col_sum(back_n2 * xhat2)
        sums_ref[6:7, :] += col_sum(back_n2)
        back_middle = cot32 + norm_back(back_n2 * vec_ref[5:6, :], xhat2, inv2)
        back_att = back_middle.astype(BF16)
        bmid_ref[...] = back_att.reshape(group, length, width)
        sums_ref[4:5, :] += col_sum(back_middle)
        gout_ref[...] += tn(ctx, back_att)
        back_ctx = nt(back_att, wout_ref[...]).astype(BF16)
        bctx_ref[...] = back_ctx.reshape(group, length, width)
        pick = (lax.broadcasted_iota(jnp.int32, (16, width), 1) // HEAD_DIM == lax.broadcasted_iota(jnp.int32, (16, width), 0)).astype(BF16)
        for r in range(group):
            rows = slice(r * length, (r + 1) * length)
            product = ctx[rows].astype(F32) * back_ctx[rows].astype(F32)
            product = jnp.concatenate([product, jnp.zeros((PAD - length, width), F32)], axis=0)
            high = product.astype(BF16)
            dots = nt(pick, high) + nt(pick, (product - high.astype(F32)).astype(BF16))
            for half in range(HALVES):
                dot_ref[half, r, 0:FOUR, :] = dots[half * FOUR:(half + 1) * FOUR]
                dot_ref[half, r, FOUR:, :] = jnp.zeros((8 - FOUR, PAD), F32)

    @pl.when(step == pl.num_programs(0) - 1)
    def _():
        g2_out[:, 0:width] = gout_ref[...].astype(BF16)
        g2_out[:, width:] = gup_ref[...].astype(BF16)
        for u in range(chunks):
            g3_out[u * width:(u + 1) * width, :] = gdn_ref[:, u * width:(u + 1) * width].T.astype(BF16)
        if remote_on:
            pltpu.make_async_copy(w1_ref, w1_out, out_sem).wait()
            for g in gathers:
                g.drain()


def whole(shape):
    return pl.BlockSpec(shape, lambda s, *_: (0,) * len(shape), pipeline_mode=pl.Buffered(1))


def phase_a(remote_on, off, x, cot, weights):
    rows, length, width = x.shape
    pairs = rows // GROUP
    if remote_on:
        sizes = [(weights[0].shape[0], 3 * SIDE + LANES), (weights[1].shape[0], width + weights[2].shape[1]), weights[3].shape]
        w2_shape, w3_shape = (CHIPS * sizes[1][0], sizes[1][1]), (CHIPS * sizes[2][0], sizes[2][1])
    else:
        w2_shape, w3_shape = weights[1].shape, weights[2].shape
    hidden = w3_shape[0]
    blk = lambda w, index: pl.BlockSpec((GROUP, length, w), index)
    both = lambda s, *_: (lax.rem(s, pairs), 0, 0)
    late = lambda s, *_: (jnp.maximum(s - HALVES * pairs, 0), 0, 0)
    sided = lambda s, *_: (jnp.minimum(s // pairs, HALVES - 1), jnp.where(s < HALVES * pairs, lax.rem(s, pairs), pairs - 1), 0, 0)
    sds = jax.ShapeDtypeStruct
    out_specs = [blk(width, late), pl.BlockSpec((1, GROUP, length, 3 * SIDE), sided), blk(width, late), blk(width, late),
                 pl.BlockSpec((1, GROUP, 8, PAD), sided), pl.BlockSpec((HALVES, GROUP, 8, PAD), lambda s, *_: (0,) + late(s)),
                 whole(w2_shape), whole(w3_shape), whole((LANES, width))]
    out_shape = [sds(x.shape, BF16), sds((HALVES, rows, length, 3 * SIDE), BF16), sds(x.shape, BF16), sds(x.shape, BF16),
                 sds((HALVES, rows, 8, PAD), F32), sds((HALVES, rows, 8, PAD), F32),
                 sds(w2_shape, BF16), sds(w3_shape, BF16), sds((LANES, width), F32)]
    scratch = [pltpu.VMEM((width, hidden), F32), pltpu.VMEM((width, hidden), F32), pltpu.VMEM((width, width), F32),
               pltpu.VMEM((rows, length, width), BF16), pltpu.VMEM((rows, length, width), BF16), pltpu.VMEM((GROUP, length, PAD), F32),
               pltpu.VMEM((GROUP, FOUR * PAD, SIDE), BF16), pltpu.VMEM((GROUP, FOUR * PAD, SIDE), BF16),
               pltpu.VMEM((GROUP, length, FOUR * PAD), BF16), pltpu.VMEM((LANES, width), F32)]
    params = dict(vmem_limit_bytes=62 << 20)
    if remote_on:
        out_specs.append(pl.BlockSpec(memory_space=pl.ANY))
        out_shape.append(sds((HALVES, 4, 4) + sizes[0], BF16))
        scratch += [pltpu.VMEM((HALVES, 4, 4) + sizes[0], BF16)] + [pltpu.VMEM((4, 4) + s, BF16) for s in sizes[1:]]
        scratch += [DMA((4,)), DMA((4, 9)), DMA]
        params.update(collective_id=0, has_side_effects=True)
    return pl.pallas_call(
        lambda *refs: kernel_a(remote_on, *refs),
        name="phase_a",
        grid_spec=pltpu.PrefetchScalarGridSpec(
            num_scalar_prefetch=0,
            grid=(3 * pairs,),
            in_specs=[whole(off.shape), blk(width, both), blk(width, late)] + [whole(w.shape) for w in weights],
            out_specs=out_specs,
            scratch_shapes=scratch,
        ),
        out_shape=out_shape,
        compiler_params=pltpu.CompilerParams(**params),
    )(off, x, cot, *weights)


def moments_of(grad, first, second):
    new_first = beta_first * first + (1.0 - beta_first) * grad
    new_second = beta_second * second + (1.0 - beta_second) * grad * grad
    direction = new_first / (1.0 - beta_first**STEP) / (jnp.sqrt(new_second / (1.0 - beta_second**STEP)) + adam_eps)
    return new_first, new_second, direction


def lanes_of(v):
    total = None
    for j in range(v.shape[1] // LANES):
        piece = v[:, j * LANES:(j + 1) * LANES]
        total = piece if total is None else total + piece
    return jnp.sum(total, axis=0, keepdims=True)


def kernel_b(remote_on, off_ref, x_ref, qkv_ref, bctx_ref, bmid_ref, lse_ref, dot_ref, w1_ref, sums_a_ref, *refs):
    if remote_on:
        far = refs[0:14]
        xgrad_ref, r1a_ref, r1b_ref, r2_ref, r3_ref, rv_ref, norms_ref = refs[14:21]
        refs = refs[21:]
    else:
        xgrad_ref, g1_out, gv_out = refs[:3]
        refs = refs[3:]
    gqkv_ref, bqkv_ref, n1_ref, bias_ref, qstack_ref, ostack_ref, kstack_ref, p_ref, ds_ref, dsk_ref, sums_ref, vec_ref = refs[:12]
    refs = refs[12:]
    step = pl.program_id(0)
    group, length, width = x_ref.shape
    pairs = pl.num_programs(0) // 3
    early_steps = HALVES * pairs
    tokens = group * length
    if remote_on:
        bufs, finals, refs = refs[:20], refs[20:24], refs[24:]
        g1a_ref, g1b_ref, tile_ref, got_q, late_ref, send, recv, send_q, recv_q = refs[:9]
        held, sem_in = refs[9:23], refs[23]
        loads = [pltpu.make_async_copy(src, dst, sem_in.at[i]) for i, (src, dst) in enumerate(zip(far, held))]
        g2_ref, g3_ref, masters, firsts, seconds = held[0], held[1], held[2:6], held[6:10], held[10:14]
        chip, core = lax.axis_index("fsdp"), lax.axis_index("dp")
        shape4 = lambda ref: ref.reshape(4, 4, ref.shape[0] // CHIPS, ref.shape[1])
        scatters = [Scatter(g, bufs[5 * i:5 * i + 5], finals[i], send.at[i], recv.at[i], chip, core)
                    for i, g in enumerate((g1a_ref, g1b_ref, shape4(g2_ref), shape4(g3_ref)))]
        first, second, mid, down = scatters
        norm = Total(tile_ref, got_q, send_q, recv_q, chip, core)

    def one(s):
        def run():
            s.add0()
            s.start1()
        return run

    def two(s):
        def run():
            s.add1()
            s.start2()
        return run

    def both_one():
        one(mid)()
        one(down)()

    events = {0: [both_one], 4: [one(first), two(mid)], 5: [two(down)], 6: [two(first)], 7: [mid.add2]} if remote_on else {}

    @pl.when(step == 0)
    def _():
        if remote_on:
            loads[0].start()
            loads[1].start()
            meet(chip, core, FLIPS, (0, 1, 2, 3))
            loads[0].wait()
            mid.start0()
            loads[1].wait()
            down.start0()
            for load in loads[2:]:
                load.start()
        for ref in (gqkv_ref, qstack_ref, ostack_ref, kstack_ref):
            ref[...] = jnp.zeros_like(ref)
        sums_ref[...] = sums_a_ref[...]
        vec_ref[...] = side_of(w1_ref, 0, 3 * SIDE, 3 * SIDE + LANES).astype(F32).T

    @pl.when(step < pairs)
    def _():
        x = x_ref[...].reshape(tokens, width).astype(F32)
        xhat, _ = xhat_of(x)
        n1 = (xhat * vec_ref[0:1, :] + vec_ref[1:2, :]).astype(BF16)
        n1_ref[pl.ds(step * group, group)] = n1.reshape(group, length, width)

    if remote_on:
        @pl.when(step == pairs)
        def _():
            g1a_ref[...] = gqkv_ref[0].astype(BF16).reshape(g1a_ref.shape)
            first.start0()

    @pl.when(step < early_steps)
    def _():
        half = step // pairs
        first_row = lax.rem(step, pairs) * group

        def products(r):
            row = first_row + r
            crop_k = crop_of(*offsets_of(off_ref, row), (length, 1), 0)
            crop_q = crop_of(*offsets_of(off_ref, row), (1, PAD), 1)
            bias_ref[r] = jnp.where(crop_q == crop_k, 0.0, NEG)
            tiles = lambda ref, at: [ref[..., at + c * LANES:at + (c + 1) * LANES] for c in range(2)]
            stack_heads(qstack_ref.at[r], tiles(qkv_ref.at[0, r], 0), PAD)
            stack_heads(kstack_ref.at[r], tiles(qkv_ref.at[0, r], SIDE), length)
            stack_heads(ostack_ref.at[r], tiles(bctx_ref.at[r], 0), PAD)
            return nt(qkv_ref[0, r, :, SIDE:2 * SIDE], qstack_ref[r]), nt(qkv_ref[0, r, :, 2 * SIDE:], ostack_ref[r])

        def softmax(r, head, scores, back_probs):
            lanes = slice(head * PAD, (head + 1) * PAD)
            p = jnp.exp((scores[:, lanes] + bias_ref[r]) - lse_ref[0, r, head:head + 1, :])
            ds = (p * (back_probs[:, lanes] - dot_ref[0, r, head:head + 1, :])).astype(BF16)
            p_ref[r, :, lanes] = p.astype(BF16)
            ds_ref[r, :, lanes] = ds
            dsk_ref[r, head * length:(head + 1) * length, :] = ds

        def back_value(r):
            bqkv_ref[half, first_row + r, :, 2 * SIDE:] = nn(p_ref[r], ostack_ref[r]).astype(BF16)

        def back_key(r):
            bqkv_ref[half, first_row + r, :, SIDE:2 * SIDE] = nn(ds_ref[r], qstack_ref[r]).astype(BF16)

        def back_query(r):
            dq = tn(dsk_ref[r], kstack_ref[r])[:length] * HEAD_DIM ** (-0.5)
            bqkv_ref[half, first_row + r, :, 0:SIDE] = dq.astype(BF16)

        scores = [products(r) for r in range(group)]
        after = (back_value, back_key, back_query)
        for r in range(group):
            for head in range(FOUR):
                softmax(r, head, *scores[r])
                if r and head < len(after):
                    after[head](r - 1)
        for work in after:
            work(group - 1)
        for at, todo in events.items():
            def run(todo=todo):
                for event in todo:
                    event()
            pl.when(step == at)(run)
        n1 = n1_ref[pl.ds(first_row, group)].reshape(tokens, width)
        back = bqkv_ref[half, pl.ds(first_row, group)].reshape(tokens, 3 * SIDE)
        side = pl.ds(pl.multiple_of(half * SIDE, SIDE), SIDE)
        sums_ref[2:3, side] += col_sum(back[:, :SIDE].astype(F32))
        sums_ref[3:4, side] += col_sum(back[:, 2 * SIDE:].astype(F32))
        gqkv_ref[half] += tn(n1, back)

    @pl.when(step == early_steps)
    def _():
        if remote_on:
            g1b_ref[..., 0:3 * SIDE] = gqkv_ref[1].astype(BF16).reshape(g1a_ref.shape)
            g1b_ref[..., 3 * SIDE:] = sums_ref[...].T.astype(BF16).reshape(g1a_ref.shape[:3] + (LANES,))
            second.start0()
            first.add2()
            down.add2()
        else:
            g1_out[...] = gqkv_ref[...].astype(BF16)

    @pl.when(step >= early_steps)
    def _():
        x = x_ref[...].reshape(tokens, width).astype(F32)
        xhat, inv = xhat_of(x)
        back_n1 = None
        for half in range(HALVES):
            back = bqkv_ref[half, pl.ds((step - early_steps) * group, group)].reshape(tokens, 3 * SIDE)
            term = nt(back, side_of(w1_ref, half, 0, 3 * SIDE))
            back_n1 = term if back_n1 is None else back_n1 + term
        sums_ref[0:1, :] += col_sum(back_n1 * xhat)
        sums_ref[1:2, :] += col_sum(back_n1)
        grad = bmid_ref[...].reshape(tokens, width).astype(F32) + norm_back(back_n1 * vec_ref[0:1, :], xhat, inv)
        xgrad_ref[...] = grad.astype(BF16).reshape(group, length, width)

    @pl.when(step == early_steps)
    def _():
        if remote_on:
            one(second)()

    @pl.when(step == pl.num_programs(0) - 1)
    def _():
        if not remote_on:
            gv_out[...] = sums_ref[...].T.astype(BF16)
            return
        wide = masters[2].shape[1]
        mine, deep = mid.rows_mine, down.rows_mine

        def square(i, rows, places):
            sums = [None, None]
            for grad, cols in places:
                master = masters[i][rows, cols]
                _, _, direction = moments_of(grad, firsts[i][rows, cols], seconds[i][rows, cols])
                update = direction + weight_decay * master
                for n, v in enumerate((master, update)):
                    part = lanes_of(v * v)
                    sums[n] = part if sums[n] is None else sums[n] + part
            tile_ref[0, i:i + 1, width:] = sums[0]
            tile_ref[0, 4 + i:5 + i, width:] = sums[1]

        for load in loads[2:]:
            load.wait()
        tile_ref[0, :, 0:width] = jnp.zeros((8, width), F32)
        tile_ref[0, 0:2, 0:width] = sums_ref[0:2, :]
        full = slice(None)
        square(1, mine, [(finals[2][mine, 0:width], full)])
        square(2, mine, [(finals[2][mine, width:width + wide], full)])
        square(3, deep, [(finals[3][deep, :], full)])
        second.add1()
        second.start2()
        for s in (first, mid, down):
            s.finish()
        r1a_ref[...] = finals[0][...]
        r2_ref[...] = finals[2][...]
        r3_ref[...] = finals[3][...]
        second.add2()
        square(0, mine, [(finals[half][mine, part * SIDE:(part + 1) * SIDE], slice(part * width + half * SIDE, part * width + (half + 1) * SIDE))
                         for half in range(HALVES) for part in range(3)])
        norm.start(0)
        second.finish()
        r1b_ref[...] = finals[1][:, 0:3 * SIDE]
        norm.add(0)
        norm.start(1)
        norm.add(1)
        norms_ref[...] = jnp.broadcast_to(jnp.sqrt(jnp.sum(tile_ref[2, :, width:], axis=1, keepdims=True)), (8, LANES))
        late = jnp.concatenate([tile_ref[2, :, 0:width], jnp.zeros((LANES - 8, width), F32)], axis=0)
        late_ref[...] = late.T
        thin = width // CHIPS
        mine_late = late_ref[pl.ds(pl.multiple_of(chip * thin, thin), thin), :]
        table = jnp.where(lax.broadcasted_iota(jnp.int32, (1, LANES), 1) < 2, mine_late, finals[1][:, 3 * SIDE:])
        count = rv_ref.shape[0]
        for at, row in enumerate(flat_of(table, count * LANES // table.shape[0], count)):
            rv_ref[at:at + 1, :] = row


def phase_b(remote_on, off, x, qkv, bctx, bmid, lse, dots, w1, sums_a, grads=(), masters=(), firsts=(), seconds=(), flat_rows=0):
    rows, length, width = x.shape
    pairs = rows // GROUP
    blk = lambda w, index: pl.BlockSpec((GROUP, length, w), index)
    both = lambda s, *_: (lax.rem(s, pairs), 0, 0)
    late = lambda s, *_: (jnp.maximum(s - HALVES * pairs, 0), 0, 0)
    side = lambda s: jnp.minimum(s // pairs, HALVES - 1)
    pair = lambda s: jnp.where(s < HALVES * pairs, lax.rem(s, pairs), pairs - 1)
    sds = jax.ShapeDtypeStruct
    rowed = pl.BlockSpec((1, GROUP, 8, PAD), lambda s, *_: (side(s), pair(s), 0, 0))
    extra = (*grads, *masters, *firsts, *seconds)
    stack = lambda: pltpu.VMEM((GROUP, FOUR * PAD, SIDE), BF16)
    probs = lambda: pltpu.VMEM((GROUP, length, FOUR * PAD), BF16)
    scratch = [pltpu.VMEM((HALVES, width, 3 * SIDE), F32), pltpu.VMEM((HALVES, rows, length, 3 * SIDE), BF16),
               pltpu.VMEM((rows, length, width), BF16), pltpu.VMEM((GROUP, length, PAD), F32), stack(), stack(),
               pltpu.VMEM((GROUP, FOUR * length, SIDE), BF16), probs(), probs(), pltpu.VMEM((GROUP, FOUR * length, PAD), BF16),
               pltpu.VMEM((LANES, width), F32), pltpu.VMEM((LANES, width), F32)]
    params = dict(vmem_limit_bytes=62 << 20)
    if remote_on:
        thin = width // CHIPS
        sizes = [(thin, 3 * SIDE), (thin, 3 * SIDE + LANES)] + [(g.shape[0] // CHIPS, g.shape[1]) for g in grads]
        outs = [sds(s, F32) for s in [sizes[0]] * HALVES + sizes[2:] + [(flat_rows, LANES), (8, LANES)]]
        for s in sizes:
            scratch += scatter_bufs(*s)
        scratch += [pltpu.VMEM(s, F32) for s in sizes]
        scratch += [pltpu.VMEM((4, 4) + sizes[0], BF16), pltpu.VMEM((4, 4) + sizes[1], BF16), pltpu.VMEM((3, 8, width + LANES), F32),
                    pltpu.VMEM((10, 8, width + LANES), F32), pltpu.VMEM((width, LANES), F32), DMA((4, 8)), DMA((4, 8)), DMA((10,)), DMA((10,))]
        scratch += [pltpu.VMEM(e.shape, e.dtype) for e in extra] + [DMA((len(extra),))]
        params.update(collective_id=1, has_side_effects=True)
    else:
        outs = [sds((HALVES, width, 3 * SIDE), BF16), sds((width, LANES), BF16)]
    return pl.pallas_call(
        lambda *refs: kernel_b(remote_on, *refs),
        name="phase_b",
        grid_spec=pltpu.PrefetchScalarGridSpec(
            num_scalar_prefetch=0,
            grid=(3 * pairs,),
            in_specs=[whole(off.shape), blk(width, both), pl.BlockSpec((1, GROUP, length, 3 * SIDE), lambda s, *_: (side(s), pair(s), 0, 0)),
                      pl.BlockSpec((GROUP, length, SIDE), lambda s, *_: (pair(s), 0, side(s))), blk(width, late),
                      rowed, rowed, whole(w1.shape),
                      whole(sums_a.shape)] + [pl.BlockSpec(memory_space=pl.ANY)] * len(extra),
            out_specs=[blk(width, late)] + [whole(o.shape) for o in outs],
            scratch_shapes=scratch,
        ),
        out_shape=[sds(x.shape, BF16)] + outs,
        compiler_params=pltpu.CompilerParams(**params),
    )(off, x, qkv, bctx, bmid, lse, dots, w1, sums_a, *extra)


def update_kernel(*refs):
    n_in, n_out = 17, 17
    y_ref, xgrad_ref, y_out, xgrad_out = refs[0], refs[1], refs[2 + n_in], refs[3 + n_in]
    ins, outs = refs[2:2 + n_in], refs[4 + n_in:4 + n_in + n_out]
    held_y, held_x, wide_x = refs[4 + n_in + n_out:7 + n_in + n_out]
    kept = refs[7 + n_in + n_out:]
    held_in, held_out, sem_in, sem_out, sems = kept[:n_in], kept[n_in:n_in + n_out], *kept[n_in + n_out:]
    count = y_ref.shape[0]
    load = [pltpu.make_async_copy(src, dst, sem_in.at[i]) for i, (src, dst) in enumerate(zip(ins, held_in))]
    load_x = [pltpu.make_async_copy(xgrad_ref.at[row], held_x.at[row], sems.at[0, row]) for row in range(count)]
    load_y = [pltpu.make_async_copy(y_ref.at[row], held_y.at[row], sems.at[1, row]) for row in range(count)]
    store_x = [pltpu.make_async_copy(wide_x.at[row], xgrad_out.at[row], sems.at[2, row]) for row in range(count)]
    store_y = [pltpu.make_async_copy(held_y.at[row], y_out.at[row], sems.at[3, row]) for row in range(count)]
    for copy in load_x + load + load_y:
        copy.start()
    for row in range(count):
        load_x[row].wait()
        wide_x[row] = held_x[row].astype(F32)
        store_x[row].start()
    for copy in load:
        copy.wait()
    r1a, r1b, r2, r3, norms_ref = held_in[:5]
    masters, firsts, seconds = held_in[5:9], held_in[9:13], held_in[13:17]
    new_m, new_f, new_s, copies, norm_out = held_out[0:4], held_out[4:8], held_out[8:12], held_out[12:16], held_out[16]
    store = [pltpu.make_async_copy(src, dst, sem_out.at[i]) for i, (src, dst) in enumerate(zip(held_out, outs))]
    width, wide = masters[1].shape[1], masters[2].shape[1]
    full = slice(None)
    places = [(3, r3[...], full, True), (2, r2[:, width:width + wide], full, True), (1, r2[:, 0:width], full, True)]
    places += [(0, (r1a, r1b)[half][:, part * SIDE:(part + 1) * SIDE], slice(part * width + half * SIDE, part * width + (half + 1) * SIDE),
                half == HALVES - 1 and part == 2) for half in range(HALVES) for part in range(3)]
    row = lax.broadcasted_iota(jnp.int32, (3, 4), 0)
    col = lax.broadcasted_iota(jnp.int32, (3, 4), 1)
    table = jnp.zeros((3, 4), F32)
    for i, grad, cols, final in places:
        weight_norm, update_norm = norms_ref[i:i + 1, 0:1], norms_ref[4 + i:5 + i, 0:1]
        trust = weight_norm / update_norm
        first, second, direction = moments_of(grad, firsts[i][:, cols], seconds[i][:, cols])
        master = masters[i][:, cols]
        new = master - matrix_rate * trust * (direction + weight_decay * master)
        new_m[i][:, cols] = new
        copies[i][:, cols] = new.astype(BF16)
        new_f[i][:, cols] = first
        new_s[i][:, cols] = second
        if final:
            for block in range(4):
                store[4 * block + i].start()
        for r, value in enumerate((weight_norm, update_norm, trust)):
            table = jnp.where((row == r) & (col == i), value, table)
    norm_out[...] = table
    store[16].start()
    for row in range(count):
        load_y[row].wait()
        store_y[row].start()
    for copy in store_x + store + store_y:
        copy.wait()


def update_all(y, xgrad, reduced, norms, masters, firsts, seconds):
    sds = jax.ShapeDtypeStruct
    place = pl.BlockSpec(memory_space=pl.ANY)
    ins = (*reduced, norms, *masters, *firsts, *seconds)
    outs = [sds(m.shape, F32) for m in masters] * 3 + [sds(m.shape, BF16) for m in masters] + [sds((3, 4), F32)]
    return pl.pallas_call(
        update_kernel,
        name="update",
        out_shape=[sds(y.shape, y.dtype), sds(xgrad.shape, F32)] + outs,
        in_specs=[place] * (2 + len(ins)),
        out_specs=[place] * (2 + len(outs)),
        scratch_shapes=[pltpu.VMEM(y.shape, y.dtype), pltpu.VMEM(xgrad.shape, xgrad.dtype), pltpu.VMEM(xgrad.shape, F32)]
        + [pltpu.VMEM(a.shape, a.dtype) for a in (*ins, *outs)] + [DMA((len(ins),)), DMA((len(outs),)), DMA((4, y.shape[0]))],
        compiler_params=pltpu.CompilerParams(vmem_limit_bytes=62 << 20),
    )(y, xgrad, *ins)


def shards(block_in, offsets, cotangent, w_qkv, w_out, w_up, w_down, vectors, *moments):
    masters = (w_qkv, w_out, w_up, w_down)
    firsts, seconds = moments[:5], moments[5:]
    micro, local_rows, length, width = block_in.shape
    rows = micro * local_rows
    chips = lax.axis_size("fsdp")
    near = chips == CHIPS and lax.axis_size("dp") == 2 and vectors.shape[0] % LANES == 0
    columns = vectors.shape[0] * chips // width
    x = block_in.reshape(rows, length, width)
    cot = cotangent.reshape(rows, length, width)
    off = offsets.transpose(0, 2, 1)
    if near:
        flat = vectors.reshape(-1, LANES)
        y, qkv, bctx, bmid, lse, dots, g2, g3, sums_a, w1 = phase_a(True, off, x, cot, (*masters, flat))
        xgrad, *reduced, norms = phase_b(True, off, x, qkv, bctx, bmid, lse, dots, w1, sums_a, (g2, g3), masters, firsts[:4], seconds[:4],
                                           flat.shape[0])
    else:
        table = jnp.pad(vectors.reshape(-1, columns), ((0, 0), (0, LANES - columns)))
        sides = w_qkv.reshape(-1, 3, HALVES, SIDE).transpose(2, 0, 1, 3).reshape(HALVES, -1, 3 * SIDE)
        owns = [jnp.concatenate([sides, jnp.broadcast_to(table, (HALVES,) + table.shape)], axis=2),
                jnp.concatenate([w_out, w_up], axis=1), w_down]
        wholes = [lax.all_gather(o.astype(BF16), "fsdp", axis=o.ndim - 2, tiled=True) for o in owns]
        y, qkv, bctx, bmid, lse, dots, g2, g3, sums_a = phase_a(False, off, x, cot, wholes)
        xgrad, g1, gv = phase_b(False, off, x, qkv, bctx, bmid, lse, dots, wholes[0], sums_a)
        reduced = [lax.psum(lax.psum_scatter(g.astype(F32), "fsdp", scatter_dimension=0, tiled=True), "dp")
                   for g in (g1[0], g1[1], g2, g3, gv)]
        reduced[4] = reduced[4][:, :columns]
        grad1 = jnp.stack(reduced[:2]).reshape(HALVES, -1, 3, SIDE).transpose(1, 2, 0, 3).reshape(w_qkv.shape)
        grads = (grad1, reduced[2][:, :width], reduced[2][:, width:], reduced[3])
        updates = [moments_of(g, m, s)[2] + weight_decay * w for g, m, s, w in zip(grads, firsts, seconds, masters)]
        squares = jnp.stack([jnp.sum(w * w) for w in masters] + [jnp.sum(u * u) for u in updates])
        norms = jnp.broadcast_to(jnp.sqrt(lax.psum(squares, "fsdp"))[:, None], (8, LANES))
    y, xgrad, *news, matrix_norms = update_all(y, xgrad, reduced[:4], norms, masters, firsts[:4], seconds[:4])
    vec_first, vec_second, vec_direction = moments_of(reduced[4].reshape(-1), firsts[4], seconds[4])
    vec_new = vectors - vector_rate * vec_direction
    return (y.reshape(block_in.shape), xgrad.reshape(block_in.shape), *news[0:4], vec_new, *news[4:8], vec_first,
            *news[8:12], vec_second, *news[12:16], vec_new.astype(BF16), matrix_norms)


def solution(mesh):
    batch, matrix, vector = P(None, ("fsdp", "dp"), None, None), P("fsdp", None), P("fsdp")
    params = (matrix,) * 4 + (vector,)
    in_specs = (batch, P(None, ("fsdp", "dp"), None), batch) + params * 3
    out_specs = (batch, batch) + params * 4 + (P(),)
    return jax.shard_map(shards, mesh=mesh, in_specs=in_specs, out_specs=out_specs, check_vma=False)
```

```python
import jax
import jax.numpy as jnp
from jax import lax
from jax.experimental import pallas as pl
from jax.experimental.pallas import tpu as pltpu
from jax.sharding import PartitionSpec as P

HEAD_DIM = 64
STEP = 5
EPS = 1e-05
beta_first = 0.5
beta_second = 0.5
adam_eps = 1e-06
weight_decay = 0.01
matrix_rate = 1.0
vector_rate = 0.1
CHIPS = 16
GROUP = 2
LANES = 128
HALVES = 2
SIDE = 256
FOUR = 4
PAD = 384
NEG = -1e30
C0 = 0.7978845608028654
C1 = 0.044715
F32 = jnp.float32
BF16 = jnp.bfloat16
MESH = pl.DeviceIdType.MESH
DMA = pltpu.SemaphoreType.DMA


def nn(a, b):
    return lax.dot_general(a, b, (((1,), (0,)), ((), ())), preferred_element_type=F32)


def nt(a, b):
    return lax.dot_general(a, b, (((1,), (1,)), ((), ())), preferred_element_type=F32)


def tn(a, b):
    return lax.dot_general(a, b, (((0,), (0,)), ((), ())), preferred_element_type=F32)


def xhat_of(v):
    center = v - jnp.mean(v, axis=-1, keepdims=True)
    spread = jnp.mean(center * center, axis=-1, keepdims=True)
    inv = lax.rsqrt(spread + EPS)
    return center * inv, inv


def norm_back(e, xhat, inv):
    return (e - jnp.mean(e, axis=-1, keepdims=True) - xhat * jnp.mean(e * xhat, axis=-1, keepdims=True)) * inv


def crop_of(first, second, shape, axis):
    t = lax.broadcasted_iota(jnp.int32, shape, axis).astype(F32)
    return (t >= first).astype(jnp.int32) + (t >= second).astype(jnp.int32)


def side_of(ref, half, lo, hi):
    v = ref[half, ..., lo:hi]
    return v.reshape(-1, hi - lo)


def stack_heads(ref, tiles, pitch):
    low = lax.broadcasted_iota(jnp.int32, (1, LANES), 1) < HEAD_DIM
    for head in range(FOUR):
        tile = tiles[head // 2]
        keep = low if head % 2 == 0 else jnp.logical_not(low)
        lanes = slice(head // 2 * LANES, head // 2 * LANES + LANES)
        ref[head * pitch:head * pitch + tile.shape[0], lanes] = jnp.where(keep, tile, jnp.zeros_like(tile))


def offsets_of(ref, row):
    micro, inner = row // ref.shape[2], lax.rem(row, ref.shape[2])
    table = ref[micro].astype(F32)
    at = lax.broadcasted_iota(jnp.int32, (1, ref.shape[2]), 1)
    both = jnp.sum(jnp.where(at == inner, table, 0.0), axis=1, keepdims=True)
    return both[0:1], both[1:2]


def flat_places(rows, columns, at, axis_row, axis_lane, shape):
    row = lax.broadcasted_iota(jnp.int32, shape, axis_row)
    lane = lax.broadcasted_iota(jnp.int32, shape, axis_lane)
    return [row * columns + c == lane + at * LANES for c in range(columns)]


def table_of(flat, rows, columns):
    masks = [flat_places(rows, columns, at, 0, 1, (rows, LANES)) for at in range(flat.shape[0])]
    lane = lax.broadcasted_iota(jnp.int32, (1, LANES), 1)
    table = jnp.zeros((rows, LANES), F32)
    for c in range(columns):
        found = jnp.zeros((rows, LANES), F32)
        for at in range(flat.shape[0]):
            found = jnp.where(masks[at][c], flat[at:at + 1, :], found)
        table = jnp.where(lane == c, jnp.sum(found, axis=1, keepdims=True), table)
    return table


def flat_of(table, columns, count):
    rows = table.shape[0]
    out = []
    for at in range(count):
        masks = flat_places(rows, columns, at, 0, 1, (rows, LANES))
        found = jnp.zeros((rows, LANES), F32)
        for c in range(columns):
            found = jnp.where(masks[c], table[:, c:c + 1], found)
        out.append(jnp.sum(found, axis=0, keepdims=True))
    return out


def col_sum(v):
    return jnp.sum(v, axis=0, keepdims=True)


def partner(chip, flip):
    out = chip
    for bit in (1, 2, 4, 8):
        if flip & bit:
            out = out + bit - 2 * bit * lax.rem(chip // bit, 2)
    return out


def meet(chip, core, flips, others):
    barrier = pltpu.get_barrier_semaphore()
    for flip in flips:
        pl.semaphore_signal(barrier, inc=1, device_id=(partner(chip, flip), core), device_id_type=MESH)
    for flip in others:
        pl.semaphore_signal(barrier, inc=1, device_id=(partner(chip, flip), 1 - core), device_id_type=MESH)
    pl.semaphore_wait(barrier, len(flips) + len(others))


def remote(src, dst, send_sem, recv_sem, chip, core):
    return pltpu.make_async_remote_copy(src_ref=src, dst_ref=dst, send_sem=send_sem, recv_sem=recv_sem,
                                        device_id=(chip, core), device_id_type=MESH)


def wait_bytes(ref, sem):
    pltpu.make_async_copy(ref, ref, sem).wait()


class Gather:
    def __init__(self, whole, cols, send, recv, chip, core, quick, calm):
        self.whole, self.cols, self.chip, self.core, self.send, self.recv, self.quick, self.calm = whole, cols, chip, core, send, recv, quick, calm
        self.half = whole.shape[-2] // 2
        start = pl.multiple_of(core * self.half, self.half)
        self.rows, self.all = pl.ds(start, self.half), pl.ds(0, cols)
        self.mine = (self.rows, self.all)
        if self.half >= 32:
            q = self.half // 2
            self.cuts = [(pl.ds(start + i * q, q), self.all) for i in range(2)]
        else:
            q = cols // 256 * 128
            self.cuts = [(self.rows, pl.ds(0, q)), (self.rows, pl.ds(q, cols - q))]

    def column(self, flip, cut):
        return self.whole.at[:, lax.rem(partner(self.chip, flip), 4), cut[0], cut[1]]

    def shard(self, flip):
        at = partner(self.chip, flip)
        return self.whole.at[at // 4, lax.rem(at, 4), self.rows, self.all]

    def push(self, ref, sem, to):
        remote(ref, ref, self.send, self.recv.at[sem], partner(self.chip, to), self.core).start()

    def to_twin(self, flip):
        if self.calm and flip != 3:
            return
        ref = self.whole.at[:, :, self.rows, self.all] if self.calm else self.column(flip, self.mine)
        remote(ref, ref, self.send, self.recv.at[8], self.chip, 1 - self.core).start()

    def start(self):
        own = self.shard(0)
        for flip in (4, 8, 12):
            self.push(own, flip // 4, flip)
        if self.quick:
            self.push(own, 4, 1)
            self.push(own, 5, 2)

    def spread(self):
        for flip in (4, 8, 12):
            ref = self.shard(flip)
            wait_bytes(ref, self.recv.at[flip // 4])
            if self.quick:
                self.push(ref, 4, 1)
                self.push(ref, 5, 2)
        ref = self.column(0, self.mine)
        if not self.quick:
            self.push(ref, 4, 1)
            self.push(ref, 5, 2)
        self.to_twin(0)

    def cross(self):
        for sem, via, to, cut in ((4, 1, 2, 0), (5, 2, 1, 1)):
            wait_bytes(self.column(via, self.mine), self.recv.at[sem])
            self.push(self.column(via, self.cuts[cut]), 6 + cut, to)
            self.to_twin(via)

    def last(self):
        for cut in range(2):
            wait_bytes(self.column(3, self.cuts[cut]), self.recv.at[6 + cut])
        self.to_twin(3)

    def finish(self):
        wait_bytes(self.whole.at[:, :, pl.ds(0, self.half), self.all], self.recv.at[8])

    def drain(self):
        rows = pl.ds(0, self.half)
        for zs, yxs in (((0, 4), (0, 4)), ((0, 3), (0, 4)), ((0, 1), (0, 3))):
            wait_bytes(self.whole.at[pl.ds(*zs), pl.ds(*yxs), rows, self.all], self.send)


class Scatter:
    def __init__(self, grad, bufs, out, send, recv, chip, core):
        self.grad, self.out, self.send, self.recv, self.chip, self.core = grad, out, send, recv, chip, core
        self.got0, self.part, self.got1, self.col, self.got2 = bufs
        self.half = grad.shape[2] // 2
        self.start_mine = pl.multiple_of(core * self.half, self.half)
        self.rows_mine = pl.ds(self.start_mine, self.half)
        self.z, self.yx = chip // 4, lax.rem(chip, 4)

    def copy0(self):
        theirs = pl.ds(pl.multiple_of((1 - self.core) * self.half, self.half), self.half)
        return remote(self.grad.at[:, :, theirs, :], self.got0, self.send.at[0], self.recv.at[0], self.chip, 1 - self.core)

    def start0(self):
        self.copy0().start()

    def add0(self):
        self.copy0().wait()

        def one(i, _):
            z, yx = i // 4, lax.rem(i, 4)
            mine = self.grad[z, yx, pl.ds(self.start_mine, self.half), :].astype(F32)
            self.part[z, yx] = (mine + self.got0[z, yx].astype(F32)).astype(BF16)
            return 0

        lax.fori_loop(0, CHIPS, one, 0)

    def copy1(self, flip):
        to = partner(self.chip, flip)
        return remote(self.part.at[:, lax.rem(to, 4)], self.got1.at[flip - 1], self.send.at[flip], self.recv.at[flip], to, self.core)

    def start1(self):
        for flip in (3, 1, 2):
            self.copy1(flip).start()

    def add1(self):
        for flip in (1, 2, 3):
            self.copy1(flip).wait()

        def one(z, _):
            total = self.part[z, self.yx].astype(F32)
            for k in range(3):
                total = total + self.got1[k, z].astype(F32)
            self.col[z] = total.astype(BF16)
            return 0

        lax.fori_loop(0, 4, one, 0)

    def copy2(self, flip):
        to = partner(self.chip, 4 * flip)
        return remote(self.col.at[to // 4], self.got2.at[flip - 1], self.send.at[3 + flip], self.recv.at[3 + flip], to, self.core)

    def start2(self):
        for flip in (1, 2, 3):
            self.copy2(flip).start()

    def copy3(self):
        ref = self.out.at[pl.ds(self.start_mine, self.half), :]
        return remote(ref, ref, self.send.at[7], self.recv.at[7], self.chip, 1 - self.core)

    def add2(self):
        for flip in (1, 2, 3):
            self.copy2(flip).wait()
        total = self.col[self.z].astype(F32)
        for k in range(3):
            total = total + self.got2[k].astype(F32)
        self.out[pl.ds(self.start_mine, self.half), :] = total
        self.copy3().start()

    def finish(self):
        self.copy3().wait()


def scatter_bufs(rows, cols):
    half = rows // 2
    return [pltpu.VMEM((4, 4, half, cols), BF16), pltpu.VMEM((4, 4, half, cols), BF16), pltpu.VMEM((3, 4, half, cols), BF16),
            pltpu.VMEM((4, half, cols), BF16), pltpu.VMEM((3, half, cols), BF16)]


class Total:
    def __init__(self, tile, got, send, recv, chip, core):
        self.tile, self.got, self.send, self.recv, self.chip, self.core = tile, got, send, recv, chip, core

    def copies(self, turn):
        if turn == 0:
            peers = [(flip, other) for flip in range(4) for other in range(2) if flip or other]
        else:
            peers = [(flip, 0) for flip in (4, 8, 12)]
        out = []
        for n, (flip, other) in enumerate(peers):
            at = 7 * turn + n
            out.append(remote(self.tile.at[turn], self.got.at[at], self.send.at[at], self.recv.at[at], partner(self.chip, flip),
                              1 - self.core if other else self.core))
        return out

    def start(self, turn):
        for copy in self.copies(turn):
            copy.start()

    def add(self, turn):
        copies = self.copies(turn)
        for copy in copies:
            copy.wait()
        total = self.tile[turn]
        for n in range(len(copies)):
            total = total + self.got[7 * turn + n]
        self.tile[turn + 1] = total


FLIPS = (1, 2, 3, 4, 8, 12)


def kernel_a(remote_on, off_ref, x_ref, cot_ref, *refs):
    if remote_on:
        masters, refs = refs[:5], refs[5:]
    else:
        w_in, refs = refs[:3], refs[3:]
    y_ref, qkv_ref, bctx_ref, bmid_ref, lse_ref, dot_ref, g2_out, g3_out, sums_ref = refs[:9]
    refs = refs[9:]
    if remote_on:
        w1_out, refs = refs[0], refs[1:]
    gup_ref, gdn_ref, gout_ref, ctx_ref, n1_ref, bias_ref, kstack_ref, vstack_ref, p_ref, vec_ref = refs[:10]
    refs = refs[10:]
    step = pl.program_id(0)
    group, length, width = x_ref.shape
    pairs = pl.num_programs(0) // 3
    early = HALVES * pairs
    tokens = group * length
    hidden = gup_ref.shape[1]
    chunks = hidden // width
    if remote_on:
        w1_ref, whole2, whole3, send, recv, out_sem = refs
        chip, core = lax.axis_index("fsdp"), lax.axis_index("dp")
        wide = 3 * SIDE
        gathers = [Gather(w, cols, send.at[i], recv.at[i], chip, core, i in (0, 2), i in (1, 2)) for i, (w, cols) in enumerate((
            (w1_ref.at[0], wide + LANES), (w1_ref.at[1], wide), (whole2, width + hidden), (whole3, width)))]
        w2_ref, w3_ref = [w.reshape(CHIPS * w.shape[2], w.shape[3]) for w in (whole2, whole3)]
    else:
        w1_ref, w2_ref, w3_ref = w_in
    wout_ref, wup_ref = w2_ref.at[:, 0:width], w2_ref.at[:, width:width + hidden]

    @pl.when(step == 0)
    def _():
        if remote_on:
            rows = [g.rows for g in gathers]
            z, yx = chip // 4, lax.rem(chip, 4)

            def cast_side(half):
                for part in range(3):
                    at = part * width + half * SIDE
                    w1_ref[half, z, yx, rows[0], part * SIDE:(part + 1) * SIDE] = masters[0][rows[0], at:at + SIDE].astype(BF16)

            cast_side(0)
            thin = w1_ref.shape[3]
            table = table_of(masters[4][...], thin, masters[4].shape[0] * LANES // thin)
            w1_ref[0, z, yx, rows[0], wide:] = jnp.where(core == 0, table[:thin // 2], table[thin // 2:]).astype(BF16)
            meet(chip, core, FLIPS, (0,))
            gathers[0].start()
            cast_side(1)
            whole2[z, yx, rows[2], 0:width] = masters[1][rows[2], :].astype(BF16)
            whole2[z, yx, rows[2], width:] = masters[2][rows[2], :].astype(BF16)
            whole3[z, yx, rows[3], :] = masters[3][rows[3], :].astype(BF16)
        gup_ref[...] = jnp.zeros_like(gup_ref)
        gdn_ref[...] = jnp.zeros_like(gdn_ref)
        gout_ref[...] = jnp.zeros_like(gout_ref)
        sums_ref[...] = jnp.zeros_like(sums_ref)
        kstack_ref[...] = jnp.zeros_like(kstack_ref)
        vstack_ref[...] = jnp.zeros_like(vstack_ref)
        if remote_on:
            gathers[0].spread()
            for g in gathers[1:]:
                g.start()
            gathers[0].cross()
            gathers[0].last()
            gathers[1].spread()
            gathers[0].finish()
        vec_ref[...] = side_of(w1_ref, 0, 3 * SIDE, 3 * SIDE + LANES).astype(F32).T

    events = {}
    if remote_on:
        events = {0: [gathers[1].cross, gathers[2].spread], 1: [gathers[1].last], 2: [gathers[3].spread], 3: [gathers[2].cross], 5: [gathers[3].cross, gathers[2].last], 6: [gathers[3].last]}

    @pl.when(step < pairs)
    def _():
        x = x_ref[...].reshape(tokens, width).astype(F32)
        xhat, _ = xhat_of(x)
        n1 = (xhat * vec_ref[0:1, :] + vec_ref[1:2, :]).astype(BF16)
        n1_ref[pl.ds(step * group, group)] = n1.reshape(group, length, width)

    if remote_on:
        @pl.when(step == pairs)
        def _():
            gathers[1].finish()

    @pl.when(step < early)
    def _():
        half = step // pairs
        first_row = lax.rem(step, pairs) * group
        side = pl.ds(pl.multiple_of(half * SIDE, SIDE), SIDE)
        n1 = n1_ref[pl.ds(first_row, group)].reshape(tokens, width)
        q = ((nn(n1, side_of(w1_ref, half, 0, SIDE)) + vec_ref[2:3, side]) * HEAD_DIM ** (-0.5)).astype(BF16)
        k = nn(n1, side_of(w1_ref, half, SIDE, 2 * SIDE)).astype(BF16)
        v = (nn(n1, side_of(w1_ref, half, 2 * SIDE, 3 * SIDE)) + vec_ref[3:4, side]).astype(BF16)
        for part, value in enumerate((q, k, v)):
            qkv_ref[0, :, :, part * SIDE:(part + 1) * SIDE] = value.reshape(group, length, SIDE)
        lane = lax.broadcasted_iota(jnp.int32, (1, LANES), 1)

        def products(r):
            row = first_row + r
            crop_q = crop_of(*offsets_of(off_ref, row), (length, 1), 0)
            crop_k = crop_of(*offsets_of(off_ref, row), (1, PAD), 1)
            inside = lax.broadcasted_iota(jnp.int32, (1, PAD), 1) < length
            bias_ref[r] = jnp.where((crop_q == crop_k) & inside, 0.0, NEG)
            kr, vr = [[t[r * length:(r + 1) * length, c * LANES:(c + 1) * LANES] for c in range(2)] for t in (k, v)]
            stack_heads(kstack_ref.at[r], kr, PAD)
            stack_heads(vstack_ref.at[r], vr, PAD)
            return nt(q[r * length:(r + 1) * length], kstack_ref[r])

        def softmax(r, head, scores):
            lanes = slice(head * PAD, (head + 1) * PAD)
            s = scores[:, lanes] + bias_ref[r]
            peak = jnp.max(s, axis=-1, keepdims=True)
            e = jnp.exp(s - peak)
            p_ref[r, :, lanes] = e.astype(BF16)
            total = jnp.sum(e, axis=-1, keepdims=True)
            return 1.0 / total, peak + jnp.log(total)

        def contexts(r, stats):
            ctx = nn(p_ref[r], vstack_ref[r])
            for c in range(2):
                inverse = jnp.where(lane < HEAD_DIM, stats[2 * c][0], stats[2 * c + 1][0])
                lanes = pl.ds(pl.multiple_of(half * SIDE + c * LANES, LANES), LANES)
                ctx_ref[first_row + r, :, lanes] = (ctx[:, c * LANES:(c + 1) * LANES] * inverse).astype(BF16)
            table = jnp.zeros((length, LANES), F32)
            for head in range(FOUR):
                table = jnp.where(lane == head, stats[head][1], table)
            table = jnp.concatenate([table, jnp.zeros((PAD - length, LANES), F32)], axis=0)
            lse_ref[0, r] = table.T[:8]

        scores = [products(r) for r in range(group)]
        stats = []
        for r in range(group):
            stats.append([softmax(r, head, scores[r]) for head in range(FOUR)])
            if r:
                contexts(r - 1, stats[r - 1])
        contexts(group - 1, stats[group - 1])
        for at, todo in events.items():
            def run(todo=todo):
                for event in todo:
                    event()
            pl.when(step == at)(run)

    @pl.when(step == early)
    def _():
        if remote_on:
            gathers[2].finish()
            gathers[3].finish()
            pltpu.make_async_copy(w1_ref, w1_out, out_sem).start()

    @pl.when(step >= early)
    def _():
        first_row = (step - early) * group
        ctx = ctx_ref[pl.ds(first_row, group)].reshape(tokens, width)
        middle = x_ref[...].reshape(tokens, width).astype(F32) + (nn(ctx, wout_ref[...]) + vec_ref[4:5, :])
        xhat2, inv2 = xhat_of(middle)
        n2 = (xhat2 * vec_ref[5:6, :] + vec_ref[6:7, :]).astype(BF16)
        cot = cot_ref[...].reshape(tokens, width)
        result = middle + vec_ref[7 + chunks:8 + chunks, :]
        back_n2 = jnp.zeros((tokens, width), F32)

        def weight_grads(cols, active, back_up):
            gdn_ref[:, cols] += tn(cot, active)
            gup_ref[:, cols] += tn(n2, back_up)

        held = None

        def products(u):
            cols = slice(u * SIDE, (u + 1) * SIDE)
            bias = vec_ref[7 + u // 2:8 + u // 2, u % 2 * SIDE:(u % 2 + 1) * SIDE]
            return nn(n2, wup_ref[:, cols]) + bias, nt(cot, w3_ref[cols, :])

        ahead = products(0)
        for u in range(hidden // SIDE):
            cols = slice(u * SIDE, (u + 1) * SIDE)
            up, back_act = ahead
            if u + 1 < hidden // SIDE:
                ahead = products(u + 1)
            if held is not None:
                weight_grads(*held)
            square = up * up
            gate = 0.5 + 0.5 * jnp.tanh(up * (C0 + (C0 * C1) * square))
            active = up * gate
            slope = gate + active * (1.0 - gate) * (2.0 * C0 + (6.0 * C0 * C1) * square)
            active = active.astype(BF16)
            back_up = back_act * slope
            sums_ref[7 + u // 2:8 + u // 2, u % 2 * SIDE:(u % 2 + 1) * SIDE] += col_sum(back_up)
            back_up = back_up.astype(BF16)
            result = result + nn(active, w3_ref[cols, :])
            back_n2 = back_n2 + nt(back_up, wup_ref[:, cols])
            held = (cols, active, back_up)
        weight_grads(*held)
        y_ref[...] = result.astype(BF16).reshape(group, length, width)
        cot32 = cot.astype(F32)
        sums_ref[7 + chunks:8 + chunks, :] += col_sum(cot32)
        sums_ref[5:6, :] += col_sum(back_n2 * xhat2)
        sums_ref[6:7, :] += col_sum(back_n2)
        back_middle = cot32 + norm_back(back_n2 * vec_ref[5:6, :], xhat2, inv2)
        back_att = back_middle.astype(BF16)
        bmid_ref[...] = back_att.reshape(group, length, width)
        sums_ref[4:5, :] += col_sum(back_middle)
        gout_ref[...] += tn(ctx, back_att)
        back_ctx = nt(back_att, wout_ref[...]).astype(BF16)
        bctx_ref[...] = back_ctx.reshape(group, length, width)
        pick = (lax.broadcasted_iota(jnp.int32, (16, width), 1) // HEAD_DIM == lax.broadcasted_iota(jnp.int32, (16, width), 0)).astype(BF16)
        for r in range(group):
            rows = slice(r * length, (r + 1) * length)
            product = ctx[rows].astype(F32) * back_ctx[rows].astype(F32)
            product = jnp.concatenate([product, jnp.zeros((PAD - length, width), F32)], axis=0)
            high = product.astype(BF16)
            dots = nt(pick, high) + nt(pick, (product - high.astype(F32)).astype(BF16))
            for half in range(HALVES):
                dot_ref[half, r, 0:FOUR, :] = dots[half * FOUR:(half + 1) * FOUR]
                dot_ref[half, r, FOUR:, :] = jnp.zeros((8 - FOUR, PAD), F32)

    @pl.when(step == pl.num_programs(0) - 1)
    def _():
        g2_out[:, 0:width] = gout_ref[...].astype(BF16)
        g2_out[:, width:] = gup_ref[...].astype(BF16)
        for u in range(chunks):
            g3_out[u * width:(u + 1) * width, :] = gdn_ref[:, u * width:(u + 1) * width].T.astype(BF16)
        if remote_on:
            pltpu.make_async_copy(w1_ref, w1_out, out_sem).wait()
            for g in gathers:
                g.drain()


def whole(shape):
    return pl.BlockSpec(shape, lambda s, *_: (0,) * len(shape), pipeline_mode=pl.Buffered(1))


def phase_a(remote_on, off, x, cot, weights):
    rows, length, width = x.shape
    pairs = rows // GROUP
    if remote_on:
        sizes = [(weights[0].shape[0], 3 * SIDE + LANES), (weights[1].shape[0], width + weights[2].shape[1]), weights[3].shape]
        w2_shape, w3_shape = (CHIPS * sizes[1][0], sizes[1][1]), (CHIPS * sizes[2][0], sizes[2][1])
    else:
        w2_shape, w3_shape = weights[1].shape, weights[2].shape
    hidden = w3_shape[0]
    blk = lambda w, index: pl.BlockSpec((GROUP, length, w), index)
    both = lambda s, *_: (lax.rem(s, pairs), 0, 0)
    late = lambda s, *_: (jnp.maximum(s - HALVES * pairs, 0), 0, 0)
    sided = lambda s, *_: (jnp.minimum(s // pairs, HALVES - 1), jnp.where(s < HALVES * pairs, lax.rem(s, pairs), pairs - 1), 0, 0)
    sds = jax.ShapeDtypeStruct
    out_specs = [blk(width, late), pl.BlockSpec((1, GROUP, length, 3 * SIDE), sided), blk(width, late), blk(width, late),
                 pl.BlockSpec((1, GROUP, 8, PAD), sided), pl.BlockSpec((HALVES, GROUP, 8, PAD), lambda s, *_: (0,) + late(s)),
                 whole(w2_shape), whole(w3_shape), whole((LANES, width))]
    out_shape = [sds(x.shape, BF16), sds((HALVES, rows, length, 3 * SIDE), BF16), sds(x.shape, BF16), sds(x.shape, BF16),
                 sds((HALVES, rows, 8, PAD), F32), sds((HALVES, rows, 8, PAD), F32),
                 sds(w2_shape, BF16), sds(w3_shape, BF16), sds((LANES, width), F32)]
    scratch = [pltpu.VMEM((width, hidden), F32), pltpu.VMEM((width, hidden), F32), pltpu.VMEM((width, width), F32),
               pltpu.VMEM((rows, length, width), BF16), pltpu.VMEM((rows, length, width), BF16), pltpu.VMEM((GROUP, length, PAD), F32),
               pltpu.VMEM((GROUP, FOUR * PAD, SIDE), BF16), pltpu.VMEM((GROUP, FOUR * PAD, SIDE), BF16),
               pltpu.VMEM((GROUP, length, FOUR * PAD), BF16), pltpu.VMEM((LANES, width), F32)]
    params = dict(vmem_limit_bytes=62 << 20)
    if remote_on:
        out_specs.append(pl.BlockSpec(memory_space=pl.ANY))
        out_shape.append(sds((HALVES, 4, 4) + sizes[0], BF16))
        scratch += [pltpu.VMEM((HALVES, 4, 4) + sizes[0], BF16)] + [pltpu.VMEM((4, 4) + s, BF16) for s in sizes[1:]]
        scratch += [DMA((4,)), DMA((4, 9)), DMA]
        params.update(collective_id=0, has_side_effects=True)
    return pl.pallas_call(
        lambda *refs: kernel_a(remote_on, *refs),
        name="phase_a",
        grid_spec=pltpu.PrefetchScalarGridSpec(
            num_scalar_prefetch=0,
            grid=(3 * pairs,),
            in_specs=[whole(off.shape), blk(width, both), blk(width, late)] + [whole(w.shape) for w in weights],
            out_specs=out_specs,
            scratch_shapes=scratch,
        ),
        out_shape=out_shape,
        compiler_params=pltpu.CompilerParams(**params),
    )(off, x, cot, *weights)


def moments_of(grad, first, second):
    new_first = beta_first * first + (1.0 - beta_first) * grad
    new_second = beta_second * second + (1.0 - beta_second) * grad * grad
    direction = new_first / (1.0 - beta_first**STEP) / (jnp.sqrt(new_second / (1.0 - beta_second**STEP)) + adam_eps)
    return new_first, new_second, direction


def lanes_of(v):
    total = None
    for j in range(v.shape[1] // LANES):
        piece = v[:, j * LANES:(j + 1) * LANES]
        total = piece if total is None else total + piece
    return jnp.sum(total, axis=0, keepdims=True)


def kernel_b(remote_on, off_ref, x_ref, qkv_ref, bctx_ref, bmid_ref, lse_ref, dot_ref, w1_ref, sums_a_ref, *refs):
    if remote_on:
        far = refs[0:14]
        xgrad_ref, r1a_ref, r1b_ref, r2_ref, r3_ref, rv_ref, norms_ref = refs[14:21]
        refs = refs[21:]
    else:
        xgrad_ref, g1_out, gv_out = refs[:3]
        refs = refs[3:]
    gqkv_ref, bqkv_ref, n1_ref, bias_ref, qstack_ref, ostack_ref, kstack_ref, p_ref, ds_ref, dsk_ref, sums_ref, vec_ref = refs[:12]
    refs = refs[12:]
    step = pl.program_id(0)
    group, length, width = x_ref.shape
    pairs = pl.num_programs(0) // 3
    early_steps = HALVES * pairs
    tokens = group * length
    if remote_on:
        bufs, finals, refs = refs[:20], refs[20:24], refs[24:]
        g1a_ref, g1b_ref, tile_ref, got_q, late_ref, send, recv, send_q, recv_q = refs[:9]
        held, sem_in = refs[9:23], refs[23]
        loads = [pltpu.make_async_copy(src, dst, sem_in.at[i]) for i, (src, dst) in enumerate(zip(far, held))]
        g2_ref, g3_ref, masters, firsts, seconds = held[0], held[1], held[2:6], held[6:10], held[10:14]
        chip, core = lax.axis_index("fsdp"), lax.axis_index("dp")
        shape4 = lambda ref: ref.reshape(4, 4, ref.shape[0] // CHIPS, ref.shape[1])
        scatters = [Scatter(g, bufs[5 * i:5 * i + 5], finals[i], send.at[i], recv.at[i], chip, core)
                    for i, g in enumerate((g1a_ref, g1b_ref, shape4(g2_ref), shape4(g3_ref)))]
        first, second, mid, down = scatters
        norm = Total(tile_ref, got_q, send_q, recv_q, chip, core)

    def one(s):
        def run():
            s.add0()
            s.start1()
        return run

    def two(s):
        def run():
            s.add1()
            s.start2()
        return run

    def both_one():
        one(mid)()
        one(down)()

    events = {0: [one(mid)], 1: [one(down)], 4: [two(mid), one(first)], 5: [two(down)], 6: [two(first)], 7: [mid.add2]} if remote_on else {}

    @pl.when(step == 0)
    def _():
        if remote_on:
            loads[0].start()
            loads[1].start()
            meet(chip, core, FLIPS, (0, 1, 2, 3))
            loads[0].wait()
            mid.start0()
            loads[1].wait()
            down.start0()
            for load in loads[2:]:
                load.start()
        for ref in (gqkv_ref, qstack_ref, ostack_ref, kstack_ref):
            ref[...] = jnp.zeros_like(ref)
        sums_ref[...] = sums_a_ref[...]
        vec_ref[...] = side_of(w1_ref, 0, 3 * SIDE, 3 * SIDE + LANES).astype(F32).T

    @pl.when(step < pairs)
    def _():
        x = x_ref[...].reshape(tokens, width).astype(F32)
        xhat, _ = xhat_of(x)
        n1 = (xhat * vec_ref[0:1, :] + vec_ref[1:2, :]).astype(BF16)
        n1_ref[pl.ds(step * group, group)] = n1.reshape(group, length, width)

    if remote_on:
        @pl.when(step == pairs)
        def _():
            g1a_ref[...] = gqkv_ref[0].astype(BF16).reshape(g1a_ref.shape)
            first.start0()

    @pl.when(step < early_steps)
    def _():
        half = step // pairs
        first_row = lax.rem(step, pairs) * group

        def products(r):
            row = first_row + r
            crop_k = crop_of(*offsets_of(off_ref, row), (length, 1), 0)
            crop_q = crop_of(*offsets_of(off_ref, row), (1, PAD), 1)
            bias_ref[r] = jnp.where(crop_q == crop_k, 0.0, NEG)
            tiles = lambda ref, at: [ref[..., at + c * LANES:at + (c + 1) * LANES] for c in range(2)]
            stack_heads(qstack_ref.at[r], tiles(qkv_ref.at[0, r], 0), PAD)
            stack_heads(kstack_ref.at[r], tiles(qkv_ref.at[0, r], SIDE), length)
            stack_heads(ostack_ref.at[r], tiles(bctx_ref.at[r], 0), PAD)
            return nt(qkv_ref[0, r, :, SIDE:2 * SIDE], qstack_ref[r]), nt(qkv_ref[0, r, :, 2 * SIDE:], ostack_ref[r])

        def softmax(r, head, scores, back_probs):
            lanes = slice(head * PAD, (head + 1) * PAD)
            p = jnp.exp((scores[:, lanes] + bias_ref[r]) - lse_ref[0, r, head:head + 1, :])
            ds = (p * (back_probs[:, lanes] - dot_ref[0, r, head:head + 1, :])).astype(BF16)
            p_ref[r, :, lanes] = p.astype(BF16)
            ds_ref[r, :, lanes] = ds
            dsk_ref[r, head * length:(head + 1) * length, :] = ds

        def back_value(r):
            bqkv_ref[half, first_row + r, :, 2 * SIDE:] = nn(p_ref[r], ostack_ref[r]).astype(BF16)

        def back_key(r):
            bqkv_ref[half, first_row + r, :, SIDE:2 * SIDE] = nn(ds_ref[r], qstack_ref[r]).astype(BF16)

        def back_query(r):
            dq = tn(dsk_ref[r], kstack_ref[r])[:length] * HEAD_DIM ** (-0.5)
            bqkv_ref[half, first_row + r, :, 0:SIDE] = dq.astype(BF16)

        scores = [products(r) for r in range(group)]
        after = (back_value, back_key, back_query)
        for r in range(group):
            for head in range(FOUR):
                softmax(r, head, *scores[r])
                if r and head < len(after):
                    after[head](r - 1)
        for work in after:
            work(group - 1)
        for at, todo in events.items():
            def run(todo=todo):
                for event in todo:
                    event()
            pl.when(step == at)(run)
        n1 = n1_ref[pl.ds(first_row, group)].reshape(tokens, width)
        back = bqkv_ref[half, pl.ds(first_row, group)].reshape(tokens, 3 * SIDE)
        side = pl.ds(pl.multiple_of(half * SIDE, SIDE), SIDE)
        sums_ref[2:3, side] += col_sum(back[:, :SIDE].astype(F32))
        sums_ref[3:4, side] += col_sum(back[:, 2 * SIDE:].astype(F32))
        gqkv_ref[half] += tn(n1, back)

    @pl.when(step == early_steps)
    def _():
        if remote_on:
            g1b_ref[..., 0:3 * SIDE] = gqkv_ref[1].astype(BF16).reshape(g1a_ref.shape)
            g1b_ref[..., 3 * SIDE:] = sums_ref[...].T.astype(BF16).reshape(g1a_ref.shape[:3] + (LANES,))
            second.start0()
            first.add2()
            down.add2()
        else:
            g1_out[...] = gqkv_ref[...].astype(BF16)

    @pl.when(step >= early_steps)
    def _():
        x = x_ref[...].reshape(tokens, width).astype(F32)
        xhat, inv = xhat_of(x)
        back_n1 = None
        for half in range(HALVES):
            back = bqkv_ref[half, pl.ds((step - early_steps) * group, group)].reshape(tokens, 3 * SIDE)
            term = nt(back, side_of(w1_ref, half, 0, 3 * SIDE))
            back_n1 = term if back_n1 is None else back_n1 + term
        sums_ref[0:1, :] += col_sum(back_n1 * xhat)
        sums_ref[1:2, :] += col_sum(back_n1)
        grad = bmid_ref[...].reshape(tokens, width).astype(F32) + norm_back(back_n1 * vec_ref[0:1, :], xhat, inv)
        xgrad_ref[...] = grad.astype(BF16).reshape(group, length, width)

    @pl.when(step == early_steps)
    def _():
        if remote_on:
            one(second)()

    @pl.when(step == pl.num_programs(0) - 1)
    def _():
        if not remote_on:
            gv_out[...] = sums_ref[...].T.astype(BF16)
            return
        wide = masters[2].shape[1]
        mine, deep = mid.rows_mine, down.rows_mine

        def square(i, rows, places):
            sums = [None, None]
            for grad, cols in places:
                master = masters[i][rows, cols]
                _, _, direction = moments_of(grad, firsts[i][rows, cols], seconds[i][rows, cols])
                update = direction + weight_decay * master
                for n, v in enumerate((master, update)):
                    part = lanes_of(v * v)
                    sums[n] = part if sums[n] is None else sums[n] + part
            tile_ref[0, i:i + 1, width:] = sums[0]
            tile_ref[0, 4 + i:5 + i, width:] = sums[1]

        for load in loads[2:]:
            load.wait()
        tile_ref[0, :, 0:width] = jnp.zeros((8, width), F32)
        tile_ref[0, 0:2, 0:width] = sums_ref[0:2, :]
        full = slice(None)
        square(1, mine, [(finals[2][mine, 0:width], full)])
        square(2, mine, [(finals[2][mine, width:width + wide], full)])
        square(3, deep, [(finals[3][deep, :], full)])
        second.add1()
        second.start2()
        for s in (first, mid, down):
            s.finish()
        r1a_ref[...] = finals[0][...]
        r2_ref[...] = finals[2][...]
        r3_ref[...] = finals[3][...]
        second.add2()
        square(0, mine, [(finals[half][mine, part * SIDE:(part + 1) * SIDE], slice(part * width + half * SIDE, part * width + (half + 1) * SIDE))
                         for half in range(HALVES) for part in range(3)])
        norm.start(0)
        second.finish()
        r1b_ref[...] = finals[1][:, 0:3 * SIDE]
        norm.add(0)
        norm.start(1)
        norm.add(1)
        norms_ref[...] = jnp.broadcast_to(jnp.sqrt(jnp.sum(tile_ref[2, :, width:], axis=1, keepdims=True)), (8, LANES))
        late = jnp.concatenate([tile_ref[2, :, 0:width], jnp.zeros((LANES - 8, width), F32)], axis=0)
        late_ref[...] = late.T
        thin = width // CHIPS
        mine_late = late_ref[pl.ds(pl.multiple_of(chip * thin, thin), thin), :]
        table = jnp.where(lax.broadcasted_iota(jnp.int32, (1, LANES), 1) < 2, mine_late, finals[1][:, 3 * SIDE:])
        count = rv_ref.shape[0]
        for at, row in enumerate(flat_of(table, count * LANES // table.shape[0], count)):
            rv_ref[at:at + 1, :] = row


def phase_b(remote_on, off, x, qkv, bctx, bmid, lse, dots, w1, sums_a, grads=(), masters=(), firsts=(), seconds=(), flat_rows=0):
    rows, length, width = x.shape
    pairs = rows // GROUP
    blk = lambda w, index: pl.BlockSpec((GROUP, length, w), index)
    both = lambda s, *_: (lax.rem(s, pairs), 0, 0)
    late = lambda s, *_: (jnp.maximum(s - HALVES * pairs, 0), 0, 0)
    side = lambda s: jnp.minimum(s // pairs, HALVES - 1)
    pair = lambda s: jnp.where(s < HALVES * pairs, lax.rem(s, pairs), pairs - 1)
    sds = jax.ShapeDtypeStruct
    rowed = pl.BlockSpec((1, GROUP, 8, PAD), lambda s, *_: (side(s), pair(s), 0, 0))
    extra = (*grads, *masters, *firsts, *seconds)
    stack = lambda: pltpu.VMEM((GROUP, FOUR * PAD, SIDE), BF16)
    probs = lambda: pltpu.VMEM((GROUP, length, FOUR * PAD), BF16)
    scratch = [pltpu.VMEM((HALVES, width, 3 * SIDE), F32), pltpu.VMEM((HALVES, rows, length, 3 * SIDE), BF16),
               pltpu.VMEM((rows, length, width), BF16), pltpu.VMEM((GROUP, length, PAD), F32), stack(), stack(),
               pltpu.VMEM((GROUP, FOUR * length, SIDE), BF16), probs(), probs(), pltpu.VMEM((GROUP, FOUR * length, PAD), BF16),
               pltpu.VMEM((LANES, width), F32), pltpu.VMEM((LANES, width), F32)]
    params = dict(vmem_limit_bytes=62 << 20)
    if remote_on:
        thin = width // CHIPS
        sizes = [(thin, 3 * SIDE), (thin, 3 * SIDE + LANES)] + [(g.shape[0] // CHIPS, g.shape[1]) for g in grads]
        outs = [sds(s, F32) for s in [sizes[0]] * HALVES + sizes[2:] + [(flat_rows, LANES), (8, LANES)]]
        for s in sizes:
            scratch += scatter_bufs(*s)
        scratch += [pltpu.VMEM(s, F32) for s in sizes]
        scratch += [pltpu.VMEM((4, 4) + sizes[0], BF16), pltpu.VMEM((4, 4) + sizes[1], BF16), pltpu.VMEM((3, 8, width + LANES), F32),
                    pltpu.VMEM((10, 8, width + LANES), F32), pltpu.VMEM((width, LANES), F32), DMA((4, 8)), DMA((4, 8)), DMA((10,)), DMA((10,))]
        scratch += [pltpu.VMEM(e.shape, e.dtype) for e in extra] + [DMA((len(extra),))]
        params.update(collective_id=1, has_side_effects=True)
    else:
        outs = [sds((HALVES, width, 3 * SIDE), BF16), sds((width, LANES), BF16)]
    return pl.pallas_call(
        lambda *refs: kernel_b(remote_on, *refs),
        name="phase_b",
        grid_spec=pltpu.PrefetchScalarGridSpec(
            num_scalar_prefetch=0,
            grid=(3 * pairs,),
            in_specs=[whole(off.shape), blk(width, both), pl.BlockSpec((1, GROUP, length, 3 * SIDE), lambda s, *_: (side(s), pair(s), 0, 0)),
                      pl.BlockSpec((GROUP, length, SIDE), lambda s, *_: (pair(s), 0, side(s))), blk(width, late),
                      rowed, rowed, whole(w1.shape),
                      whole(sums_a.shape)] + [pl.BlockSpec(memory_space=pl.ANY)] * len(extra),
            out_specs=[blk(width, late)] + [whole(o.shape) for o in outs],
            scratch_shapes=scratch,
        ),
        out_shape=[sds(x.shape, BF16)] + outs,
        compiler_params=pltpu.CompilerParams(**params),
    )(off, x, qkv, bctx, bmid, lse, dots, w1, sums_a, *extra)


def update_kernel(*refs):
    n_in, n_out = 17, 17
    y_ref, xgrad_ref, y_out, xgrad_out = refs[0], refs[1], refs[2 + n_in], refs[3 + n_in]
    ins, outs = refs[2:2 + n_in], refs[4 + n_in:4 + n_in + n_out]
    held_y, held_x, wide_x = refs[4 + n_in + n_out:7 + n_in + n_out]
    kept = refs[7 + n_in + n_out:]
    held_in, held_out, sem_in, sem_out, sems = kept[:n_in], kept[n_in:n_in + n_out], *kept[n_in + n_out:]
    count = y_ref.shape[0]
    load = [pltpu.make_async_copy(src, dst, sem_in.at[i]) for i, (src, dst) in enumerate(zip(ins, held_in))]
    load_x = [pltpu.make_async_copy(xgrad_ref.at[row], held_x.at[row], sems.at[0, row]) for row in range(count)]
    load_y = [pltpu.make_async_copy(y_ref.at[row], held_y.at[row], sems.at[1, row]) for row in range(count)]
    store_x = [pltpu.make_async_copy(wide_x.at[row], xgrad_out.at[row], sems.at[2, row]) for row in range(count)]
    store_y = [pltpu.make_async_copy(held_y.at[row], y_out.at[row], sems.at[3, row]) for row in range(count)]
    for copy in load_x + load + load_y:
        copy.start()
    for row in range(count):
        load_x[row].wait()
        wide_x[row] = held_x[row].astype(F32)
        store_x[row].start()
    for copy in load:
        copy.wait()
    r1a, r1b, r2, r3, norms_ref = held_in[:5]
    masters, firsts, seconds = held_in[5:9], held_in[9:13], held_in[13:17]
    new_m, new_f, new_s, copies, norm_out = held_out[0:4], held_out[4:8], held_out[8:12], held_out[12:16], held_out[16]
    store = [pltpu.make_async_copy(src, dst, sem_out.at[i]) for i, (src, dst) in enumerate(zip(held_out, outs))]
    width, wide = masters[1].shape[1], masters[2].shape[1]
    full = slice(None)
    places = [(3, r3[...], full, True), (2, r2[:, width:width + wide], full, True), (1, r2[:, 0:width], full, True)]
    places += [(0, (r1a, r1b)[half][:, part * SIDE:(part + 1) * SIDE], slice(part * width + half * SIDE, part * width + (half + 1) * SIDE),
                half == HALVES - 1 and part == 2) for half in range(HALVES) for part in range(3)]
    row = lax.broadcasted_iota(jnp.int32, (3, 4), 0)
    col = lax.broadcasted_iota(jnp.int32, (3, 4), 1)
    table = jnp.zeros((3, 4), F32)
    for i, grad, cols, final in places:
        weight_norm, update_norm = norms_ref[i:i + 1, 0:1], norms_ref[4 + i:5 + i, 0:1]
        trust = weight_norm / update_norm
        first, second, direction = moments_of(grad, firsts[i][:, cols], seconds[i][:, cols])
        master = masters[i][:, cols]
        new = master - matrix_rate * trust * (direction + weight_decay * master)
        new_m[i][:, cols] = new
        copies[i][:, cols] = new.astype(BF16)
        new_f[i][:, cols] = first
        new_s[i][:, cols] = second
        if final:
            for block in range(4):
                store[4 * block + i].start()
        for r, value in enumerate((weight_norm, update_norm, trust)):
            table = jnp.where((row == r) & (col == i), value, table)
    norm_out[...] = table
    store[16].start()
    for row in range(count):
        load_y[row].wait()
        store_y[row].start()
    for copy in store_x + store + store_y:
        copy.wait()


def update_all(y, xgrad, reduced, norms, masters, firsts, seconds):
    sds = jax.ShapeDtypeStruct
    place = pl.BlockSpec(memory_space=pl.ANY)
    ins = (*reduced, norms, *masters, *firsts, *seconds)
    outs = [sds(m.shape, F32) for m in masters] * 3 + [sds(m.shape, BF16) for m in masters] + [sds((3, 4), F32)]
    return pl.pallas_call(
        update_kernel,
        name="update",
        out_shape=[sds(y.shape, y.dtype), sds(xgrad.shape, F32)] + outs,
        in_specs=[place] * (2 + len(ins)),
        out_specs=[place] * (2 + len(outs)),
        scratch_shapes=[pltpu.VMEM(y.shape, y.dtype), pltpu.VMEM(xgrad.shape, xgrad.dtype), pltpu.VMEM(xgrad.shape, F32)]
        + [pltpu.VMEM(a.shape, a.dtype) for a in (*ins, *outs)] + [DMA((len(ins),)), DMA((len(outs),)), DMA((4, y.shape[0]))],
        compiler_params=pltpu.CompilerParams(vmem_limit_bytes=62 << 20),
    )(y, xgrad, *ins)


def shards(block_in, offsets, cotangent, w_qkv, w_out, w_up, w_down, vectors, *moments):
    masters = (w_qkv, w_out, w_up, w_down)
    firsts, seconds = moments[:5], moments[5:]
    micro, local_rows, length, width = block_in.shape
    rows = micro * local_rows
    chips = lax.axis_size("fsdp")
    near = chips == CHIPS and lax.axis_size("dp") == 2 and vectors.shape[0] % LANES == 0
    columns = vectors.shape[0] * chips // width
    x = block_in.reshape(rows, length, width)
    cot = cotangent.reshape(rows, length, width)
    off = offsets.transpose(0, 2, 1)
    if near:
        flat = vectors.reshape(-1, LANES)
        y, qkv, bctx, bmid, lse, dots, g2, g3, sums_a, w1 = phase_a(True, off, x, cot, (*masters, flat))
        xgrad, *reduced, norms = phase_b(True, off, x, qkv, bctx, bmid, lse, dots, w1, sums_a, (g2, g3), masters, firsts[:4], seconds[:4],
                                           flat.shape[0])
    else:
        table = jnp.pad(vectors.reshape(-1, columns), ((0, 0), (0, LANES - columns)))
        sides = w_qkv.reshape(-1, 3, HALVES, SIDE).transpose(2, 0, 1, 3).reshape(HALVES, -1, 3 * SIDE)
        owns = [jnp.concatenate([sides, jnp.broadcast_to(table, (HALVES,) + table.shape)], axis=2),
                jnp.concatenate([w_out, w_up], axis=1), w_down]
        wholes = [lax.all_gather(o.astype(BF16), "fsdp", axis=o.ndim - 2, tiled=True) for o in owns]
        y, qkv, bctx, bmid, lse, dots, g2, g3, sums_a = phase_a(False, off, x, cot, wholes)
        xgrad, g1, gv = phase_b(False, off, x, qkv, bctx, bmid, lse, dots, wholes[0], sums_a)
        reduced = [lax.psum(lax.psum_scatter(g.astype(F32), "fsdp", scatter_dimension=0, tiled=True), "dp")
                   for g in (g1[0], g1[1], g2, g3, gv)]
        reduced[4] = reduced[4][:, :columns]
        grad1 = jnp.stack(reduced[:2]).reshape(HALVES, -1, 3, SIDE).transpose(1, 2, 0, 3).reshape(w_qkv.shape)
        grads = (grad1, reduced[2][:, :width], reduced[2][:, width:], reduced[3])
        updates = [moments_of(g, m, s)[2] + weight_decay * w for g, m, s, w in zip(grads, firsts, seconds, masters)]
        squares = jnp.stack([jnp.sum(w * w) for w in masters] + [jnp.sum(u * u) for u in updates])
        norms = jnp.broadcast_to(jnp.sqrt(lax.psum(squares, "fsdp"))[:, None], (8, LANES))
    y, xgrad, *news, matrix_norms = update_all(y, xgrad, reduced[:4], norms, masters, firsts[:4], seconds[:4])
    vec_first, vec_second, vec_direction = moments_of(reduced[4].reshape(-1), firsts[4], seconds[4])
    vec_new = vectors - vector_rate * vec_direction
    return (y.reshape(block_in.shape), xgrad.reshape(block_in.shape), *news[0:4], vec_new, *news[4:8], vec_first,
            *news[8:12], vec_second, *news[12:16], vec_new.astype(BF16), matrix_norms)


def solution(mesh):
    batch, matrix, vector = P(None, ("fsdp", "dp"), None, None), P("fsdp", None), P("fsdp")
    params = (matrix,) * 4 + (vector,)
    in_specs = (batch, P(None, ("fsdp", "dp"), None), batch) + params * 3
    out_specs = (batch, batch) + params * 4 + (P(),)
    return jax.shard_map(shards, mesh=mesh, in_specs=in_specs, out_specs=out_specs, check_vma=False)
```
